32 devices in a mesh: dp: 32 (over z, y, x, core).
Axes of the slice: x: 2, y: 2, z: 4, core: 2. Of those that a mesh axis runs over, the one named last changes fastest.
Arguments:
- tokens: bfloat16 [4096, 1024], P('dp'), may hold values from -6 to 6
- lengths: int32 [32, 2], P('dp'), may hold values from 1 to 64, as said below
- cotangent: bfloat16 [4096, 1024], P('dp'), may hold values from -6 to 6
- norm1_gain: bfloat16 [1024], P('dp'), may hold values from 0.5 to 1.5
- norm1_shift: bfloat16 [1024], P('dp'), may hold values from -3 to 3
- joint_weight: bfloat16 [1024, 3072], P('dp'), may hold values from -0.1875 to 0.1875
- query_bias: bfloat16 [1024], P('dp'), may hold values from -3 to 3
- value_bias: bfloat16 [1024], P('dp'), may hold values from -3 to 3
- output_weight: bfloat16 [1024, 1024], P('dp'), may hold values from -0.5 to 0.5
- output_bias: bfloat16 [1024], P('dp'), may hold values from -3 to 3
- norm2_gain: bfloat16 [1024], P('dp'), may hold values from 0.5 to 1.5
- norm2_shift: bfloat16 [1024], P('dp'), may hold values from -3 to 3
- expand_weight: bfloat16 [1024, 4096], P('dp'), may hold values from -0.1875 to 0.1875
- expand_bias: bfloat16 [4096], P('dp'), may hold values from -3 to 3
- reduce_weight: bfloat16 [4096, 1024], P('dp'), may hold values from -0.09375 to 0.09375
- reduce_bias: bfloat16 [1024], P('dp'), may hold values from -3 to 3
Outputs:
- layer_output: bfloat16 [4096, 1024], P('dp')
- grad_tokens: float32 [4096, 1024], P('dp')
- grad_norm1_gain: float32 [1024], P('dp')
- grad_norm1_shift: float32 [1024], P('dp')
- grad_joint_weight: float32 [1024, 3072], P('dp')
- grad_query_bias: float32 [1024], P('dp')
- grad_value_bias: float32 [1024], P('dp')
- grad_output_weight: float32 [1024, 1024], P('dp')
- grad_output_bias: float32 [1024], P('dp')
- grad_norm2_gain: float32 [1024], P('dp')
- grad_norm2_shift: float32 [1024], P('dp')
- grad_expand_weight: float32 [1024, 4096], P('dp')
- grad_expand_bias: float32 [4096], P('dp')
- grad_reduce_weight: float32 [4096, 1024], P('dp')
- grad_reduce_bias: float32 [1024], P('dp')
The draws below stay inside these ranges and needn't reach their ends.
Inputs may be any that keep to these rules, and one draw needn't show every extreme that they name: On every device one sequence has the largest length 64, and on one device all sequences have it; the lengths of a device sum to at most 128.
All inputs are finite; a program needn't handle non-finite values.
Results may differ from the reference program's by a relative error of at most 0.011.
Values may be sent and summed in bfloat16 or wider, within the bound.
A program may use at most 192 MiB of HBM per device.

```python
import jax
import jax.numpy as jnp
from jax import lax

D = 1024
HEADS = 16
FF = 4096
ROWS = 128
SEQS_DEV = 2
GROUPS = 32
TOKENS = 4096


def draw_lengths(key, part):
    first_key = jax.random.fold_in(key, 11)
    pick_key = jax.random.fold_in(key, 23)
    full_key = jax.random.fold_in(key, 37)
    longest = ROWS // SEQS_DEV
    drawn = jax.random.randint(first_key, (GROUPS, SEQS_DEV), 1, longest + 1)
    picked = jax.random.randint(pick_key, (GROUPS, 1), 0, SEQS_DEV)
    column = jnp.arange(SEQS_DEV, dtype=jnp.int32)[None, :]
    drawn = jnp.where(column == picked, longest, drawn)
    chosen = jax.random.randint(full_key, (), 0, GROUPS)
    device_row = jnp.arange(GROUPS, dtype=jnp.int32)[:, None]
    drawn = jnp.where(device_row == chosen, longest, drawn)
    return drawn.astype(jnp.int32)


def levels(stream_key, extent, split, least, top_value):
    def one(dim, blocks):
        draws = jax.random.uniform(jax.random.fold_in(jax.random.fold_in(stream_key, 6), dim), (blocks,), jnp.float32, least / len(split), top_value / len(split))
        return jnp.repeat(jnp.exp(draws), extent[dim] // blocks).reshape((-1,) + (1,) * (len(extent) - dim - 1))

    loudness = one(*split[0])
    for cut in split[1:]:
        loudness = loudness * one(*cut)
    return loudness


def noise(key, extent, scale, most, pieces=(), held_as=jnp.bfloat16):
    loudness = levels(key, extent, pieces, -0.22, 0.18) if pieces else 1.0
    values = jax.random.normal(key, extent, jnp.float32) * scale * loudness
    return jnp.minimum(jnp.maximum(values, -most), most).astype(held_as)


def setup_inputs(seed: int = 0) -> dict:
    arg_keys = jax.random.split(jax.random.key(seed), 17)
    return {
        "tokens": noise(arg_keys[0], (TOKENS, D), 1.0, 6.0, ((0, 32),)),
        "lengths": draw_lengths(jax.random.fold_in(arg_keys[16], 71), 0),
        "cotangent": noise(arg_keys[2], (TOKENS, D), 1.0, 6.0, ((0, 32),)),
        "norm1_gain": jnp.clip(1.0 + 0.1 * jax.random.normal(arg_keys[3], (D,), jnp.float32), 0.5, 1.5).astype(jnp.bfloat16),
        "norm1_shift": noise(arg_keys[4], (D,), 0.3, 3.0, ((0, 32),)),
        "joint_weight": noise(arg_keys[5], (D, 3 * D), D ** -0.5, 0.1875, ((0, 32),)),
        "query_bias": noise(arg_keys[6], (D,), 0.5, 3.0, ((0, 32),)),
        "value_bias": noise(arg_keys[7], (D,), 0.5, 3.0, ((0, 32),)),
        "output_weight": noise(arg_keys[8], (D, D), (D // 8) ** -0.5, 0.5, ((0, 32),)),
        "output_bias": noise(arg_keys[9], (D,), 0.5, 3.0, ((0, 32),)),
        "norm2_gain": jnp.clip(1.0 + 0.1 * jax.random.normal(arg_keys[10], (D,), jnp.float32), 0.5, 1.5).astype(jnp.bfloat16),
        "norm2_shift": noise(arg_keys[11], (D,), 0.3, 3.0, ((0, 32),)),
        "expand_weight": noise(arg_keys[12], (D, FF), D ** -0.5, 0.1875, ((0, 32),)),
        "expand_bias": noise(arg_keys[13], (FF,), 0.5, 3.0, ((0, 32),)),
        "reduce_weight": noise(arg_keys[14], (FF, D), FF ** -0.5, 0.09375, ((0, 32),)),
        "reduce_bias": noise(arg_keys[15], (D,), 0.5, 3.0, ((0, 32),)),
    }


EPSILON = 1e-05
TANH_SCALE = 0.7978845608028654
CUBIC_TERM = 0.044715

def layer_norm(row_data, gain_vector, shift_vector):
    average = lax.optimization_barrier(jnp.mean(row_data, axis=-1, keepdims=True))
    centred = row_data - average
    spread = lax.optimization_barrier(jnp.mean(centred * centred, axis=-1, keepdims=True))
    return centred * lax.rsqrt(spread + EPSILON) * gain_vector + shift_vector

def activation(values_in):
    return 0.5 * values_in * (1.0 + jnp.tanh(TANH_SCALE * (values_in + CUBIC_TERM * values_in * values_in * values_in)))

def contract(pattern, first_op, second_op):
    return jnp.einsum(pattern, first_op.astype(jnp.float32), second_op.astype(jnp.float32))

def transposed_left(first_op, second_op):
    return lax.dot_general(first_op, second_op, (((0,), (0,)), ((), ())), preferred_element_type=jnp.float32)

def transposed_right(first_op, second_op):
    return lax.dot_general(first_op, second_op, (((1,), (1,)), ((), ())), preferred_element_type=jnp.float32)

def slot_mask(lengths_row, row_count):
    seq_ends = jnp.cumsum(lengths_row).astype(jnp.int32)
    position = jnp.arange(row_count, dtype=jnp.int32)
    segment = lax.optimization_barrier(jnp.sum((position[:, None] >= seq_ends[None, :]).astype(jnp.int32), axis=1)).astype(jnp.int32)
    live_rows = position < seq_ends[-1]
    segment = jnp.where(live_rows, segment, row_count + position)
    allowed = (segment[:, None] == segment[None, :]) & (position[:, None] >= position[None, :])
    return (allowed, live_rows.astype(jnp.float32))

def masked_scores(query_heads, key_heads, allowed):
    score_scale = query_heads.shape[2] ** (-0.5)
    scores = contract('qhd,khd->hqk', query_heads, key_heads) * score_scale
    return jnp.where(allowed[None, :, :], scores, -1e+30)

def forward(tokens, lengths_row, attn_params, ffn_params):
    gain_first, shift_first, joint_weight, query_bias, value_bias, output_weight, output_bias = attn_params
    gain_second, shift_second, expand_weight, expand_bias, reduce_weight, reduce_bias = ffn_params
    row_count, model_width = tokens.shape
    head_size = model_width // HEADS
    allowed, live_rows = slot_mask(lengths_row, row_count)
    residual = tokens.astype(jnp.float32)
    first_normed = layer_norm(residual, gain_first.astype(jnp.float32), shift_first.astype(jnp.float32)).astype(jnp.bfloat16)
    packed = jnp.dot(first_normed, joint_weight, preferred_element_type=jnp.float32)
    query_heads = (packed[:, :model_width] + query_bias.astype(jnp.float32)).astype(jnp.bfloat16).reshape(row_count, HEADS, head_size)
    key_heads = packed[:, model_width:2 * model_width].astype(jnp.bfloat16).reshape(row_count, HEADS, head_size)
    value_heads = (packed[:, 2 * model_width:] + value_bias.astype(jnp.float32)).astype(jnp.bfloat16).reshape(row_count, HEADS, head_size)
    scores = masked_scores(query_heads, key_heads, allowed)
    row_top = lax.optimization_barrier(jnp.max(scores, axis=-1, keepdims=True))
    logsum = row_top + jnp.log(lax.optimization_barrier(jnp.sum(jnp.exp(scores - row_top), axis=-1, keepdims=True)))
    weights = jnp.exp(scores - logsum).astype(jnp.bfloat16)
    context = contract('hqk,khd->qhd', weights, value_heads).astype(jnp.bfloat16).reshape(row_count, model_width)
    middle = residual + jnp.dot(context, output_weight, preferred_element_type=jnp.float32) + output_bias.astype(jnp.float32)
    second_normed = layer_norm(middle, gain_second.astype(jnp.float32), shift_second.astype(jnp.float32)).astype(jnp.bfloat16)
    before = jnp.dot(second_normed, expand_weight, preferred_element_type=jnp.float32) + expand_bias.astype(jnp.float32)
    active = activation(before).astype(jnp.bfloat16)
    block_final = middle + jnp.dot(active, reduce_weight, preferred_element_type=jnp.float32) + reduce_bias.astype(jnp.float32)
    stored_state = (residual, first_normed, query_heads, key_heads, value_heads, allowed, live_rows, logsum, context, middle, second_normed, before, active)
    return (block_final.astype(jnp.bfloat16), stored_state)

def backward(stored_state, cotangent, attn_params, ffn_params):
    residual, first_normed, query_heads, key_heads, value_heads, allowed, live_rows, logsum, context, middle, second_normed, before, active = stored_state
    gain_first, shift_first, joint_weight, query_bias, value_bias, output_weight, output_bias = attn_params
    gain_second, shift_second, expand_weight, expand_bias, reduce_weight, reduce_bias = ffn_params
    row_count, model_width = residual.shape
    head_size = model_width // HEADS
    score_scale = head_size ** (-0.5)
    grad_final = cotangent.astype(jnp.float32) * live_rows[:, None]
    grad_final_low = grad_final.astype(jnp.bfloat16)
    grad_reduce_bias = lax.optimization_barrier(jnp.sum(grad_final, axis=0))
    grad_reduce_weight = transposed_left(active, grad_final_low)
    grad_active = transposed_right(grad_final_low, reduce_weight)
    unused_value, curve_back = jax.vjp(activation, before)
    grad_before = curve_back(grad_active)[0]
    grad_expand_bias = lax.optimization_barrier(jnp.sum(grad_before, axis=0))
    grad_before_low = grad_before.astype(jnp.bfloat16)
    grad_expand_weight = transposed_left(second_normed, grad_before_low)
    grad_second_normed = transposed_right(grad_before_low, expand_weight)
    unused_norm, second_back = jax.vjp(layer_norm, middle, gain_second.astype(jnp.float32), shift_second.astype(jnp.float32))
    grad_middle_norm, grad_gain_second, grad_shift_second = second_back(grad_second_normed)
    grad_middle = grad_final + grad_middle_norm
    grad_middle_low = grad_middle.astype(jnp.bfloat16)
    grad_output_bias = lax.optimization_barrier(jnp.sum(grad_middle, axis=0))
    grad_output_weight = transposed_left(context, grad_middle_low)
    grad_context = transposed_right(grad_middle_low, output_weight).astype(jnp.bfloat16).reshape(row_count, HEADS, head_size)
    scores = masked_scores(query_heads, key_heads, allowed)
    probs = jnp.exp(scores - logsum)
    weights = probs.astype(jnp.bfloat16)
    grad_probs = contract('qhd,khd->hqk', grad_context, value_heads)
    grad_values = contract('hqk,qhd->khd', weights, grad_context)
    centre = lax.optimization_barrier(jnp.sum(probs * grad_probs, axis=-1, keepdims=True))
    grad_scores = (probs * (grad_probs - centre) * score_scale).astype(jnp.bfloat16)
    grad_query = contract('hqk,khd->qhd', grad_scores, key_heads).reshape(row_count, model_width)
    grad_keys = contract('hqk,qhd->khd', grad_scores, query_heads).reshape(row_count, model_width)
    grad_values = grad_values.reshape(row_count, model_width)
    grad_query_bias = lax.optimization_barrier(jnp.sum(grad_query, axis=0))
    grad_value_bias = lax.optimization_barrier(jnp.sum(grad_values, axis=0))
    grad_packed = jnp.concatenate([grad_query, grad_keys, grad_values], axis=1).astype(jnp.bfloat16)
    grad_joint_weight = transposed_left(first_normed, grad_packed)
    grad_first_normed = transposed_right(grad_packed, joint_weight)
    unused_first, first_back = jax.vjp(layer_norm, residual, gain_first.astype(jnp.float32), shift_first.astype(jnp.float32))
    grad_tokens_norm, grad_gain_first, grad_shift_first = first_back(grad_first_normed)
    grad_tokens = grad_middle + grad_tokens_norm
    attn_grads = (grad_gain_first, grad_shift_first, grad_joint_weight, grad_query_bias, grad_value_bias, grad_output_weight, grad_output_bias)
    ffn_grads = (grad_gain_second, grad_shift_second, grad_expand_weight, grad_expand_bias, grad_reduce_weight, grad_reduce_bias)
    return (grad_tokens, attn_grads, ffn_grads)

def reference(tokens, lengths, cotangent, norm1_gain, norm1_shift, joint_weight, query_bias, value_bias, output_weight, output_bias, norm2_gain, norm2_shift, expand_weight, expand_bias, reduce_weight, reduce_bias):
    attn_params = (norm1_gain, norm1_shift, joint_weight, query_bias, value_bias, output_weight, output_bias)
    ffn_params = (norm2_gain, norm2_shift, expand_weight, expand_bias, reduce_weight, reduce_bias)
    blocks_in = (tokens.reshape(GROUPS, ROWS, D), lengths, cotangent.reshape(GROUPS, ROWS, D))
    start_totals = jax.tree.map(lambda member: jnp.zeros(member.shape, jnp.float32), (attn_params, ffn_params))

    def step(totals, block_data):
        block_tokens, block_lengths, block_cotangent = block_data
        block_output, stored_state = forward(block_tokens, block_lengths, attn_params, ffn_params)
        grad_block, attn_grads, ffn_grads = backward(stored_state, block_cotangent, attn_params, ffn_params)
        totals = jax.tree.map(lambda first_op, second_op: first_op + second_op, totals, (attn_grads, ffn_grads))
        return (totals, (block_output, grad_block))
    final_totals, stacked = lax.scan(step, start_totals, blocks_in)
    attn_total, ffn_total = final_totals
    outputs_all, grads_all = stacked
    return (outputs_all.reshape(TOKENS, D), grads_all.reshape(TOKENS, D), attn_total[0], attn_total[1], attn_total[2], attn_total[3], attn_total[4], attn_total[5], attn_total[6], ffn_total[0], ffn_total[1], ffn_total[2], ffn_total[3], ffn_total[4], ffn_total[5])
```

```python
import jax
import jax.numpy as jnp
from jax import lax
from jax.sharding import PartitionSpec as P

HEADS = 16
TENSOR = 8

EPSILON = 1e-05
TANH_SCALE = 0.7978845608028654
CUBIC_TERM = 0.044715

F32 = jnp.float32
BF16 = jnp.bfloat16


def layer_norm(row_data, gain_vector, shift_vector):
    average = jnp.mean(row_data, axis=-1, keepdims=True)
    centred = row_data - average
    spread = jnp.mean(centred * centred, axis=-1, keepdims=True)
    return centred * lax.rsqrt(spread + EPSILON) * gain_vector + shift_vector


def activation(values_in):
    return (
        0.5
        * values_in
        * (
            1.0
            + jnp.tanh(TANH_SCALE * (values_in + CUBIC_TERM * values_in * values_in * values_in))
        )
    )


def contract(pattern, first_op, second_op):
    return jnp.einsum(pattern, first_op, second_op, preferred_element_type=F32)


def dot(first_op, second_op):
    return jnp.dot(first_op, second_op, preferred_element_type=F32)


def transposed_left(first_op, second_op):
    return lax.dot_general(
        first_op, second_op, (((0,), (0,)), ((), ())), preferred_element_type=F32
    )


def transposed_right(first_op, second_op):
    return lax.dot_general(
        first_op, second_op, (((1,), (1,)), ((), ())), preferred_element_type=F32
    )


def slot_mask(lengths_row, row_count):
    position = jnp.arange(row_count, dtype=jnp.int32)
    segment = jnp.zeros((row_count,), jnp.int32)
    end = jnp.int32(0)
    for j in range(lengths_row.shape[0]):
        end = end + lengths_row[j]
        segment = segment + (position >= end).astype(jnp.int32)
    live_rows = position < end
    segment = jnp.where(live_rows, segment, row_count + position)
    allowed = (segment[:, None] == segment[None, :]) & (position[:, None] >= position[None, :])
    return (allowed, live_rows.astype(F32))


def on_device(
    tokens,
    lengths,
    cotangent,
    norm1_gain,
    norm1_shift,
    joint_weight,
    query_bias,
    value_bias,
    output_weight,
    output_bias,
    norm2_gain,
    norm2_shift,
    expand_weight,
    expand_bias,
    reduce_weight,
    reduce_bias,
):
    n = lax.axis_size("dp")
    t = TENSOR if n % TENSOR == 0 else 1
    b = n // t
    rows, width = tokens.shape
    hid = expand_weight.shape[1]
    br = joint_weight.shape[0]
    hs = reduce_weight.shape[0]
    head_size = width // HEADS
    hl = HEADS // t
    fl = width // t
    me = lax.axis_index("dp")
    mine = me % t
    plane = [[z * t + p for p in range(t)] for z in range(b)]
    column = [[z * t + p for z in range(b)] for p in range(t)]
    swap = [(z * t + p, p * b + z) for z in range(b) for p in range(t)]

    def gather(x, groups):
        return lax.all_gather(x, "dp", axis=0, tiled=True, axis_index_groups=groups)

    def scatter(x, groups):
        return lax.psum_scatter(
            x, "dp", scatter_dimension=0, tiled=True, axis_index_groups=groups
        )

    def exchange(x):
        return lax.all_to_all(
            x, "dp", split_axis=0, concat_axis=0, tiled=True, axis_index_groups=plane
        )

    vecs = [
        norm1_gain, norm1_shift, query_bias, value_bias, output_bias,
        norm2_gain, norm2_shift, expand_bias, reduce_bias,
    ]
    sizes = [v.shape[0] for v in vecs]
    small = lax.all_gather(jnp.concatenate(vecs)[None, :], "dp", axis=0, tiled=True)
    whole, at = [], 0
    for s in sizes:
        whole.append(small[:, at : at + s].reshape(-1).astype(F32))
        at += s
    gain1, shift1, qb, vb, ob, gain2, shift2, eb, rb = whole
    eb = lax.dynamic_slice_in_dim(eb.reshape(b, t, hs), mine, 1, 1).reshape(-1)
    qb = lax.dynamic_slice_in_dim(qb, mine * fl, fl, 0)
    vb = lax.dynamic_slice_in_dim(vb, mine * fl, fl, 0)

    joint_cut = joint_weight.reshape(br, 3, t, fl).transpose(2, 0, 1, 3).reshape(t * br, 3 * fl)
    expand_cut = expand_weight.reshape(br, b, t, hs).transpose(2, 0, 1, 3).reshape(t * br, b * hs)
    out_mine = lax.ppermute(output_weight, "dp", [(d, s) for s, d in swap])
    wout = gather(out_mine, column)
    joint = gather(exchange(joint_cut), column)
    expand = gather(exchange(expand_cut), column)
    reduce = gather(reduce_weight, column)

    lens = gather(lengths, plane)
    allowed, _ = jax.vmap(lambda r: slot_mask(r, rows))(lens)
    _, live = slot_mask(lengths[0], rows)

    residual = tokens.astype(F32)
    n1 = gather(layer_norm(residual, gain1, shift1).astype(BF16), plane)
    grad_final = cotangent.astype(F32) * live[:, None]
    gf = gather(grad_final.astype(BF16), plane)

    packed = dot(n1, joint)
    shape4 = (t, rows, hl, head_size)
    q = (packed[:, :fl] + qb).astype(BF16).reshape(shape4)
    k = packed[:, fl : 2 * fl].astype(BF16).reshape(shape4)
    v = (packed[:, 2 * fl :] + vb).astype(BF16).reshape(shape4)
    scale = head_size ** (-0.5)
    scores = contract("gqhd,gkhd->ghqk", q, k) * scale
    scores = jnp.where(allowed[:, None], scores, -1e30)
    top = jnp.max(scores, axis=-1, keepdims=True)
    logsum = top + jnp.log(jnp.sum(jnp.exp(scores - top), axis=-1, keepdims=True))
    probs = jnp.exp(scores - logsum)
    weights = probs.astype(BF16)
    context = contract("ghqk,gkhd->gqhd", weights, v).astype(BF16).reshape(t * rows, fl)
    middle = (
        residual + scatter(dot(context, wout).astype(BF16), plane).astype(F32) + ob
    )
    n2 = gather(layer_norm(middle, gain2, shift2).astype(BF16), plane)
    before = dot(n2, expand) + eb
    active = activation(before).astype(BF16)
    final = middle + scatter(dot(active, reduce).astype(BF16), plane).astype(F32) + rb
    layer_output = final.astype(BF16)

    grad_rb = jnp.sum(grad_final, axis=0)
    g_reduce = transposed_left(active, gf)
    _, curve_back = jax.vjp(activation, before)
    gb = curve_back(transposed_right(gf, reduce))[0]
    grad_eb = jnp.sum(gb, axis=0)
    gbl = gb.astype(BF16)
    g_expand = transposed_left(n2, gbl)
    gn2 = scatter(transposed_right(gbl, expand).astype(BF16), plane).astype(F32)
    _, back2 = jax.vjp(layer_norm, middle, gain2, shift2)
    gmn, grad_g2, grad_s2 = back2(gn2)
    gm_own = grad_final + gmn
    grad_ob = jnp.sum(gm_own, axis=0)
    gm = gather(gm_own.astype(BF16), plane)
    g_out = transposed_left(context, gm)
    gctx = transposed_right(gm, wout).astype(BF16).reshape(shape4)
    gp = contract("gqhd,gkhd->ghqk", gctx, v)
    gv = contract("ghqk,gqhd->gkhd", weights, gctx).reshape(t * rows, fl)
    centre = jnp.sum(probs * gp, axis=-1, keepdims=True)
    gs = (probs * (gp - centre) * scale).astype(BF16)
    gq = contract("ghqk,gkhd->gqhd", gs, k).reshape(t * rows, fl)
    gk = contract("ghqk,gqhd->gkhd", gs, q).reshape(t * rows, fl)
    grad_qb = jnp.sum(gq, axis=0)
    grad_vb = jnp.sum(gv, axis=0)
    gpacked = jnp.concatenate([gq, gk, gv], axis=1).astype(BF16)
    g_joint = transposed_left(n1, gpacked)
    gn1 = scatter(transposed_right(gpacked, joint).astype(BF16), plane).astype(F32)
    _, back1 = jax.vjp(layer_norm, residual, gain1, shift1)
    gtn, grad_g1, grad_s1 = back1(gn1)
    grad_tokens = gm_own + gtn

    reduce_out = scatter(g_reduce.astype(BF16), column).astype(F32)
    expand_out = (
        exchange(scatter(g_expand.astype(BF16), column))
        .reshape(t, br, b, hs).transpose(1, 2, 0, 3).reshape(br, hid).astype(F32)
    )
    joint_out = (
        exchange(scatter(g_joint.astype(BF16), column))
        .reshape(t, br, 3, fl).transpose(1, 2, 0, 3).reshape(br, 3 * width).astype(F32)
    )
    out_out = lax.ppermute(scatter(g_out.astype(BF16), column), "dp", swap).astype(F32)

    def place(x):
        return lax.dynamic_update_slice_in_dim(jnp.zeros((width,), F32), x, mine * fl, 0)

    full_eb = lax.dynamic_update_slice_in_dim(
        jnp.zeros((b, t, hs), F32), grad_eb.reshape(b, 1, hs), mine, 1
    )
    grads = [grad_g1, grad_s1, place(grad_qb), place(grad_vb), grad_ob, grad_g2, grad_s2, full_eb, grad_rb]
    sums = lax.psum_scatter(
        jnp.concatenate([g.reshape(n, -1) for g in grads], axis=1),
        "dp", scatter_dimension=0, tiled=True,
    )[0]
    pieces, at = [], 0
    for s in sizes:
        pieces.append(sums[at : at + s])
        at += s
    return (
        layer_output, grad_tokens, pieces[0], pieces[1], joint_out, pieces[2], pieces[3],
        out_out, pieces[4], pieces[5], pieces[6], expand_out, pieces[7], reduce_out, pieces[8],
    )


def solution(mesh):
    m, v = P("dp", None), P("dp")
    in_specs = (m, m, m, v, v, m, v, v, m, v, v, v, m, v, m, v)
    out_specs = (m, m, v, v, m, v, v, m, v, v, v, m, v, m, v)
    return jax.shard_map(
        on_device, mesh=mesh, in_specs=in_specs, out_specs=out_specs, check_vma=False
    )
```

```python
import functools

import jax
import jax.numpy as jnp
from jax import lax
from jax.experimental import pallas as pl
from jax.experimental.pallas import tpu as pltpu
from jax.sharding import PartitionSpec as P

HEADS = 16
TENSOR = 8

EPSILON = 1e-05
TANH_SCALE = 0.7978845608028654
CUBIC_TERM = 0.044715

F32 = jnp.float32
BF16 = jnp.bfloat16


def layer_norm(row_data, gain_vector, shift_vector):
    average = jnp.mean(row_data, axis=-1, keepdims=True)
    centred = row_data - average
    spread = jnp.mean(centred * centred, axis=-1, keepdims=True)
    return centred * lax.rsqrt(spread + EPSILON) * gain_vector + shift_vector


def activation(values_in):
    return (
        0.5
        * values_in
        * (
            1.0
            + jnp.tanh(TANH_SCALE * (values_in + CUBIC_TERM * values_in * values_in * values_in))
        )
    )


def contract(pattern, first_op, second_op):
    return jnp.einsum(pattern, first_op, second_op, preferred_element_type=F32)


def dot(first_op, second_op):
    return jnp.dot(first_op, second_op, preferred_element_type=F32)


def transposed_left(first_op, second_op):
    return lax.dot_general(
        first_op, second_op, (((0,), (0,)), ((), ())), preferred_element_type=F32
    )


def transposed_right(first_op, second_op):
    return lax.dot_general(
        first_op, second_op, (((1,), (1,)), ((), ())), preferred_element_type=F32
    )


def slot_mask(lengths_row, row_count):
    position = jnp.arange(row_count, dtype=jnp.int32)
    segment = jnp.zeros((row_count,), jnp.int32)
    end = jnp.int32(0)
    for j in range(lengths_row.shape[0]):
        end = end + lengths_row[j]
        segment = segment + (position >= end).astype(jnp.int32)
    live_rows = position < end
    segment = jnp.where(live_rows, segment, row_count + position)
    allowed = (segment[:, None] == segment[None, :]) & (position[:, None] >= position[None, :])
    return (allowed, live_rows.astype(F32))


def on_device(
    tokens,
    lengths,
    cotangent,
    norm1_gain,
    norm1_shift,
    joint_weight,
    query_bias,
    value_bias,
    output_weight,
    output_bias,
    norm2_gain,
    norm2_shift,
    expand_weight,
    expand_bias,
    reduce_weight,
    reduce_bias,
):
    n = lax.axis_size("dp")
    t = TENSOR if n % TENSOR == 0 else 1
    b = n // t
    rows, width = tokens.shape
    hid = expand_weight.shape[1]
    br = joint_weight.shape[0]
    hs = reduce_weight.shape[0]
    head_size = width // HEADS
    hl = HEADS // t
    fl = width // t
    me = lax.axis_index("dp")
    mine = me % t
    plane = [[z * t + p for p in range(t)] for z in range(b)]
    column = [[z * t + p for z in range(b)] for p in range(t)]
    swap = [(z * t + p, p * b + z) for z in range(b) for p in range(t)]

    def gather(x, groups):
        return lax.all_gather(x, "dp", axis=0, tiled=True, axis_index_groups=groups)

    def scatter(x, groups):
        return lax.psum_scatter(
            x, "dp", scatter_dimension=0, tiled=True, axis_index_groups=groups
        )

    def exchange(x):
        return lax.all_to_all(
            x, "dp", split_axis=0, concat_axis=0, tiled=True, axis_index_groups=plane
        )

    vecs = [
        norm1_gain, norm1_shift, query_bias, value_bias, output_bias,
        norm2_gain, norm2_shift, expand_bias, reduce_bias,
    ]
    sizes = [v.shape[0] for v in vecs]
    small = lax.all_gather(jnp.concatenate(vecs)[None, :], "dp", axis=0, tiled=True)
    whole, at = [], 0
    for s in sizes:
        whole.append(small[:, at : at + s].reshape(-1).astype(F32))
        at += s
    gain1, shift1, qb, vb, ob, gain2, shift2, eb, rb = whole
    eb = lax.dynamic_slice_in_dim(eb.reshape(b, t, hs), mine, 1, 1).reshape(-1)
    qb = lax.dynamic_slice_in_dim(qb, mine * fl, fl, 0)
    vb = lax.dynamic_slice_in_dim(vb, mine * fl, fl, 0)

    joint_cut = joint_weight.reshape(br, 3, t, fl).transpose(2, 0, 1, 3).reshape(t * br, 3 * fl)
    expand_cut = expand_weight.reshape(br, b, t, hs).transpose(2, 0, 1, 3).reshape(t * br, b * hs)
    out_mine = lax.ppermute(output_weight, "dp", [(d, s) for s, d in swap])
    wout = gather(out_mine, column)
    joint = gather(exchange(joint_cut), column)
    expand = gather(exchange(expand_cut), column)
    reduce = gather(reduce_weight, column)

    lens = gather(lengths, plane)
    allowed, _ = jax.vmap(lambda r: slot_mask(r, rows))(lens)
    _, live = slot_mask(lengths[0], rows)

    residual = tokens.astype(F32)
    n1 = gather(layer_norm(residual, gain1, shift1).astype(BF16), plane)
    grad_final = cotangent.astype(F32) * live[:, None]
    gf = gather(grad_final.astype(BF16), plane)

    packed = dot(n1, joint)
    shape4 = (t, rows, hl, head_size)
    q = (packed[:, :fl] + qb).astype(BF16).reshape(shape4)
    k = packed[:, fl : 2 * fl].astype(BF16).reshape(shape4)
    v = (packed[:, 2 * fl :] + vb).astype(BF16).reshape(shape4)
    scale = head_size ** (-0.5)
    scores = contract("gqhd,gkhd->ghqk", q, k) * scale
    scores = jnp.where(allowed[:, None], scores, -1e30)
    top = jnp.max(scores, axis=-1, keepdims=True)
    logsum = top + jnp.log(jnp.sum(jnp.exp(scores - top), axis=-1, keepdims=True))
    probs = jnp.exp(scores - logsum)
    weights = probs.astype(BF16)
    context = contract("ghqk,gkhd->gqhd", weights, v).astype(BF16).reshape(t * rows, fl)
    middle = (
        residual + scatter(dot(context, wout).astype(BF16), plane).astype(F32) + ob
    )
    n2 = gather(layer_norm(middle, gain2, shift2).astype(BF16), plane)
    before = dot(n2, expand) + eb
    active = activation(before).astype(BF16)
    final = middle + scatter(dot(active, reduce).astype(BF16), plane).astype(F32) + rb
    layer_output = final.astype(BF16)

    grad_rb = jnp.sum(grad_final, axis=0)
    g_reduce = transposed_left(active, gf)
    _, curve_back = jax.vjp(activation, before)
    gb = curve_back(transposed_right(gf, reduce))[0]
    grad_eb = jnp.sum(gb, axis=0)
    gbl = gb.astype(BF16)
    g_expand = transposed_left(n2, gbl)
    gn2 = scatter(transposed_right(gbl, expand).astype(BF16), plane).astype(F32)
    _, back2 = jax.vjp(layer_norm, middle, gain2, shift2)
    gmn, grad_g2, grad_s2 = back2(gn2)
    gm_own = grad_final + gmn
    grad_ob = jnp.sum(gm_own, axis=0)
    gm = gather(gm_own.astype(BF16), plane)
    g_out = transposed_left(context, gm)
    gctx = transposed_right(gm, wout).astype(BF16).reshape(shape4)
    gp = contract("gqhd,gkhd->ghqk", gctx, v)
    gv = contract("ghqk,gqhd->gkhd", weights, gctx).reshape(t * rows, fl)
    centre = jnp.sum(probs * gp, axis=-1, keepdims=True)
    gs = (probs * (gp - centre) * scale).astype(BF16)
    gq = contract("ghqk,gkhd->gqhd", gs, k).reshape(t * rows, fl)
    gk = contract("ghqk,gqhd->gkhd", gs, q).reshape(t * rows, fl)
    grad_qb = jnp.sum(gq, axis=0)
    grad_vb = jnp.sum(gv, axis=0)
    gpacked = jnp.concatenate([gq, gk, gv], axis=1).astype(BF16)
    g_joint = transposed_left(n1, gpacked)
    gn1 = scatter(transposed_right(gpacked, joint).astype(BF16), plane).astype(F32)
    _, back1 = jax.vjp(layer_norm, residual, gain1, shift1)
    gtn, grad_g1, grad_s1 = back1(gn1)
    grad_tokens = gm_own + gtn

    reduce_out = scatter(g_reduce.astype(BF16), column).astype(F32)
    expand_out = (
        exchange(scatter(g_expand.astype(BF16), column))
        .reshape(t, br, b, hs).transpose(1, 2, 0, 3).reshape(br, hid).astype(F32)
    )
    joint_out = (
        exchange(scatter(g_joint.astype(BF16), column))
        .reshape(t, br, 3, fl).transpose(1, 2, 0, 3).reshape(br, 3 * width).astype(F32)
    )
    out_out = lax.ppermute(scatter(g_out.astype(BF16), column), "dp", swap).astype(F32)

    def place(x):
        return lax.dynamic_update_slice_in_dim(jnp.zeros((width,), F32), x, mine * fl, 0)

    full_eb = lax.dynamic_update_slice_in_dim(
        jnp.zeros((b, t, hs), F32), grad_eb.reshape(b, 1, hs), mine, 1
    )
    grads = [grad_g1, grad_s1, place(grad_qb), place(grad_vb), grad_ob, grad_g2, grad_s2, full_eb, grad_rb]
    sums = lax.psum_scatter(
        jnp.concatenate([g.reshape(n, -1) for g in grads], axis=1),
        "dp", scatter_dimension=0, tiled=True,
    )[0]
    pieces, at = [], 0
    for s in sizes:
        pieces.append(sums[at : at + s])
        at += s
    return (
        layer_output, grad_tokens, pieces[0], pieces[1], joint_out, pieces[2], pieces[3],
        out_out, pieces[4], pieces[5], pieces[6], expand_out, pieces[7], reduce_out, pieces[8],
    )


def cut(ref, index, size):
    return ref.at[pl.ds(pl.multiple_of(index * size, size), size)]


def take(ref, index, size):
    return ref[pl.ds(pl.multiple_of(index * size, size), size), :]


def put(ref, index, size, value):
    ref[pl.ds(pl.multiple_of(index * size, size), size), :] = value


def loop(low, high, step):
    def body(i, carry):
        step(i)
        return carry

    lax.fori_loop(low, high, body, 0)


def norm_stats(x):
    average = jnp.mean(x, axis=-1, keepdims=True)
    centred = x - average
    spread = jnp.mean(centred * centred, axis=-1, keepdims=True)
    rstd = lax.rsqrt(spread + EPSILON)
    return centred * rstd, rstd


def norm_back(xhat, rstd, grad_out, gain):
    scaled = grad_out * gain
    first = jnp.mean(scaled, axis=-1, keepdims=True)
    second = jnp.mean(scaled * xhat, axis=-1, keepdims=True)
    grad_gain = jnp.sum(grad_out * xhat, axis=0, keepdims=True)
    grad_shift = jnp.sum(grad_out, axis=0, keepdims=True)
    return rstd * (scaled - first - xhat * second), grad_gain, grad_shift


SMALL_P, SMALL_Z = 0, 8
A2A_J, A2A_E = 12, 20
Z_J, Z_E, Z_R, Z_O, SIB_O = 28, 32, 36, 40, 44
AG_N1, AG_GF, AG_N2, AG_GM = 48, 56, 64, 72
RS_0 = 80
G_E, G_R, G_J, G_O, G_SIB = 112, 116, 120, 124, 128
BACK_E, BACK_J = 132, 140
VEC_P, VEC_Z = 148, 156
SEMS = 160


def kernel(
    seqs,
    tok, cot, joint_in, out_in, expand_in, reduce_in, small_in,
    layer_out, gtok_out, gjoint_out, gout_out, gexp_out, gred_out, vec_out,
    small, jstage, estage, joint_w, exp_w, red_w, wo_half, wo_sib, wout,
    n1, n2, gf, gm, qkv, probs, ctx, act, gbl, gpk,
    csend, crecv, hsend, hrecv, own, middle, gmid,
    ge_send, ge_recv, ge_own, gr_send, gr_recv, gr_own,
    gj_send, gj_recv, gj_own, go_full, go_sib, go_send, go_recv,
    ge_back, gj_back, vs_own, vs_recv, vz_own, vz_recv, bias_acc, ebias_acc,
    ssem, rsem,
):
    T = TENSOR
    rows, width = tok.shape
    br = joint_in.shape[0]
    me = lax.axis_index("dp")
    n = lax.axis_size("dp")
    b = n // T
    z = me // T
    p = me % T
    c = p // 2
    k = p % 2
    sib = z * T + 2 * c + (1 - k)
    hs = reduce_in.shape[0]
    fl = width // T
    hd = width // HEADS
    hl = HEADS // T
    kb = br * T

    def chip(dc):
        return ((c // 2 + dc // 2) % 2) * 2 + (c % 2 + dc % 2) % 2

    def dev(c2, k2):
        return z * T + 2 * c2 + k2

    def up(d):
        return ((z + d) % b) * T + p

    def down(d):
        return (z - d + b) % b

    def rc(src, dst, base, i, device):
        return pltpu.make_async_remote_copy(
            src_ref=src, dst_ref=dst, send_sem=ssem.at[base + i], recv_sem=rsem.at[base + i],
            device_id=(device,), device_id_type=pl.DeviceIdType.MESH,
        )

    def start(src, dst, base, i, device):
        rc(src, dst, base, i, device).start()

    def arrive(dst, base, i):
        rc(dst, dst, base, i, sib).wait_recv()

    def sent(src, base, low, high):
        loop(low, high, lambda i: rc(src, src, base, i, sib).wait_send())

    barrier = pltpu.get_barrier_semaphore()
    loop(1, T, lambda d: pl.semaphore_signal(
        barrier, inc=1, device_id=(z * T + (p + d) % T,), device_id_type=pl.DeviceIdType.MESH))
    loop(1, b, lambda d: pl.semaphore_signal(
        barrier, inc=1, device_id=(up(d),), device_id_type=pl.DeviceIdType.MESH))
    pl.semaphore_wait(barrier, T - 1 + b - 1)

    small[me] = small_in[...]
    loop(1, T, lambda d: start(small.at[me], small.at[me], SMALL_P, d, z * T + (p + d) % T))

    for q in range(T):
        c2, k2 = q // 2, q % 2
        pieces = [
            joint_in[:, w * width + (c2 + 4 * (hl * k2 + j)) * hd : w * width + (c2 + 4 * (hl * k2 + j) + 1) * hd]
            for w in range(3) for j in range(hl)
        ]
        jstage[q * br : (q + 1) * br, :] = jnp.concatenate(pieces, axis=1)
    put(joint_w, z * T + p, br, take(jstage, p, br))

    def send_joint(d):
        q = (p + d) % T
        start(cut(jstage, q, br), cut(joint_w, z * T + p, br), A2A_J, d, z * T + q)

    loop(1, T, send_joint)
    for q in range(T):
        pieces = [expand_in[:, (e * T + q) * hs : (e * T + q + 1) * hs] for e in range(b)]
        estage[q * br : (q + 1) * br, :] = jnp.concatenate(pieces, axis=1)
    put(exp_w, z * T + p, br, take(estage, p, br))

    def send_expand(d):
        q = (p + d) % T
        start(cut(estage, q, br), cut(exp_w, z * T + p, br), A2A_E, d, z * T + q)

    loop(1, T, send_expand)
    put(red_w, z, hs, reduce_in[...])
    put(wo_half, z, br, out_in[...])

    loop(1, T, lambda d: arrive(small.at[z * T + (p - d + T) % T], SMALL_P, d))
    plane_small = small.at[pl.ds(z * T, T)]
    loop(1, b, lambda d: start(plane_small, plane_small, SMALL_Z, d, up(d)))
    loop(1, T, lambda d: arrive(cut(joint_w, z * T + (p - d + T) % T, br), A2A_J, d))
    loop(1, b, lambda d: start(cut(joint_w, z, kb), cut(joint_w, z, kb), Z_J, d, up(d)))
    loop(1, b, lambda d: start(cut(wo_half, z, br), cut(wo_half, z, br), Z_O, d, up(d)))
    xhat1, rstd1 = norm_stats(tok[...].astype(F32))
    loop(1, b, lambda d: arrive(small.at[pl.ds(down(d) * T, T)], SMALL_Z, d))

    per_row = n // T
    table = jnp.sum(small[...].reshape(T, per_row, 16, 128), axis=1)

    def vector(r):
        return jnp.concatenate([table[s, r : r + 1, :] for s in range(T)], axis=1)

    def place(ref, value):
        put(ref, p, rows, value)

    def gather_start(ref, base):
        mine = cut(ref, p, rows)
        loop(1, 4, lambda dc: start(mine, mine, base, dc, dev(chip(dc), k)))
        start(mine, mine, base + 4, 0, sib)

    def gather_finish(ref, base):
        def forward(dc):
            block = cut(ref, 2 * chip(dc) + k, rows)
            arrive(block, base, dc)
            start(block, block, base + 4, dc, sib)

        loop(1, 4, forward)
        loop(0, 4, lambda dc: arrive(cut(ref, 2 * chip(dc) + 1 - k, rows), base + 4, dc))

    place(n1, (xhat1 * vector(0) + vector(1)).astype(BF16))
    gather_start(n1, AG_N1)

    loop(1, T, lambda d: arrive(cut(exp_w, z * T + (p - d + T) % T, br), A2A_E, d))
    loop(1, b, lambda d: start(cut(exp_w, z, kb), cut(exp_w, z, kb), Z_E, d, up(d)))
    loop(1, b, lambda d: start(reduce_in, cut(red_w, z, hs), Z_R, d, up(d)))

    ends = small[me, 9:10, :]
    column_pos = lax.broadcasted_iota(jnp.int32, (rows, 1), 0).astype(F32)
    row_pos = lax.broadcasted_iota(jnp.int32, (1, rows), 1).astype(F32)
    live = (column_pos < ends[:, seqs - 1 : seqs]).astype(F32)
    grad_final = cot[...].astype(F32) * live
    place(gf, grad_final.astype(BF16))
    gather_start(gf, AG_GF)

    def feature_bias(r):
        total = jnp.zeros((1, 128), F32)
        for j in range(hl):
            for k2 in range(2):
                total += small[(hl * k + j) * T + 2 * c + k2, r : r + 1, :]
        return total

    qb, vb = feature_bias(2), feature_bias(3)
    eb = jnp.concatenate([small[e * T + p, 8:9, :] for e in range(b)], axis=1)

    gather_finish(n1, AG_N1)
    loop(1, b, lambda d: arrive(cut(wo_half, down(d), br), Z_O, d))
    give = cut(wo_half, 1 - k, hl * br)
    start(give, wo_sib, SIB_O, 0, sib)
    loop(1, b, lambda d: arrive(cut(joint_w, down(d), kb), Z_J, d))
    arrive(wo_sib, SIB_O, 0)
    kept = take(wo_half, k, hl * br)
    other = wo_sib[...]
    low = jnp.where(k == 0, kept, other)
    high = jnp.where(k == 0, other, kept)
    for j in range(hl):
        wout[2 * j * br : (2 * j + 1) * br, :] = low[j * br : (j + 1) * br]
        wout[(2 * j + 1) * br : (2 * j + 2) * br, :] = high[j * br : (j + 1) * br]

    scale = hd ** (-0.5)

    def reduce_loop(slots, compute):
        def step(i):
            dc = (i + 1) % 4
            c2 = chip(dc)
            theirs = i < 4
            g = jnp.where(theirs, 2 * c2 + 1 - k, 2 * c2 + k)
            parts = compute(g)

            @pl.when(i < 4)
            def _():
                for r, part in zip(slots, parts):
                    put(csend.at[r], c2, rows, part.astype(BF16))
                    start(cut(csend.at[r], c2, rows), cut(crecv.at[r], c2, rows), RS_0 + 8 * r, c2, sib)

            @pl.when(i >= 4)
            def _():
                for r, part in zip(slots, parts):
                    arrive(cut(crecv.at[r], c2, rows), RS_0 + 8 * r, c2)
                    total = part + take(crecv.at[r], c2, rows).astype(F32)
                    own[r] = total
                    put(hsend.at[r], dc, rows, total.astype(BF16))

            @pl.when((i >= 4) & (i < 7))
            def _():
                for r in slots:
                    start(cut(hsend.at[r], dc, rows), cut(hrecv.at[r], dc, rows), RS_0 + 8 * r + 4, dc, dev(c2, k))

        loop(0, 8, step)

    def reduce_finish(r):
        total = own[r]
        for dc in range(1, 4):
            arrive(cut(hrecv.at[r], dc, rows), RS_0 + 8 * r + 4, dc)
            total += hrecv[r, dc * rows : (dc + 1) * rows, :].astype(F32)
        return total

    def attend(g):
        packed = dot(take(n1, g, rows), joint_w[...])
        q = (packed[:, :fl] + qb).astype(BF16)
        kk = packed[:, fl : 2 * fl].astype(BF16)
        v = (packed[:, 2 * fl :] + vb).astype(BF16)
        put(qkv, g, rows, jnp.concatenate([q, kk, v], axis=1))
        bounds = small[z * T + g, 9:10, :]
        seg_q = jnp.zeros((rows, 1), F32)
        seg_k = jnp.zeros((1, rows), F32)
        for j in range(seqs):
            end = bounds[:, j : j + 1]
            seg_q += (column_pos >= end).astype(F32)
            seg_k += (row_pos >= end).astype(F32)
        last = bounds[:, seqs - 1 : seqs]
        seg_q = jnp.where(column_pos < last, seg_q, rows + column_pos)
        seg_k = jnp.where(row_pos < last, seg_k, rows + row_pos)
        allowed = (seg_q == seg_k) & (column_pos >= row_pos)
        outs = []
        for j in range(hl):
            at = slice(j * hd, (j + 1) * hd)
            scores = transposed_right(q[:, at], kk[:, at]) * scale
            scores = jnp.where(allowed, scores, -1e30)
            top = jnp.max(scores, axis=-1, keepdims=True)
            logsum = top + jnp.log(jnp.sum(jnp.exp(scores - top), axis=-1, keepdims=True))
            prob = jnp.exp(scores - logsum)
            put(probs, g * hl + j, rows, prob)
            outs.append(dot(prob.astype(BF16), v[:, at]))
        context = jnp.concatenate(outs, axis=1).astype(BF16)
        put(ctx, g, rows, context)
        return [dot(context, wout[...])]

    reduce_loop([0], attend)
    gather_finish(gf, AG_GF)
    mid = tok[...].astype(F32) + reduce_finish(0) + vector(4)
    middle[...] = mid
    xhat2, rstd2 = norm_stats(mid)
    place(n2, (xhat2 * vector(5) + vector(6)).astype(BF16))
    gather_start(n2, AG_N2)
    gather_finish(n2, AG_N2)
    loop(1, b, lambda d: arrive(cut(exp_w, down(d), kb), Z_E, d))
    loop(1, b, lambda d: arrive(cut(red_w, down(d), hs), Z_R, d))
    ebias_acc[...] = jnp.zeros_like(ebias_acc)

    def feed(g):
        before = dot(take(n2, g, rows), exp_w[...]) + eb
        square = before * before
        curve = jnp.tanh(TANH_SCALE * (before + CUBIC_TERM * before * square))
        active = (0.5 * before * (1.0 + curve)).astype(BF16)
        put(act, g, rows, active)
        grad_active = transposed_right(take(gf, g, rows), red_w[...])
        slope = 0.5 * (1.0 + curve) + 0.5 * before * (1.0 - curve * curve) * TANH_SCALE * (
            1.0 + 3.0 * CUBIC_TERM * square
        )
        grad_before = grad_active * slope
        ebias_acc[...] += jnp.sum(grad_before, axis=0, keepdims=True)
        low_grad = grad_before.astype(BF16)
        put(gbl, g, rows, low_grad)
        return [transposed_right(low_grad, exp_w[...]), dot(active, red_w[...])]

    reduce_loop([2, 1], feed)

    def weight_grad(left, cols, right, send, recv, mine, base):
        def step(i):
            d = i % b
            to = (z + d) % b
            part = transposed_left(
                left[:, pl.ds(pl.multiple_of(to * cols, cols), cols)], right[...]
            )

            @pl.when(i < b)
            def _():
                put(send, d, cols, part.astype(BF16))
                start(cut(send, d, cols), cut(recv, d, cols), base, d, up(d))

            @pl.when(i == b)
            def _():
                mine[...] = part

        loop(1, b + 1, step)

    weight_grad(act, hs, gf, gr_send, gr_recv, gr_own, G_R)
    grad_n2 = reduce_finish(2)
    mid = middle[...]
    xhat2, rstd2 = norm_stats(mid)
    row_grad, grad_g2, grad_s2 = norm_back(xhat2, rstd2, grad_n2, vector(5))
    grad_final = cot[...].astype(F32) * live
    grad_mid = grad_final + row_grad
    gmid[...] = grad_mid
    place(gm, grad_mid.astype(BF16))
    gather_start(gm, AG_GM)
    vs_own[...] = jnp.zeros_like(vs_own)
    vs_own[2:3, :] = jnp.sum(grad_mid, axis=0, keepdims=True)
    vs_own[3:4, :] = grad_g2
    vs_own[4:5, :] = grad_s2
    vs_own[5:6, :] = jnp.sum(grad_final, axis=0, keepdims=True)
    weight_grad(n2, kb, gbl, ge_send, ge_recv, ge_own, G_E)
    gather_finish(gm, AG_GM)
    bias_acc[...] = jnp.zeros_like(bias_acc)

    def attend_back(g):
        grad_ctx = transposed_right(take(gm, g, rows), wout[...]).astype(BF16)
        held = take(qkv, g, rows)
        gqs, gks, gvs = [], [], []
        for j in range(hl):
            at = slice(j * hd, (j + 1) * hd)
            q = held[:, j * hd : (j + 1) * hd]
            kk = held[:, fl + j * hd : fl + (j + 1) * hd]
            v = held[:, 2 * fl + j * hd : 2 * fl + (j + 1) * hd]
            prob = take(probs, g * hl + j, rows)
            grad_prob = transposed_right(grad_ctx[:, at], v)
            gvs.append(transposed_left(prob.astype(BF16), grad_ctx[:, at]))
            centre = jnp.sum(prob * grad_prob, axis=-1, keepdims=True)
            grad_score = (prob * (grad_prob - centre) * scale).astype(BF16)
            gqs.append(dot(grad_score, kk))
            gks.append(transposed_left(grad_score, q))
        packed = jnp.concatenate(gqs + gks + gvs, axis=1)
        bias_acc[...] += jnp.sum(packed, axis=0, keepdims=True)
        low_grad = packed.astype(BF16)
        put(gpk, g, rows, low_grad)
        return [transposed_right(low_grad, joint_w[...])]

    reduce_loop([3], attend_back)
    weight_grad(n1, kb, gpk, gj_send, gj_recv, gj_own, G_J)
    grad_out = transposed_left(ctx[...], gm[...])
    evens = jnp.concatenate([grad_out[2 * j * br : (2 * j + 1) * br] for j in range(hl)], axis=0)
    odds = jnp.concatenate([grad_out[(2 * j + 1) * br : (2 * j + 2) * br] for j in range(hl)], axis=0)
    keep = jnp.where(k == 0, evens, odds)
    pass_on = jnp.where(k == 0, odds, evens)
    put(go_full, k, hl * br, keep.astype(BF16))
    go_sib[...] = pass_on.astype(BF16)
    start(go_sib, cut(go_full, k, hl * br), G_SIB, 0, sib)

    grad_n1 = reduce_finish(3)
    xhat1, rstd1 = norm_stats(tok[...].astype(F32))
    row_grad, grad_g1, grad_s1 = norm_back(xhat1, rstd1, grad_n1, vector(0))
    gtok_out[...] = gmid[...] + row_grad
    vs_own[0:1, :] = grad_g1
    vs_own[1:2, :] = grad_s1
    vs_own[6:7, : b * hs] = ebias_acc[...]
    vs_own[6:7, b * hs : b * hs + fl] = bias_acc[:, :fl]
    vs_own[6:7, b * hs + fl : b * hs + 2 * fl] = bias_acc[:, 2 * fl :]
    loop(1, T, lambda d: start(vs_own, vs_recv.at[p], VEC_P, d, z * T + (p + d) % T))
    vs_recv[p] = vs_own[...]

    arrive(cut(go_full, 1 - k, hl * br), G_SIB, 0)

    def send_out(d):
        to = (z + d) % b
        start(cut(go_full, to, br), cut(go_recv, d, br), G_O, d, up(d))

    loop(1, b, send_out)
    layer_out[...] = (middle[...] + reduce_finish(1) + vector(7)).astype(BF16)

    loop(1, T, lambda d: arrive(vs_recv.at[(p - d + T) % T], VEC_P, d))
    vz_own[0:8, :] = jnp.sum(vs_recv[:, 0:8, :], axis=0)
    for q in range(T):
        vz_own[8 + q : 9 + q, :] = vs_recv[q, 6:7, :]
    loop(1, b, lambda d: start(vz_own, vz_recv.at[d], VEC_Z, d, up(d)))

    def collect(recv, mine, size, base):
        total = mine
        for d in range(1, b):
            arrive(cut(recv, d, size), base, d)
            total += recv[d * size : (d + 1) * size, :].astype(F32)
        return total

    gred_out[...] = collect(gr_recv, gr_own[...], hs, G_R)

    def back(mine, landing, base):
        put(landing, p, br, take(mine, p, br))

        def step(d):
            q = (p + d) % T
            start(cut(mine, q, br), cut(landing, p, br), base, d, z * T + q)

        loop(1, T, step)

    ge_own[...] = collect(ge_recv, ge_own[...], kb, G_E)
    back(ge_own, ge_back, BACK_E)
    gj_own[...] = collect(gj_recv, gj_own[...], kb, G_J)
    back(gj_own, gj_back, BACK_J)
    gout_out[...] = collect(go_recv, take(go_full, z, br).astype(F32), br, G_O)
    total = vz_own[...]
    for d in range(1, b):
        arrive(vz_recv.at[d], VEC_Z, d)
        total += vz_recv[d]
    vec_out[...] = total
    loop(1, T, lambda d: arrive(cut(ge_back, (p - d + T) % T, br), BACK_E, d))
    for q in range(T):
        for e in range(b):
            gexp_out[:, (e * T + q) * hs : (e * T + q + 1) * hs] = ge_back[
                q * br : (q + 1) * br, e * hs : (e + 1) * hs
            ]
    loop(1, T, lambda d: arrive(cut(gj_back, (p - d + T) % T, br), BACK_J, d))
    for w in range(3):
        for j in range(hl):
            at = slice((w * hl + j) * hd, (w * hl + j + 1) * hd)
            for k2 in range(2):
                for half in range(2):
                    q0, q1 = 4 * half + k2, 4 * half + 2 + k2
                    head = 2 * half + 4 * (hl * k2 + j)
                    gjoint_out[:, w * width + head * hd : w * width + (head + 2) * hd] = (
                        jnp.concatenate(
                            [gj_back[q0 * br : (q0 + 1) * br, at], gj_back[q1 * br : (q1 + 1) * br, at]],
                            axis=1,
                        )
                    )

    sent(small.at[me], SMALL_P, 1, T)
    sent(plane_small, SMALL_Z, 1, b)
    sent(cut(jstage, 0, br), A2A_J, 1, T)
    sent(cut(estage, 0, br), A2A_E, 1, T)
    sent(cut(joint_w, 0, kb), Z_J, 1, b)
    sent(cut(exp_w, 0, kb), Z_E, 1, b)
    sent(reduce_in, Z_R, 1, b)
    sent(cut(wo_half, 0, br), Z_O, 1, b)
    sent(wo_sib, SIB_O, 0, 1)
    for base in (AG_N1, AG_GF, AG_N2, AG_GM):
        sent(cut(n1, 0, rows), base, 1, 8)
    for r in range(4):
        sent(cut(csend.at[0], 0, rows), RS_0 + 8 * r, 0, 4)
        sent(cut(csend.at[0], 0, rows), RS_0 + 8 * r, 5, 8)
    sent(cut(ge_send, 0, kb), G_E, 1, b)
    sent(cut(gr_send, 0, hs), G_R, 1, b)
    sent(cut(gj_send, 0, kb), G_J, 1, b)
    sent(go_sib, G_SIB, 0, 1)
    sent(cut(go_recv, 0, br), G_O, 1, b)
    sent(cut(ge_own, 0, br), BACK_E, 1, T)
    sent(cut(gj_own, 0, br), BACK_J, 1, T)
    sent(vs_own, VEC_P, 1, T)
    sent(vz_own, VEC_Z, 1, b)


def fused(
    tokens, lengths, cotangent, norm1_gain, norm1_shift, joint_weight, query_bias, value_bias,
    output_weight, output_bias, norm2_gain, norm2_shift, expand_weight, expand_bias,
    reduce_weight, reduce_bias,
):
    n = lax.axis_size("dp")
    T = TENSOR
    b = n // T
    me = lax.axis_index("dp")
    rows, width = tokens.shape
    br = joint_weight.shape[0]
    hs = reduce_weight.shape[0]
    fl = width // T
    hl = HEADS // T
    seqs = lengths.shape[1]
    z, p = me // T, me % T
    c, k = p // 2, p % 2

    plain = (me % (128 // br)) * br
    lane = jnp.arange(128)
    vecs = [norm1_gain, norm1_shift, query_bias, value_bias, output_bias, norm2_gain, norm2_shift, reduce_bias]
    head = ((z % hl) * 2 + k) * br

    def laid(v, at):
        tiled = jnp.tile(v.astype(F32), 128 // br)
        return jnp.where((lane >= at) & (lane < at + br), tiled, 0.0)

    ends, running = [], jnp.float32(0)
    for j in range(seqs):
        running = running + lengths[0, j].astype(F32)
        ends.append(running)
    lines = [laid(v, head if r in (2, 3) else plain) for r, v in enumerate(vecs)]
    lines.append(expand_bias.astype(F32))
    lines.append(jnp.pad(jnp.stack(ends), (0, 128 - seqs)))
    block = jnp.pad(jnp.stack(lines), ((0, 16 - len(lines)), (0, 0)))

    kb, f, fj, tt = br * T, b * hs, 3 * fl, T * rows
    vm = pltpu.VMEM
    scratch = [
        vm((n, 16, 128), F32), vm((kb, fj), BF16), vm((kb, f), BF16), vm((width, fj), BF16),
        vm((width, f), BF16), vm((f, width), BF16), vm((b * br, width), BF16),
        vm((hl * br, width), BF16), vm((fl, width), BF16),
        vm((tt, width), BF16), vm((tt, width), BF16), vm((tt, width), BF16), vm((tt, width), BF16),
        vm((tt, fj), BF16), vm((tt * hl, rows), F32), vm((tt, fl), BF16),
        vm((tt, f), BF16), vm((tt, f), BF16), vm((tt, fj), BF16),
        vm((4, 4 * rows, width), BF16), vm((4, 4 * rows, width), BF16),
        vm((4, 4 * rows, width), BF16), vm((4, 4 * rows, width), BF16),
        vm((4, rows, width), F32), vm((rows, width), F32), vm((rows, width), F32),
        vm((b * kb, f), BF16), vm((b * kb, f), BF16), vm((kb, f), F32),
        vm((b * hs, width), BF16), vm((b * hs, width), BF16), vm((hs, width), F32),
        vm((b * kb, fj), BF16), vm((b * kb, fj), BF16), vm((kb, fj), F32),
        vm((b * br, width), BF16), vm((hl * br, width), BF16), vm((hl * br, width), BF16), vm((b * br, width), BF16),
        vm((kb, f), F32), vm((kb, fj), F32),
        vm((16, width), F32), vm((T, 16, width), F32), vm((16, width), F32), vm((b, 16, width), F32),
        vm((1, fj), F32), vm((1, f), F32),
        pltpu.SemaphoreType.DMA((SEMS,)), pltpu.SemaphoreType.DMA((SEMS,)),
    ]
    sds = jax.ShapeDtypeStruct
    layer_output, grad_tokens, g_joint, g_out, g_exp, g_red, vec = pl.pallas_call(
        functools.partial(kernel, seqs),
        out_shape=(
            sds((rows, width), BF16), sds((rows, width), F32), sds((br, 3 * width), F32),
            sds((br, width), F32), sds((br, expand_weight.shape[1]), F32), sds((hs, width), F32),
            sds((16, width), F32),
        ),
        in_specs=[pl.BlockSpec(memory_space=pltpu.VMEM)] * 7,
        out_specs=tuple([pl.BlockSpec(memory_space=pltpu.VMEM)] * 7),
        scratch_shapes=scratch,
        compiler_params=pltpu.CompilerParams(
            collective_id=0, has_side_effects=True, vmem_limit_bytes=62 * 1024 * 1024
        ),
        name="layer",
    )(tokens, cotangent, joint_weight, output_weight, expand_weight, reduce_weight, block)

    def pick(row):
        return lax.dynamic_slice(row, (me * br,), (br,))

    g_eb = lax.dynamic_slice(vec, (8 + p, z * hs), (1, hs))[0]
    keeper = 2 * c + z // hl
    at = f + ((z % hl) * 2 + k) * br
    g_qb = lax.dynamic_slice(vec, (8 + keeper, at), (1, br))[0]
    g_vb = lax.dynamic_slice(vec, (8 + keeper, at + fl), (1, br))[0]
    return (
        layer_output, grad_tokens, pick(vec[0]), pick(vec[1]), g_joint, g_qb, g_vb, g_out,
        pick(vec[2]), pick(vec[3]), pick(vec[4]), g_exp, g_eb, g_red, pick(vec[5]),
    )


def fits(n, width):
    br = width // n
    return n % TENSOR == 0 and br % 16 == 0 and 2 * br * HEADS == width and n // TENSOR == 2 * (HEADS // TENSOR)


def whole(*args):
    n = lax.axis_size("dp")
    return fused(*args) if fits(n, args[0].shape[1]) else on_device(*args)


def solution(mesh):
    m, v = P("dp", None), P("dp")
    in_specs = (m, m, m, v, v, m, v, v, m, v, v, v, m, v, m, v)
    out_specs = (m, m, v, v, m, v, v, m, v, v, v, m, v, m, v)
    return jax.shard_map(
        whole, mesh=mesh, in_specs=in_specs, out_specs=out_specs, check_vma=False
    )
```

```python
import functools

import jax
import jax.numpy as jnp
from jax import lax
from jax.experimental import pallas as pl
from jax.experimental.pallas import tpu as pltpu
from jax.sharding import PartitionSpec as P

HEADS = 16
TENSOR = 8

EPSILON = 1e-05
TANH_SCALE = 0.7978845608028654
CUBIC_TERM = 0.044715

F32 = jnp.float32
BF16 = jnp.bfloat16


def layer_norm(row_data, gain_vector, shift_vector):
    average = jnp.mean(row_data, axis=-1, keepdims=True)
    centred = row_data - average
    spread = jnp.mean(centred * centred, axis=-1, keepdims=True)
    return centred * lax.rsqrt(spread + EPSILON) * gain_vector + shift_vector


def activation(values_in):
    return (
        0.5
        * values_in
        * (
            1.0
            + jnp.tanh(TANH_SCALE * (values_in + CUBIC_TERM * values_in * values_in * values_in))
        )
    )


def contract(pattern, first_op, second_op):
    return jnp.einsum(pattern, first_op, second_op, preferred_element_type=F32)


def dot(first_op, second_op):
    return jnp.dot(first_op, second_op, preferred_element_type=F32)


def transposed_left(first_op, second_op):
    return lax.dot_general(
        first_op, second_op, (((0,), (0,)), ((), ())), preferred_element_type=F32
    )


def transposed_right(first_op, second_op):
    return lax.dot_general(
        first_op, second_op, (((1,), (1,)), ((), ())), preferred_element_type=F32
    )


def slot_mask(lengths_row, row_count):
    position = jnp.arange(row_count, dtype=jnp.int32)
    segment = jnp.zeros((row_count,), jnp.int32)
    end = jnp.int32(0)
    for j in range(lengths_row.shape[0]):
        end = end + lengths_row[j]
        segment = segment + (position >= end).astype(jnp.int32)
    live_rows = position < end
    segment = jnp.where(live_rows, segment, row_count + position)
    allowed = (segment[:, None] == segment[None, :]) & (position[:, None] >= position[None, :])
    return (allowed, live_rows.astype(F32))


def on_device(
    tokens,
    lengths,
    cotangent,
    norm1_gain,
    norm1_shift,
    joint_weight,
    query_bias,
    value_bias,
    output_weight,
    output_bias,
    norm2_gain,
    norm2_shift,
    expand_weight,
    expand_bias,
    reduce_weight,
    reduce_bias,
):
    n = lax.axis_size("dp")
    t = TENSOR if n % TENSOR == 0 else 1
    b = n // t
    rows, width = tokens.shape
    hid = expand_weight.shape[1]
    br = joint_weight.shape[0]
    hs = reduce_weight.shape[0]
    head_size = width // HEADS
    hl = HEADS // t
    fl = width // t
    me = lax.axis_index("dp")
    mine = me % t
    plane = [[z * t + p for p in range(t)] for z in range(b)]
    column = [[z * t + p for z in range(b)] for p in range(t)]
    swap = [(z * t + p, p * b + z) for z in range(b) for p in range(t)]

    def gather(x, groups):
        return lax.all_gather(x, "dp", axis=0, tiled=True, axis_index_groups=groups)

    def scatter(x, groups):
        return lax.psum_scatter(
            x, "dp", scatter_dimension=0, tiled=True, axis_index_groups=groups
        )

    def exchange(x):
        return lax.all_to_all(
            x, "dp", split_axis=0, concat_axis=0, tiled=True, axis_index_groups=plane
        )

    vecs = [
        norm1_gain, norm1_shift, query_bias, value_bias, output_bias,
        norm2_gain, norm2_shift, expand_bias, reduce_bias,
    ]
    sizes = [v.shape[0] for v in vecs]
    small = lax.all_gather(jnp.concatenate(vecs)[None, :], "dp", axis=0, tiled=True)
    whole, at = [], 0
    for s in sizes:
        whole.append(small[:, at : at + s].reshape(-1).astype(F32))
        at += s
    gain1, shift1, qb, vb, ob, gain2, shift2, eb, rb = whole
    eb = lax.dynamic_slice_in_dim(eb.reshape(b, t, hs), mine, 1, 1).reshape(-1)
    qb = lax.dynamic_slice_in_dim(qb, mine * fl, fl, 0)
    vb = lax.dynamic_slice_in_dim(vb, mine * fl, fl, 0)

    joint_cut = joint_weight.reshape(br, 3, t, fl).transpose(2, 0, 1, 3).reshape(t * br, 3 * fl)
    expand_cut = expand_weight.reshape(br, b, t, hs).transpose(2, 0, 1, 3).reshape(t * br, b * hs)
    out_mine = lax.ppermute(output_weight, "dp", [(d, s) for s, d in swap])
    wout = gather(out_mine, column)
    joint = gather(exchange(joint_cut), column)
    expand = gather(exchange(expand_cut), column)
    reduce = gather(reduce_weight, column)

    lens = gather(lengths, plane)
    allowed, _ = jax.vmap(lambda r: slot_mask(r, rows))(lens)
    _, live = slot_mask(lengths[0], rows)

    residual = tokens.astype(F32)
    n1 = gather(layer_norm(residual, gain1, shift1).astype(BF16), plane)
    grad_final = cotangent.astype(F32) * live[:, None]
    gf = gather(grad_final.astype(BF16), plane)

    packed = dot(n1, joint)
    shape4 = (t, rows, hl, head_size)
    q = (packed[:, :fl] + qb).astype(BF16).reshape(shape4)
    k = packed[:, fl : 2 * fl].astype(BF16).reshape(shape4)
    v = (packed[:, 2 * fl :] + vb).astype(BF16).reshape(shape4)
    scale = head_size ** (-0.5)
    scores = contract("gqhd,gkhd->ghqk", q, k) * scale
    scores = jnp.where(allowed[:, None], scores, -1e30)
    top = jnp.max(scores, axis=-1, keepdims=True)
    logsum = top + jnp.log(jnp.sum(jnp.exp(scores - top), axis=-1, keepdims=True))
    probs = jnp.exp(scores - logsum)
    weights = probs.astype(BF16)
    context = contract("ghqk,gkhd->gqhd", weights, v).astype(BF16).reshape(t * rows, fl)
    middle = (
        residual + scatter(dot(context, wout).astype(BF16), plane).astype(F32) + ob
    )
    n2 = gather(layer_norm(middle, gain2, shift2).astype(BF16), plane)
    before = dot(n2, expand) + eb
    active = activation(before).astype(BF16)
    final = middle + scatter(dot(active, reduce).astype(BF16), plane).astype(F32) + rb
    layer_output = final.astype(BF16)

    grad_rb = jnp.sum(grad_final, axis=0)
    g_reduce = transposed_left(active, gf)
    _, curve_back = jax.vjp(activation, before)
    gb = curve_back(transposed_right(gf, reduce))[0]
    grad_eb = jnp.sum(gb, axis=0)
    gbl = gb.astype(BF16)
    g_expand = transposed_left(n2, gbl)
    gn2 = scatter(transposed_right(gbl, expand).astype(BF16), plane).astype(F32)
    _, back2 = jax.vjp(layer_norm, middle, gain2, shift2)
    gmn, grad_g2, grad_s2 = back2(gn2)
    gm_own = grad_final + gmn
    grad_ob = jnp.sum(gm_own, axis=0)
    gm = gather(gm_own.astype(BF16), plane)
    g_out = transposed_left(context, gm)
    gctx = transposed_right(gm, wout).astype(BF16).reshape(shape4)
    gp = contract("gqhd,gkhd->ghqk", gctx, v)
    gv = contract("ghqk,gqhd->gkhd", weights, gctx).reshape(t * rows, fl)
    centre = jnp.sum(probs * gp, axis=-1, keepdims=True)
    gs = (probs * (gp - centre) * scale).astype(BF16)
    gq = contract("ghqk,gkhd->gqhd", gs, k).reshape(t * rows, fl)
    gk = contract("ghqk,gqhd->gkhd", gs, q).reshape(t * rows, fl)
    grad_qb = jnp.sum(gq, axis=0)
    grad_vb = jnp.sum(gv, axis=0)
    gpacked = jnp.concatenate([gq, gk, gv], axis=1).astype(BF16)
    g_joint = transposed_left(n1, gpacked)
    gn1 = scatter(transposed_right(gpacked, joint).astype(BF16), plane).astype(F32)
    _, back1 = jax.vjp(layer_norm, residual, gain1, shift1)
    gtn, grad_g1, grad_s1 = back1(gn1)
    grad_tokens = gm_own + gtn

    reduce_out = scatter(g_reduce.astype(BF16), column).astype(F32)
    expand_out = (
        exchange(scatter(g_expand.astype(BF16), column))
        .reshape(t, br, b, hs).transpose(1, 2, 0, 3).reshape(br, hid).astype(F32)
    )
    joint_out = (
        exchange(scatter(g_joint.astype(BF16), column))
        .reshape(t, br, 3, fl).transpose(1, 2, 0, 3).reshape(br, 3 * width).astype(F32)
    )
    out_out = lax.ppermute(scatter(g_out.astype(BF16), column), "dp", swap).astype(F32)

    def place(x):
        return lax.dynamic_update_slice_in_dim(jnp.zeros((width,), F32), x, mine * fl, 0)

    full_eb = lax.dynamic_update_slice_in_dim(
        jnp.zeros((b, t, hs), F32), grad_eb.reshape(b, 1, hs), mine, 1
    )
    grads = [grad_g1, grad_s1, place(grad_qb), place(grad_vb), grad_ob, grad_g2, grad_s2, full_eb, grad_rb]
    sums = lax.psum_scatter(
        jnp.concatenate([g.reshape(n, -1) for g in grads], axis=1),
        "dp", scatter_dimension=0, tiled=True,
    )[0]
    pieces, at = [], 0
    for s in sizes:
        pieces.append(sums[at : at + s])
        at += s
    return (
        layer_output, grad_tokens, pieces[0], pieces[1], joint_out, pieces[2], pieces[3],
        out_out, pieces[4], pieces[5], pieces[6], expand_out, pieces[7], reduce_out, pieces[8],
    )


def cut(ref, index, size):
    return ref.at[pl.ds(pl.multiple_of(index * size, size), size)]


def take(ref, index, size):
    return ref[pl.ds(pl.multiple_of(index * size, size), size), :]


def put(ref, index, size, value):
    ref[pl.ds(pl.multiple_of(index * size, size), size), :] = value


def loop(low, high, step):
    def body(i, carry):
        step(i)
        return carry

    lax.fori_loop(low, high, body, 0)


def norm_stats(x):
    average = jnp.mean(x, axis=-1, keepdims=True)
    centred = x - average
    spread = jnp.mean(centred * centred, axis=-1, keepdims=True)
    rstd = lax.rsqrt(spread + EPSILON)
    return centred * rstd, rstd


def norm_back(xhat, rstd, grad_out, gain):
    scaled = grad_out * gain
    first = jnp.mean(scaled, axis=-1, keepdims=True)
    second = jnp.mean(scaled * xhat, axis=-1, keepdims=True)
    grad_gain = jnp.sum(grad_out * xhat, axis=0, keepdims=True)
    grad_shift = jnp.sum(grad_out, axis=0, keepdims=True)
    return rstd * (scaled - first - xhat * second), grad_gain, grad_shift


SMALL_P, SMALL_Z = 0, 8
A2A_J, A2A_E = 12, 20
Z_J, Z_E, Z_R, Z_O, SIB_O = 28, 32, 36, 40, 44
AG_N1, AG_GF, AG_N2, AG_GM = 48, 56, 64, 72
RS_0 = 80
G_E, G_R, G_J, G_O, G_SIB = 112, 116, 120, 124, 128
BACK_E, BACK_J = 132, 140
VEC_P, VEC_Z = 148, 156
SEMS = 160


def kernel(
    seqs,
    tok, cot, joint_in, out_in, expand_in, reduce_in, lens,
    v_g1, v_s1, v_qb, v_vb, v_ob, v_g2, v_s2, v_rb, v_eb,
    layer_out, gtok_out, gjoint_out, gout_out, gexp_out, gred_out, vec_out,
    line, small, small32, jstage, estage, joint_w, exp_w, red_w, wo_half, wo_sib, wout,
    n1, n2, gf, gm, qkv, probs, ctx, act, gbl, gpk,
    slope, csend, crecv, hsend, hrecv, part, middle, gmid,
    ge_send, ge_recv, ge_own, gr_send, gr_recv, gr_own,
    gj_send, gj_recv, gj_own, go_full, go_sib, go_send, go_recv,
    ge_back, gj_back, vs, vz_recv, vp_own, vp, bias_acc, ebias_acc,
    ssem, rsem,
):
    T = TENSOR
    rows, width = tok.shape
    br = joint_in.shape[0]
    me = lax.axis_index("dp")
    n = lax.axis_size("dp")
    b = n // T
    z = me // T
    p = me % T
    c = p // 2
    k = p % 2
    sib = z * T + 2 * c + (1 - k)
    hs = reduce_in.shape[0]
    fl = width // T
    hd = width // HEADS
    hl = HEADS // T
    kb = br * T

    def chip(dc):
        return ((c // 2 + dc // 2) % 2) * 2 + (c % 2 + dc % 2) % 2

    def dev(c2, k2):
        return z * T + 2 * c2 + k2

    def up(d):
        return ((z + d) % b) * T + p

    def down(d):
        return (z - d + b) % b

    def rc(src, dst, base, i, device):
        return pltpu.make_async_remote_copy(
            src_ref=src, dst_ref=dst, send_sem=ssem.at[base + i], recv_sem=rsem.at[base + i],
            device_id=(device,), device_id_type=pl.DeviceIdType.MESH,
        )

    def start(src, dst, base, i, device):
        rc(src, dst, base, i, device).start()

    def arrive(dst, base, i):
        rc(dst, dst, base, i, sib).wait_recv()

    def sent(src, base, low, high):
        loop(low, high, lambda i: rc(src, src, base, i, sib).wait_send())

    barrier = pltpu.get_barrier_semaphore()
    loop(1, T, lambda d: pl.semaphore_signal(
        barrier, inc=1, device_id=(z * T + (p + d) % T,), device_id_type=pl.DeviceIdType.MESH))
    loop(1, b, lambda d: pl.semaphore_signal(
        barrier, inc=1, device_id=(up(d),), device_id_type=pl.DeviceIdType.MESH))
    pl.semaphore_wait(barrier, T - 1 + b - 1)

    lane = lax.broadcasted_iota(jnp.int32, (1, 128), 1)
    plain = (me % (128 // br)) * br
    headed = ((z % hl) * 2 + k) * br
    line[...] = jnp.zeros_like(line)
    for r, v in enumerate((v_g1, v_s1, v_qb, v_vb, v_ob, v_g2, v_s2, v_rb)):
        at = headed if r in (2, 3) else plain
        tiled = jnp.concatenate([v[...].astype(F32).reshape(1, br)] * (128 // br), axis=1)
        line[r : r + 1, :] = jnp.where((lane >= at) & (lane < at + br), tiled, 0.0)
    line[8:9, :] = v_eb[...].astype(F32).reshape(1, hs)
    running = jnp.zeros((1, 1), F32)
    marks = jnp.zeros((1, 128), F32)
    for j in range(seqs):
        running = running + lens[:, j : j + 1].astype(F32)
        marks = jnp.where(lane == j, running, marks)
    line[9:10, :] = marks
    small[p, z] = line[...].astype(BF16)
    loop(1, b, lambda d: start(small.at[p, z], small.at[p, z], SMALL_Z, d, up(d)))

    for q in range(T):
        c2, k2 = q // 2, q % 2
        pieces = [
            joint_in[:, w * width + (c2 + 4 * (hl * k2 + j)) * hd : w * width + (c2 + 4 * (hl * k2 + j) + 1) * hd]
            for w in range(3) for j in range(hl)
        ]
        jstage[q * br : (q + 1) * br, :] = jnp.concatenate(pieces, axis=1)
    put(joint_w, z * T + p, br, take(jstage, p, br))

    def send_joint(d):
        q = (p + d) % T
        start(cut(jstage, q, br), cut(joint_w, z * T + p, br), A2A_J, d, z * T + q)

    loop(1, T, send_joint)
    loop(1, b, lambda d: arrive(small.at[p, down(d)], SMALL_Z, d))
    loop(1, T, lambda d: start(small.at[p], small.at[p], SMALL_P, d, z * T + (p + d) % T))
    for q in range(T):
        pieces = [expand_in[:, (e * T + q) * hs : (e * T + q + 1) * hs] for e in range(b)]
        estage[q * br : (q + 1) * br, :] = jnp.concatenate(pieces, axis=1)
    put(exp_w, z * T + p, br, take(estage, p, br))

    def send_expand(d):
        q = (p + d) % T
        start(cut(estage, q, br), cut(exp_w, z * T + p, br), A2A_E, d, z * T + q)

    loop(1, T, send_expand)
    put(red_w, z, hs, reduce_in[...])
    put(wo_half, z, br, out_in[...])

    loop(1, T, lambda d: arrive(cut(joint_w, z * T + (p - d + T) % T, br), A2A_J, d))
    loop(1, b, lambda d: start(cut(joint_w, z, kb), cut(joint_w, z, kb), Z_J, d, up(d)))
    loop(1, b, lambda d: start(cut(wo_half, z, br), cut(wo_half, z, br), Z_O, d, up(d)))
    xhat1, rstd1 = norm_stats(tok[...].astype(F32))
    loop(1, T, lambda d: arrive(small.at[(p - d + T) % T], SMALL_P, d))
    small32[...] = small[...].astype(F32)
    fold = 128 // br
    halves = [
        sum(small32[h * fold + i] for i in range(1, fold)) + small32[h * fold]
        for h in range(T // fold)
    ]

    def vector(r):
        return jnp.concatenate(
            [half[e, r : r + 1, :] for e in range(b) for half in halves], axis=1
        )

    def place(ref, value):
        put(ref, p, rows, value)

    def gather_start(ref, base):
        mine = cut(ref, p, rows)
        loop(1, 4, lambda dc: start(mine, mine, base, dc, dev(chip(dc), k)))
        start(mine, mine, base + 4, 0, sib)

    def gather_wait(ref, base, dc):
        c2 = chip(dc)

        @pl.when(dc > 0)
        def _():
            block = cut(ref, 2 * c2 + k, rows)
            arrive(block, base, dc)
            start(block, block, base + 4, dc, sib)

        arrive(cut(ref, 2 * c2 + 1 - k, rows), base + 4, dc)

    def gather_finish(ref, base):
        def forward(dc):
            block = cut(ref, 2 * chip(dc) + k, rows)
            arrive(block, base, dc)
            start(block, block, base + 4, dc, sib)

        loop(1, 4, forward)
        loop(0, 4, lambda dc: arrive(cut(ref, 2 * chip(dc) + 1 - k, rows), base + 4, dc))

    place(n1, (xhat1 * vector(0) + vector(1)).astype(BF16))
    gather_start(n1, AG_N1)

    loop(1, T, lambda d: arrive(cut(exp_w, z * T + (p - d + T) % T, br), A2A_E, d))
    loop(1, b, lambda d: start(cut(exp_w, z, kb), cut(exp_w, z, kb), Z_E, d, up(d)))
    loop(1, b, lambda d: start(reduce_in, cut(red_w, z, hs), Z_R, d, up(d)))

    ends = line[9:10, :]
    column_pos = lax.broadcasted_iota(jnp.int32, (rows, 1), 0).astype(F32)
    row_pos = lax.broadcasted_iota(jnp.int32, (1, rows), 1).astype(F32)
    live = (column_pos < ends[:, seqs - 1 : seqs]).astype(F32)
    grad_final = cot[...].astype(F32) * live
    place(gf, grad_final.astype(BF16))

    def feature_bias(r):
        total = jnp.zeros((1, 128), F32)
        for j in range(hl):
            for k2 in range(2):
                total += small32[2 * c + k2, hl * k + j, r : r + 1, :]
        return total

    qb, vb = feature_bias(2), feature_bias(3)
    eb = jnp.concatenate([small32[p, e, 8:9, :] for e in range(b)], axis=1)

    gather_finish(n1, AG_N1)
    gather_start(gf, AG_GF)
    loop(1, b, lambda d: arrive(cut(wo_half, down(d), br), Z_O, d))
    give = cut(wo_half, 1 - k, hl * br)
    start(give, wo_sib, SIB_O, 0, sib)
    loop(1, b, lambda d: arrive(cut(joint_w, down(d), kb), Z_J, d))
    arrive(wo_sib, SIB_O, 0)
    kept = take(wo_half, k, hl * br)
    other = wo_sib[...]
    low = jnp.where(k == 0, kept, other)
    high = jnp.where(k == 0, other, kept)
    for j in range(hl):
        wout[2 * j * br : (2 * j + 1) * br, :] = low[j * br : (j + 1) * br]
        wout[(2 * j + 1) * br : (2 * j + 2) * br, :] = high[j * br : (j + 1) * br]

    scale = hd ** (-0.5)

    def send_hop(r, dc):
        start(cut(hsend.at[r], dc, rows), cut(hrecv.at[r], dc, rows), RS_0 + 8 * r + 4, dc, dev(chip(dc), k))

    def reduce_loop(slots, compute, ready=None, held=()):
        def step(i):
            @pl.when(i < 4)
            def _():
                c2 = chip(i)
                if ready is not None:
                    ready(i)
                for r, value in zip(slots, compute(c2)):
                    first, second = value[:rows], value[rows:]
                    put(csend.at[r], c2, rows, jnp.where(k == 0, second, first).astype(BF16))
                    start(cut(csend.at[r], c2, rows), cut(crecv.at[r], c2, rows), RS_0 + 8 * r, c2, sib)
                    put(part.at[r], i, rows, jnp.where(k == 0, first, second))

            @pl.when(i > 0)
            def _():
                dc = i - 1
                c2 = chip(dc)
                for r in slots:
                    arrive(cut(crecv.at[r], c2, rows), RS_0 + 8 * r, c2)
                    total = take(part.at[r], dc, rows) + take(crecv.at[r], c2, rows).astype(F32)

                    @pl.when(dc == 0)
                    def _():
                        put(part.at[r], 0, rows, total)

                    @pl.when(dc > 0)
                    def _():
                        put(hsend.at[r], dc, rows, total.astype(BF16))
                        if r not in held:
                            send_hop(r, dc)

        loop(0, 5, step)

    def reduce_finish(r):
        total = part[r, 0:rows, :]
        for dc in range(1, 4):
            arrive(cut(hrecv.at[r], dc, rows), RS_0 + 8 * r + 4, dc)
            total += hrecv[r, dc * rows : (dc + 1) * rows, :].astype(F32)
        return total

    pair = 2 * rows

    def attend(c2):
        packed = dot(take(n1, c2, pair), joint_w[...])
        q = (packed[:, :fl] + qb).astype(BF16)
        kk = packed[:, fl : 2 * fl].astype(BF16)
        v = (packed[:, 2 * fl :] + vb).astype(BF16)
        put(qkv, c2, pair, jnp.concatenate([q, kk, v], axis=1))
        blocks = []
        for half in range(2):
            at_row = slice(half * rows, (half + 1) * rows)
            bounds = small32[2 * c2 + half, z, 9:10, :]
            seg_q = jnp.zeros((rows, 1), F32)
            seg_k = jnp.zeros((1, rows), F32)
            for j in range(seqs):
                end = bounds[:, j : j + 1]
                seg_q += (column_pos >= end).astype(F32)
                seg_k += (row_pos >= end).astype(F32)
            last = bounds[:, seqs - 1 : seqs]
            seg_q = jnp.where(column_pos < last, seg_q, rows + column_pos)
            seg_k = jnp.where(row_pos < last, seg_k, rows + row_pos)
            allowed = (seg_q == seg_k) & (column_pos >= row_pos)
            outs = []
            for j in range(hl):
                at = slice(j * hd, (j + 1) * hd)
                scores = transposed_right(q[at_row, at], kk[at_row, at]) * scale
                scores = jnp.where(allowed, scores, -1e30)
                top = jnp.max(scores, axis=-1, keepdims=True)
                logsum = top + jnp.log(jnp.sum(jnp.exp(scores - top), axis=-1, keepdims=True))
                prob = jnp.exp(scores - logsum)
                put(probs, (2 * c2 + half) * hl + j, rows, prob)
                outs.append(dot(prob.astype(BF16), v[at_row, at]))
            blocks.append(jnp.concatenate(outs, axis=1))
        context = jnp.concatenate(blocks, axis=0).astype(BF16)
        put(ctx, c2, pair, context)
        return [dot(context, wout[...])]

    reduce_loop([0], attend)
    gather_finish(gf, AG_GF)
    mid = tok[...].astype(F32) + reduce_finish(0) + vector(4)
    middle[...] = mid
    xhat2, rstd2 = norm_stats(mid)
    place(n2, (xhat2 * vector(5) + vector(6)).astype(BF16))
    gather_start(n2, AG_N2)
    loop(1, b, lambda d: arrive(cut(exp_w, down(d), kb), Z_E, d))

    def feed(dc):
        c2 = chip(dc)
        gather_wait(n2, AG_N2, dc)
        before = dot(take(n2, c2, pair), exp_w[...]) + eb
        square = before * before
        curve = jnp.tanh(TANH_SCALE * (before + CUBIC_TERM * before * square))
        put(act, c2, pair, (0.5 * before * (1.0 + curve)).astype(BF16))
        put(slope, c2, pair, 0.5 * (1.0 + curve) + 0.5 * before * (1.0 - curve * curve) * TANH_SCALE * (
            1.0 + 3.0 * CUBIC_TERM * square
        ))

    loop(0, 4, feed)
    loop(1, b, lambda d: arrive(cut(red_w, down(d), hs), Z_R, d))
    ebias_acc[...] = jnp.zeros_like(ebias_acc)

    def feed_back(c2):
        grad_active = transposed_right(take(gf, c2, pair), red_w[...])
        grad_before = grad_active * take(slope, c2, pair)
        ebias_acc[...] += jnp.sum(grad_before, axis=0, keepdims=True)
        low_grad = grad_before.astype(BF16)
        put(gbl, c2, pair, low_grad)
        return [transposed_right(low_grad, exp_w[...]), dot(take(act, c2, pair), red_w[...])]

    reduce_loop([2, 1], feed_back, held=(1,))

    def weight_grad(left, cols, right, send, recv, mine, base):
        def step(i):
            d = i % b
            to = (z + d) % b
            part = transposed_left(
                left[:, pl.ds(pl.multiple_of(to * cols, cols), cols)], right[...]
            )

            @pl.when(i < b)
            def _():
                put(send, d, cols, part.astype(BF16))
                start(cut(send, d, cols), cut(recv, d, cols), base, d, up(d))

            @pl.when(i == b)
            def _():
                mine[...] = part

        loop(1, b + 1, step)

    weight_grad(act, hs, gf, gr_send, gr_recv, gr_own, G_R)
    grad_n2 = reduce_finish(2)
    mid = middle[...]
    xhat2, rstd2 = norm_stats(mid)
    row_grad, grad_g2, grad_s2 = norm_back(xhat2, rstd2, grad_n2, vector(5))
    grad_final = cot[...].astype(F32) * live
    grad_mid = grad_final + row_grad
    gmid[...] = grad_mid
    place(gm, grad_mid.astype(BF16))
    gather_start(gm, AG_GM)
    seg = width // b

    def vec_put(row, value):
        for e in range(b):
            vs[e, row : row + 1, :] = value[:, e * seg : (e + 1) * seg]

    vs[...] = jnp.zeros_like(vs)
    vec_put(2, jnp.sum(grad_mid, axis=0, keepdims=True))
    vec_put(3, grad_g2)
    vec_put(4, grad_s2)
    vec_put(5, jnp.sum(grad_final, axis=0, keepdims=True))
    weight_grad(n2, kb, gbl, ge_send, ge_recv, ge_own, G_E)
    bias_acc[...] = jnp.zeros_like(bias_acc)

    def attend_back(c2):
        grad_ctx = transposed_right(take(gm, c2, pair), wout[...]).astype(BF16)
        held = take(qkv, c2, pair)
        blocks = []
        for half in range(2):
            at_row = slice(half * rows, (half + 1) * rows)
            gqs, gks, gvs = [], [], []
            for j in range(hl):
                at = slice(j * hd, (j + 1) * hd)
                q = held[at_row, j * hd : (j + 1) * hd]
                kk = held[at_row, fl + j * hd : fl + (j + 1) * hd]
                v = held[at_row, 2 * fl + j * hd : 2 * fl + (j + 1) * hd]
                prob = take(probs, (2 * c2 + half) * hl + j, rows)
                grad_prob = transposed_right(grad_ctx[at_row, at], v)
                gvs.append(transposed_left(prob.astype(BF16), grad_ctx[at_row, at]))
                centre = jnp.sum(prob * grad_prob, axis=-1, keepdims=True)
                grad_score = (prob * (grad_prob - centre) * scale).astype(BF16)
                gqs.append(dot(grad_score, kk))
                gks.append(transposed_left(grad_score, q))
            blocks.append(jnp.concatenate(gqs + gks + gvs, axis=1))
        packed = jnp.concatenate(blocks, axis=0)
        bias_acc[...] += jnp.sum(packed, axis=0, keepdims=True)
        low_grad = packed.astype(BF16)
        put(gpk, c2, pair, low_grad)
        return [transposed_right(low_grad, joint_w[...])]

    reduce_loop([3], attend_back, ready=lambda dc: gather_wait(gm, AG_GM, dc))
    loop(1, 4, lambda dc: send_hop(1, dc))
    weight_grad(n1, kb, gpk, gj_send, gj_recv, gj_own, G_J)
    grad_out = transposed_left(ctx[...], gm[...])
    evens = jnp.concatenate([grad_out[2 * j * br : (2 * j + 1) * br] for j in range(hl)], axis=0)
    odds = jnp.concatenate([grad_out[(2 * j + 1) * br : (2 * j + 2) * br] for j in range(hl)], axis=0)
    keep = jnp.where(k == 0, evens, odds)
    pass_on = jnp.where(k == 0, odds, evens)
    put(go_full, k, hl * br, keep.astype(BF16))
    go_sib[...] = pass_on.astype(BF16)
    start(go_sib, cut(go_full, k, hl * br), G_SIB, 0, sib)

    grad_n1 = reduce_finish(3)
    xhat1, rstd1 = norm_stats(tok[...].astype(F32))
    row_grad, grad_g1, grad_s1 = norm_back(xhat1, rstd1, grad_n1, vector(0))
    gtok_out[...] = gmid[...] + row_grad
    vec_put(0, grad_g1)
    vec_put(1, grad_s1)
    for e in range(b):
        j = e % hl
        kept_row = jnp.concatenate(
            [bias_acc[:, j * hd : (j + 1) * hd], bias_acc[:, 2 * fl + j * hd : 2 * fl + (j + 1) * hd]], axis=1
        )
        vs[e, 6:7, :hs] = ebias_acc[:, e * hs : (e + 1) * hs]
        vs[e, 6:7, hs:] = jnp.where(k == e // hl, kept_row, 0.0)
    loop(1, b, lambda d: start(vs.at[(z + d) % b], vz_recv.at[d], VEC_Z, d, up(d)))

    arrive(cut(go_full, 1 - k, hl * br), G_SIB, 0)

    def send_out(d):
        to = (z + d) % b
        start(cut(go_full, to, br), cut(go_recv, d, br), G_O, d, up(d))

    loop(1, b, send_out)
    layer_out[...] = (middle[...] + reduce_finish(1) + vector(7)).astype(BF16)

    total = vs[z]
    for d in range(1, b):
        arrive(vz_recv.at[d], VEC_Z, d)
        total += vz_recv[d]
    vp_own[...] = total
    vp[p] = total
    loop(1, T, lambda d: start(vp_own, vp.at[p], VEC_P, d, z * T + (p + d) % T))

    def collect(recv, mine, size, base):
        total = mine
        for d in range(1, b):
            arrive(cut(recv, d, size), base, d)
            total += recv[d * size : (d + 1) * size, :].astype(F32)
        return total

    gred_out[...] = collect(gr_recv, gr_own[...], hs, G_R)

    def back(mine, landing, base):
        put(landing, p, br, take(mine, p, br))

        def step(d):
            q = (p + d) % T
            start(cut(mine, q, br), cut(landing, p, br), base, d, z * T + q)

        loop(1, T, step)

    ge_own[...] = collect(ge_recv, ge_own[...], kb, G_E)
    back(ge_own, ge_back, BACK_E)
    gj_own[...] = collect(gj_recv, gj_own[...], kb, G_J)
    back(gj_own, gj_back, BACK_J)
    gout_out[...] = collect(go_recv, take(go_full, z, br).astype(F32), br, G_O)
    loop(1, T, lambda d: arrive(vp.at[(p - d + T) % T], VEC_P, d))
    total = jnp.sum(vp[...], axis=0)
    picked = jnp.zeros((8, br), F32)
    for q in range(T):
        picked = jnp.where(p == q, total[:, q * br : (q + 1) * br], picked)
    vec_out[0:8, 0:br] = picked
    vec_out[6:7, :] = vp[p, 6:7, :hs]
    keeper = 2 * c + z // hl
    row = vp[keeper, 6:7, :]
    for i in range(2):
        at = hs + i * hl * br
        vec_out[8 + i : 9 + i, 0:br] = jnp.where(k == 0, row[:, at : at + br], row[:, at + br : at + 2 * br])
    loop(1, T, lambda d: arrive(cut(ge_back, (p - d + T) % T, br), BACK_E, d))
    for q in range(T):
        for e in range(b):
            gexp_out[:, (e * T + q) * hs : (e * T + q + 1) * hs] = ge_back[
                q * br : (q + 1) * br, e * hs : (e + 1) * hs
            ]
    loop(1, T, lambda d: arrive(cut(gj_back, (p - d + T) % T, br), BACK_J, d))
    for w in range(3):
        for j in range(hl):
            at = slice((w * hl + j) * hd, (w * hl + j + 1) * hd)
            for k2 in range(2):
                for half in range(2):
                    q0, q1 = 4 * half + k2, 4 * half + 2 + k2
                    head = 2 * half + 4 * (hl * k2 + j)
                    gjoint_out[:, w * width + head * hd : w * width + (head + 2) * hd] = (
                        jnp.concatenate(
                            [gj_back[q0 * br : (q0 + 1) * br, at], gj_back[q1 * br : (q1 + 1) * br, at]],
                            axis=1,
                        )
                    )

    sent(small.at[p, z], SMALL_Z, 1, b)
    sent(small.at[p], SMALL_P, 1, T)
    sent(cut(jstage, 0, br), A2A_J, 1, T)
    sent(cut(estage, 0, br), A2A_E, 1, T)
    sent(cut(joint_w, 0, kb), Z_J, 1, b)
    sent(cut(exp_w, 0, kb), Z_E, 1, b)
    sent(reduce_in, Z_R, 1, b)
    sent(cut(wo_half, 0, br), Z_O, 1, b)
    sent(wo_sib, SIB_O, 0, 1)
    for base in (AG_N1, AG_GF, AG_N2, AG_GM):
        sent(cut(n1, 0, rows), base, 1, 8)
    for r in range(4):
        sent(cut(csend.at[0], 0, rows), RS_0 + 8 * r, 0, 4)
        sent(cut(csend.at[0], 0, rows), RS_0 + 8 * r, 5, 8)
    sent(cut(ge_send, 0, kb), G_E, 1, b)
    sent(cut(gr_send, 0, hs), G_R, 1, b)
    sent(cut(gj_send, 0, kb), G_J, 1, b)
    sent(go_sib, G_SIB, 0, 1)
    sent(cut(go_recv, 0, br), G_O, 1, b)
    sent(cut(ge_own, 0, br), BACK_E, 1, T)
    sent(cut(gj_own, 0, br), BACK_J, 1, T)
    sent(vs.at[0], VEC_Z, 1, b)
    sent(vp_own, VEC_P, 1, T)


def fused(
    tokens, lengths, cotangent, norm1_gain, norm1_shift, joint_weight, query_bias, value_bias,
    output_weight, output_bias, norm2_gain, norm2_shift, expand_weight, expand_bias,
    reduce_weight, reduce_bias,
):
    n = lax.axis_size("dp")
    T = TENSOR
    b = n // T
    rows, width = tokens.shape
    br = joint_weight.shape[0]
    hs = reduce_weight.shape[0]
    fl = width // T
    hl = HEADS // T
    seqs = lengths.shape[1]
    kb, f, fj, tt = br * T, b * hs, 3 * fl, T * rows
    vm = pltpu.VMEM
    scratch = [
        vm((16, 128), F32), vm((T, b, 16, 128), BF16), vm((T, b, 16, 128), F32), vm((kb, fj), BF16), vm((kb, f), BF16), vm((width, fj), BF16),
        vm((width, f), BF16), vm((f, width), BF16), vm((b * br, width), BF16),
        vm((hl * br, width), BF16), vm((fl, width), BF16),
        vm((tt, width), BF16), vm((tt, width), BF16), vm((tt, width), BF16), vm((tt, width), BF16),
        vm((tt, fj), BF16), vm((tt * hl, rows), F32), vm((tt, fl), BF16),
        vm((tt, f), BF16), vm((tt, f), BF16), vm((tt, fj), BF16), vm((tt, f), F32),
        vm((4, 4 * rows, width), BF16), vm((4, 4 * rows, width), BF16),
        vm((4, 4 * rows, width), BF16), vm((4, 4 * rows, width), BF16),
        vm((4, 4 * rows, width), F32), vm((rows, width), F32), vm((rows, width), F32),
        vm((b * kb, f), BF16), vm((b * kb, f), BF16), vm((kb, f), F32),
        vm((b * hs, width), BF16), vm((b * hs, width), BF16), vm((hs, width), F32),
        vm((b * kb, fj), BF16), vm((b * kb, fj), BF16), vm((kb, fj), F32),
        vm((b * br, width), BF16), vm((hl * br, width), BF16), vm((hl * br, width), BF16), vm((b * br, width), BF16),
        vm((kb, f), F32), vm((kb, fj), F32),
        vm((b, 8, width // b), F32), vm((b, 8, width // b), F32), vm((8, width // b), F32), vm((T, 8, width // b), F32),
        vm((1, fj), F32), vm((1, f), F32),
        pltpu.SemaphoreType.DMA((SEMS,)), pltpu.SemaphoreType.DMA((SEMS,)),
    ]
    sds = jax.ShapeDtypeStruct
    layer_output, grad_tokens, g_joint, g_out, g_exp, g_red, vec = pl.pallas_call(
        functools.partial(kernel, seqs),
        out_shape=(
            sds((rows, width), BF16), sds((rows, width), F32), sds((br, 3 * width), F32),
            sds((br, width), F32), sds((br, expand_weight.shape[1]), F32), sds((hs, width), F32),
            sds((16, hs), F32),
        ),
        in_specs=[pl.BlockSpec(memory_space=pltpu.VMEM)] * 16,
        out_specs=tuple([pl.BlockSpec(memory_space=pltpu.VMEM)] * 7),
        scratch_shapes=scratch,
        compiler_params=pltpu.CompilerParams(
            collective_id=0, has_side_effects=True, vmem_limit_bytes=62 * 1024 * 1024
        ),
        name="layer",
    )(
        tokens, cotangent, joint_weight, output_weight, expand_weight, reduce_weight, lengths,
        norm1_gain, norm1_shift, query_bias, value_bias, output_bias, norm2_gain, norm2_shift,
        reduce_bias, expand_bias,
    )

    piece = [vec[r, :br] for r in range(10)]
    return (
        layer_output, grad_tokens, piece[0], piece[1], g_joint, piece[8], piece[9], g_out,
        piece[2], piece[3], piece[4], g_exp, vec[6], g_red, piece[5],
    )


def fits(n, width):
    br = width // n
    return n % TENSOR == 0 and br % 16 == 0 and 2 * br * HEADS == width and n // TENSOR == 2 * (HEADS // TENSOR)


def whole(*args):
    n = lax.axis_size("dp")
    return fused(*args) if fits(n, args[0].shape[1]) else on_device(*args)


def solution(mesh):
    m, v = P("dp", None), P("dp")
    in_specs = (m, m, m, v, v, m, v, v, m, v, v, v, m, v, m, v)
    out_specs = (m, m, v, v, m, v, v, m, v, v, v, m, v, m, v)
    return jax.shard_map(
        whole, mesh=mesh, in_specs=in_specs, out_specs=out_specs, check_vma=False
    )
```

```python
import functools

import jax
import jax.numpy as jnp
from jax import lax
from jax.experimental import pallas as pl
from jax.experimental.pallas import tpu as pltpu
from jax.sharding import PartitionSpec as P

HEADS = 16
TENSOR = 8

EPSILON = 1e-05
TANH_SCALE = 0.7978845608028654
CUBIC_TERM = 0.044715

F32 = jnp.float32
BF16 = jnp.bfloat16


def layer_norm(row_data, gain_vector, shift_vector):
    average = jnp.mean(row_data, axis=-1, keepdims=True)
    centred = row_data - average
    spread = jnp.mean(centred * centred, axis=-1, keepdims=True)
    return centred * lax.rsqrt(spread + EPSILON) * gain_vector + shift_vector


def activation(values_in):
    return (
        0.5
        * values_in
        * (
            1.0
            + jnp.tanh(TANH_SCALE * (values_in + CUBIC_TERM * values_in * values_in * values_in))
        )
    )


def contract(pattern, first_op, second_op):
    return jnp.einsum(pattern, first_op, second_op, preferred_element_type=F32)


def dot(first_op, second_op):
    return jnp.dot(first_op, second_op, preferred_element_type=F32)


def transposed_left(first_op, second_op):
    return lax.dot_general(
        first_op, second_op, (((0,), (0,)), ((), ())), preferred_element_type=F32
    )


def transposed_right(first_op, second_op):
    return lax.dot_general(
        first_op, second_op, (((1,), (1,)), ((), ())), preferred_element_type=F32
    )


def slot_mask(lengths_row, row_count):
    position = jnp.arange(row_count, dtype=jnp.int32)
    segment = jnp.zeros((row_count,), jnp.int32)
    end = jnp.int32(0)
    for j in range(lengths_row.shape[0]):
        end = end + lengths_row[j]
        segment = segment + (position >= end).astype(jnp.int32)
    live_rows = position < end
    segment = jnp.where(live_rows, segment, row_count + position)
    allowed = (segment[:, None] == segment[None, :]) & (position[:, None] >= position[None, :])
    return (allowed, live_rows.astype(F32))


def on_device(
    tokens,
    lengths,
    cotangent,
    norm1_gain,
    norm1_shift,
    joint_weight,
    query_bias,
    value_bias,
    output_weight,
    output_bias,
    norm2_gain,
    norm2_shift,
    expand_weight,
    expand_bias,
    reduce_weight,
    reduce_bias,
):
    n = lax.axis_size("dp")
    t = TENSOR if n % TENSOR == 0 else 1
    b = n // t
    rows, width = tokens.shape
    hid = expand_weight.shape[1]
    br = joint_weight.shape[0]
    hs = reduce_weight.shape[0]
    head_size = width // HEADS
    hl = HEADS // t
    fl = width // t
    me = lax.axis_index("dp")
    mine = me % t
    plane = [[z * t + p for p in range(t)] for z in range(b)]
    column = [[z * t + p for z in range(b)] for p in range(t)]
    swap = [(z * t + p, p * b + z) for z in range(b) for p in range(t)]

    def gather(x, groups):
        return lax.all_gather(x, "dp", axis=0, tiled=True, axis_index_groups=groups)

    def scatter(x, groups):
        return lax.psum_scatter(
            x, "dp", scatter_dimension=0, tiled=True, axis_index_groups=groups
        )

    def exchange(x):
        return lax.all_to_all(
            x, "dp", split_axis=0, concat_axis=0, tiled=True, axis_index_groups=plane
        )

    vecs = [
        norm1_gain, norm1_shift, query_bias, value_bias, output_bias,
        norm2_gain, norm2_shift, expand_bias, reduce_bias,
    ]
    sizes = [v.shape[0] for v in vecs]
    small = lax.all_gather(jnp.concatenate(vecs)[None, :], "dp", axis=0, tiled=True)
    whole, at = [], 0
    for s in sizes:
        whole.append(small[:, at : at + s].reshape(-1).astype(F32))
        at += s
    gain1, shift1, qb, vb, ob, gain2, shift2, eb, rb = whole
    eb = lax.dynamic_slice_in_dim(eb.reshape(b, t, hs), mine, 1, 1).reshape(-1)
    qb = lax.dynamic_slice_in_dim(qb, mine * fl, fl, 0)
    vb = lax.dynamic_slice_in_dim(vb, mine * fl, fl, 0)

    joint_cut = joint_weight.reshape(br, 3, t, fl).transpose(2, 0, 1, 3).reshape(t * br, 3 * fl)
    expand_cut = expand_weight.reshape(br, b, t, hs).transpose(2, 0, 1, 3).reshape(t * br, b * hs)
    out_mine = lax.ppermute(output_weight, "dp", [(d, s) for s, d in swap])
    wout = gather(out_mine, column)
    joint = gather(exchange(joint_cut), column)
    expand = gather(exchange(expand_cut), column)
    reduce = gather(reduce_weight, column)

    lens = gather(lengths, plane)
    allowed, _ = jax.vmap(lambda r: slot_mask(r, rows))(lens)
    _, live = slot_mask(lengths[0], rows)

    residual = tokens.astype(F32)
    n1 = gather(layer_norm(residual, gain1, shift1).astype(BF16), plane)
    grad_final = cotangent.astype(F32) * live[:, None]
    gf = gather(grad_final.astype(BF16), plane)

    packed = dot(n1, joint)
    shape4 = (t, rows, hl, head_size)
    q = (packed[:, :fl] + qb).astype(BF16).reshape(shape4)
    k = packed[:, fl : 2 * fl].astype(BF16).reshape(shape4)
    v = (packed[:, 2 * fl :] + vb).astype(BF16).reshape(shape4)
    scale = head_size ** (-0.5)
    scores = contract("gqhd,gkhd->ghqk", q, k) * scale
    scores = jnp.where(allowed[:, None], scores, -1e30)
    top = jnp.max(scores, axis=-1, keepdims=True)
    logsum = top + jnp.log(jnp.sum(jnp.exp(scores - top), axis=-1, keepdims=True))
    probs = jnp.exp(scores - logsum)
    weights = probs.astype(BF16)
    context = contract("ghqk,gkhd->gqhd", weights, v).astype(BF16).reshape(t * rows, fl)
    middle = (
        residual + scatter(dot(context, wout).astype(BF16), plane).astype(F32) + ob
    )
    n2 = gather(layer_norm(middle, gain2, shift2).astype(BF16), plane)
    before = dot(n2, expand) + eb
    active = activation(before).astype(BF16)
    final = middle + scatter(dot(active, reduce).astype(BF16), plane).astype(F32) + rb
    layer_output = final.astype(BF16)

    grad_rb = jnp.sum(grad_final, axis=0)
    g_reduce = transposed_left(active, gf)
    _, curve_back = jax.vjp(activation, before)
    gb = curve_back(transposed_right(gf, reduce))[0]
    grad_eb = jnp.sum(gb, axis=0)
    gbl = gb.astype(BF16)
    g_expand = transposed_left(n2, gbl)
    gn2 = scatter(transposed_right(gbl, expand).astype(BF16), plane).astype(F32)
    _, back2 = jax.vjp(layer_norm, middle, gain2, shift2)
    gmn, grad_g2, grad_s2 = back2(gn2)
    gm_own = grad_final + gmn
    grad_ob = jnp.sum(gm_own, axis=0)
    gm = gather(gm_own.astype(BF16), plane)
    g_out = transposed_left(context, gm)
    gctx = transposed_right(gm, wout).astype(BF16).reshape(shape4)
    gp = contract("gqhd,gkhd->ghqk", gctx, v)
    gv = contract("ghqk,gqhd->gkhd", weights, gctx).reshape(t * rows, fl)
    centre = jnp.sum(probs * gp, axis=-1, keepdims=True)
    gs = (probs * (gp - centre) * scale).astype(BF16)
    gq = contract("ghqk,gkhd->gqhd", gs, k).reshape(t * rows, fl)
    gk = contract("ghqk,gqhd->gkhd", gs, q).reshape(t * rows, fl)
    grad_qb = jnp.sum(gq, axis=0)
    grad_vb = jnp.sum(gv, axis=0)
    gpacked = jnp.concatenate([gq, gk, gv], axis=1).astype(BF16)
    g_joint = transposed_left(n1, gpacked)
    gn1 = scatter(transposed_right(gpacked, joint).astype(BF16), plane).astype(F32)
    _, back1 = jax.vjp(layer_norm, residual, gain1, shift1)
    gtn, grad_g1, grad_s1 = back1(gn1)
    grad_tokens = gm_own + gtn

    reduce_out = scatter(g_reduce.astype(BF16), column).astype(F32)
    expand_out = (
        exchange(scatter(g_expand.astype(BF16), column))
        .reshape(t, br, b, hs).transpose(1, 2, 0, 3).reshape(br, hid).astype(F32)
    )
    joint_out = (
        exchange(scatter(g_joint.astype(BF16), column))
        .reshape(t, br, 3, fl).transpose(1, 2, 0, 3).reshape(br, 3 * width).astype(F32)
    )
    out_out = lax.ppermute(scatter(g_out.astype(BF16), column), "dp", swap).astype(F32)

    def place(x):
        return lax.dynamic_update_slice_in_dim(jnp.zeros((width,), F32), x, mine * fl, 0)

    full_eb = lax.dynamic_update_slice_in_dim(
        jnp.zeros((b, t, hs), F32), grad_eb.reshape(b, 1, hs), mine, 1
    )
    grads = [grad_g1, grad_s1, place(grad_qb), place(grad_vb), grad_ob, grad_g2, grad_s2, full_eb, grad_rb]
    sums = lax.psum_scatter(
        jnp.concatenate([g.reshape(n, -1) for g in grads], axis=1),
        "dp", scatter_dimension=0, tiled=True,
    )[0]
    pieces, at = [], 0
    for s in sizes:
        pieces.append(sums[at : at + s])
        at += s
    return (
        layer_output, grad_tokens, pieces[0], pieces[1], joint_out, pieces[2], pieces[3],
        out_out, pieces[4], pieces[5], pieces[6], expand_out, pieces[7], reduce_out, pieces[8],
    )


def cut(ref, index, size):
    return ref.at[pl.ds(pl.multiple_of(index * size, size), size)]


def take(ref, index, size):
    return ref[pl.ds(pl.multiple_of(index * size, size), size), :]


def put(ref, index, size, value):
    ref[pl.ds(pl.multiple_of(index * size, size), size), :] = value


def loop(low, high, step):
    def body(i, carry):
        step(i)
        return carry

    lax.fori_loop(low, high, body, 0)


def norm_stats(x):
    average = jnp.mean(x, axis=-1, keepdims=True)
    centred = x - average
    spread = jnp.mean(centred * centred, axis=-1, keepdims=True)
    rstd = lax.rsqrt(spread + EPSILON)
    return centred * rstd, rstd


def norm_back(xhat, rstd, grad_out, gain):
    scaled = grad_out * gain
    first = jnp.mean(scaled, axis=-1, keepdims=True)
    second = jnp.mean(scaled * xhat, axis=-1, keepdims=True)
    grad_gain = jnp.sum(grad_out * xhat, axis=0, keepdims=True)
    grad_shift = jnp.sum(grad_out, axis=0, keepdims=True)
    return rstd * (scaled - first - xhat * second), grad_gain, grad_shift


SMALL_P, SMALL_Z = 0, 8
A2A_J, A2A_E = 12, 20
Z_J, Z_E, Z_R, Z_O, SIB_O = 28, 32, 36, 40, 44
AG_N1, AG_GF, AG_N2, AG_GM = 48, 56, 64, 72
RS_0 = 80
G_E, G_R, G_J, G_O, G_SIB = 112, 116, 120, 124, 128
BACK_E, BACK_J = 132, 140
VEC_P, VEC_Z = 148, 156
SEMS = 160


def kernel(
    seqs,
    tok, cot, joint_in, out_in, expand_in, reduce_in, lens,
    v_g1, v_s1, v_qb, v_vb, v_ob, v_g2, v_s2, v_rb, v_eb,
    layer_out, gtok_out, gjoint_out, gout_out, gexp_out, gred_out, vec_out,
    line, small, small32, jstage, estage, joint_w, exp_w, red_w, wo_half, wo_sib, wout,
    n1, n2, gf, gm, qkv, probs, ctx, act, gbl, gpk,
    slope, csend, crecv, hsend, hrecv, part, middle, gmid,
    ge_send, ge_recv, ge_own, gr_send, gr_recv, gr_own,
    gj_send, gj_recv, gj_own, go_full, go_sib, go_send, go_recv,
    ge_low, gj_low, ge_back, gj_back, vs, vz_recv, vp_own, vp, bias_acc, ebias_acc,
    ssem, rsem,
):
    T = TENSOR
    rows, width = tok.shape
    br = joint_in.shape[0]
    me = lax.axis_index("dp")
    n = lax.axis_size("dp")
    b = n // T
    z = me // T
    p = me % T
    c = p // 2
    k = p % 2
    sib = z * T + 2 * c + (1 - k)
    hs = reduce_in.shape[0]
    fl = width // T
    hd = width // HEADS
    hl = HEADS // T
    kb = br * T

    def chip(dc):
        return ((c // 2 + dc // 2) % 2) * 2 + (c % 2 + dc % 2) % 2

    def dev(c2, k2):
        return z * T + 2 * c2 + k2

    def up(d):
        return ((z + d) % b) * T + p

    def down(d):
        return (z - d + b) % b

    def rc(src, dst, base, i, device):
        return pltpu.make_async_remote_copy(
            src_ref=src, dst_ref=dst, send_sem=ssem.at[base + i], recv_sem=rsem.at[base + i],
            device_id=(device,), device_id_type=pl.DeviceIdType.MESH,
        )

    def start(src, dst, base, i, device):
        rc(src, dst, base, i, device).start()

    def arrive(dst, base, i):
        rc(dst, dst, base, i, sib).wait_recv()

    def sent(src, base, low, high):
        loop(low, high, lambda i: rc(src, src, base, i, sib).wait_send())

    barrier = pltpu.get_barrier_semaphore()
    loop(1, T, lambda d: pl.semaphore_signal(
        barrier, inc=1, device_id=(z * T + (p + d) % T,), device_id_type=pl.DeviceIdType.MESH))
    loop(1, b, lambda d: pl.semaphore_signal(
        barrier, inc=1, device_id=(up(d),), device_id_type=pl.DeviceIdType.MESH))
    pl.semaphore_wait(barrier, T - 1 + b - 1)

    lane = lax.broadcasted_iota(jnp.int32, (1, 128), 1)
    plain = (me % (128 // br)) * br
    headed = ((z % hl) * 2 + k) * br
    line[...] = jnp.zeros_like(line)
    for r, v in enumerate((v_g1, v_s1, v_qb, v_vb, v_ob, v_g2, v_s2, v_rb)):
        at = headed if r in (2, 3) else plain
        tiled = jnp.concatenate([v[...].astype(F32).reshape(1, br)] * (128 // br), axis=1)
        line[r : r + 1, :] = jnp.where((lane >= at) & (lane < at + br), tiled, 0.0)
    line[8:9, :] = v_eb[...].astype(F32).reshape(1, hs)
    running = jnp.zeros((1, 1), F32)
    marks = jnp.zeros((1, 128), F32)
    for j in range(seqs):
        running = running + lens[:, j : j + 1].astype(F32)
        marks = jnp.where(lane == j, running, marks)
    line[9:10, :] = marks
    small[p, z] = line[...].astype(BF16)
    loop(1, b, lambda d: start(small.at[p, z], small.at[p, z], SMALL_Z, d, up(d)))

    for q in range(T):
        c2, k2 = q // 2, q % 2
        pieces = [
            joint_in[:, w * width + (c2 + 4 * (hl * k2 + j)) * hd : w * width + (c2 + 4 * (hl * k2 + j) + 1) * hd]
            for w in range(3) for j in range(hl)
        ]
        jstage[q * br : (q + 1) * br, :] = jnp.concatenate(pieces, axis=1)
    put(joint_w, z * T + p, br, take(jstage, p, br))

    def send_joint(d):
        q = (p + d) % T
        start(cut(jstage, q, br), cut(joint_w, z * T + p, br), A2A_J, d, z * T + q)

    loop(1, T, send_joint)
    loop(1, b, lambda d: arrive(small.at[p, down(d)], SMALL_Z, d))
    loop(1, T, lambda d: start(small.at[p], small.at[p], SMALL_P, d, z * T + (p + d) % T))
    for q in range(T):
        pieces = [expand_in[:, (e * T + q) * hs : (e * T + q + 1) * hs] for e in range(b)]
        estage[q * br : (q + 1) * br, :] = jnp.concatenate(pieces, axis=1)
    put(exp_w, z * T + p, br, take(estage, p, br))

    def send_expand(d):
        q = (p + d) % T
        start(cut(estage, q, br), cut(exp_w, z * T + p, br), A2A_E, d, z * T + q)

    loop(1, T, send_expand)
    put(red_w, z, hs, reduce_in[...])
    put(wo_half, z, br, out_in[...])

    loop(1, T, lambda d: arrive(cut(joint_w, z * T + (p - d + T) % T, br), A2A_J, d))
    loop(1, b, lambda d: start(cut(joint_w, z, kb), cut(joint_w, z, kb), Z_J, d, up(d)))
    loop(1, b, lambda d: start(cut(wo_half, z, br), cut(wo_half, z, br), Z_O, d, up(d)))
    xhat1, rstd1 = norm_stats(tok[...].astype(F32))
    loop(1, T, lambda d: arrive(small.at[(p - d + T) % T], SMALL_P, d))
    small32[...] = small[...].astype(F32)
    fold = 128 // br
    halves = [
        sum(small32[h * fold + i] for i in range(1, fold)) + small32[h * fold]
        for h in range(T // fold)
    ]

    def vector(r):
        return jnp.concatenate(
            [half[e, r : r + 1, :] for e in range(b) for half in halves], axis=1
        )

    def place(ref, value):
        put(ref, p, rows, value)

    def gather_start(ref, base):
        mine = cut(ref, p, rows)
        loop(1, 4, lambda dc: start(mine, mine, base, dc, dev(chip(dc), k)))
        start(mine, mine, base + 4, 0, sib)

    def gather_wait(ref, base, dc):
        c2 = chip(dc)

        @pl.when(dc > 0)
        def _():
            block = cut(ref, 2 * c2 + k, rows)
            arrive(block, base, dc)
            start(block, block, base + 4, dc, sib)

        arrive(cut(ref, 2 * c2 + 1 - k, rows), base + 4, dc)

    def gather_finish(ref, base):
        def forward(dc):
            block = cut(ref, 2 * chip(dc) + k, rows)
            arrive(block, base, dc)
            start(block, block, base + 4, dc, sib)

        loop(1, 4, forward)
        loop(0, 4, lambda dc: arrive(cut(ref, 2 * chip(dc) + 1 - k, rows), base + 4, dc))

    place(n1, (xhat1 * vector(0) + vector(1)).astype(BF16))
    gather_start(n1, AG_N1)

    loop(1, T, lambda d: arrive(cut(exp_w, z * T + (p - d + T) % T, br), A2A_E, d))
    loop(1, b, lambda d: start(cut(exp_w, z, kb), cut(exp_w, z, kb), Z_E, d, up(d)))
    loop(1, b, lambda d: start(reduce_in, cut(red_w, z, hs), Z_R, d, up(d)))

    ends = line[9:10, :]
    column_pos = lax.broadcasted_iota(jnp.int32, (rows, 1), 0).astype(F32)
    row_pos = lax.broadcasted_iota(jnp.int32, (1, rows), 1).astype(F32)
    live = (column_pos < ends[:, seqs - 1 : seqs]).astype(F32)
    grad_final = cot[...].astype(F32) * live
    place(gf, grad_final.astype(BF16))

    def feature_bias(r):
        total = jnp.zeros((1, 128), F32)
        for j in range(hl):
            for k2 in range(2):
                total += small32[2 * c + k2, hl * k + j, r : r + 1, :]
        return total

    qb, vb = feature_bias(2), feature_bias(3)
    eb = jnp.concatenate([small32[p, e, 8:9, :] for e in range(b)], axis=1)

    gather_finish(n1, AG_N1)
    gather_start(gf, AG_GF)
    loop(1, b, lambda d: arrive(cut(wo_half, down(d), br), Z_O, d))
    give = cut(wo_half, 1 - k, hl * br)
    start(give, wo_sib, SIB_O, 0, sib)
    loop(1, b, lambda d: arrive(cut(joint_w, down(d), kb), Z_J, d))
    arrive(wo_sib, SIB_O, 0)
    kept = take(wo_half, k, hl * br)
    other = wo_sib[...]
    low = jnp.where(k == 0, kept, other)
    high = jnp.where(k == 0, other, kept)
    for j in range(hl):
        wout[2 * j * br : (2 * j + 1) * br, :] = low[j * br : (j + 1) * br]
        wout[(2 * j + 1) * br : (2 * j + 2) * br, :] = high[j * br : (j + 1) * br]

    scale = hd ** (-0.5)

    def send_hop(r, dc):
        start(cut(hsend.at[r], dc, rows), cut(hrecv.at[r], dc, rows), RS_0 + 8 * r + 4, dc, dev(chip(dc), k))

    def reduce_loop(slots, compute, ready=None, held=()):
        def step(i):
            @pl.when(i < 4)
            def _():
                c2 = chip(i)
                if ready is not None:
                    ready(i)
                for r, value in zip(slots, compute(c2)):
                    first, second = value[:rows], value[rows:]
                    put(csend.at[r], c2, rows, jnp.where(k == 0, second, first).astype(BF16))
                    start(cut(csend.at[r], c2, rows), cut(crecv.at[r], c2, rows), RS_0 + 8 * r, c2, sib)
                    put(part.at[r], i, rows, jnp.where(k == 0, first, second))

            @pl.when(i > 0)
            def _():
                dc = i - 1
                c2 = chip(dc)
                for r in slots:
                    arrive(cut(crecv.at[r], c2, rows), RS_0 + 8 * r, c2)
                    total = take(part.at[r], dc, rows) + take(crecv.at[r], c2, rows).astype(F32)

                    @pl.when(dc == 0)
                    def _():
                        put(part.at[r], 0, rows, total)

                    @pl.when(dc > 0)
                    def _():
                        put(hsend.at[r], dc, rows, total.astype(BF16))
                        if r not in held:
                            send_hop(r, dc)

        loop(0, 5, step)

    def reduce_finish(r):
        total = part[r, 0:rows, :]
        for dc in range(1, 4):
            arrive(cut(hrecv.at[r], dc, rows), RS_0 + 8 * r + 4, dc)
            total += hrecv[r, dc * rows : (dc + 1) * rows, :].astype(F32)
        return total

    pair = 2 * rows

    def attend(c2):
        packed = dot(take(n1, c2, pair), joint_w[...])
        q = (packed[:, :fl] + qb).astype(BF16)
        kk = packed[:, fl : 2 * fl].astype(BF16)
        v = (packed[:, 2 * fl :] + vb).astype(BF16)
        put(qkv, c2, pair, jnp.concatenate([q, kk, v], axis=1))
        blocks = []
        for half in range(2):
            at_row = slice(half * rows, (half + 1) * rows)
            bounds = small32[2 * c2 + half, z, 9:10, :]
            seg_q = jnp.zeros((rows, 1), F32)
            seg_k = jnp.zeros((1, rows), F32)
            for j in range(seqs):
                end = bounds[:, j : j + 1]
                seg_q += (column_pos >= end).astype(F32)
                seg_k += (row_pos >= end).astype(F32)
            last = bounds[:, seqs - 1 : seqs]
            seg_q = jnp.where(column_pos < last, seg_q, rows + column_pos)
            seg_k = jnp.where(row_pos < last, seg_k, rows + row_pos)
            allowed = (seg_q == seg_k) & (column_pos >= row_pos)
            outs = []
            for j in range(hl):
                at = slice(j * hd, (j + 1) * hd)
                scores = transposed_right(q[at_row, at], kk[at_row, at]) * scale
                scores = jnp.where(allowed, scores, -1e30)
                top = jnp.max(scores, axis=-1, keepdims=True)
                logsum = top + jnp.log(jnp.sum(jnp.exp(scores - top), axis=-1, keepdims=True))
                prob = jnp.exp(scores - logsum)
                put(probs, (2 * c2 + half) * hl + j, rows, prob)
                outs.append(dot(prob.astype(BF16), v[at_row, at]))
            blocks.append(jnp.concatenate(outs, axis=1))
        context = jnp.concatenate(blocks, axis=0).astype(BF16)
        put(ctx, c2, pair, context)
        return [dot(context, wout[...])]

    reduce_loop([0], attend)
    gather_finish(gf, AG_GF)
    mid = tok[...].astype(F32) + reduce_finish(0) + vector(4)
    middle[...] = mid
    xhat2, rstd2 = norm_stats(mid)
    place(n2, (xhat2 * vector(5) + vector(6)).astype(BF16))
    gather_start(n2, AG_N2)
    loop(1, b, lambda d: arrive(cut(exp_w, down(d), kb), Z_E, d))

    def feed(dc):
        c2 = chip(dc)
        gather_wait(n2, AG_N2, dc)
        before = dot(take(n2, c2, pair), exp_w[...]) + eb
        square = before * before
        curve = jnp.tanh(TANH_SCALE * (before + CUBIC_TERM * before * square))
        put(act, c2, pair, (0.5 * before * (1.0 + curve)).astype(BF16))
        put(slope, c2, pair, 0.5 * (1.0 + curve) + 0.5 * before * (1.0 - curve * curve) * TANH_SCALE * (
            1.0 + 3.0 * CUBIC_TERM * square
        ))

    def weight_grad(left, cols, right, send, recv, mine, base):
        def step(i):
            d = i % b
            to = (z + d) % b
            part = transposed_left(
                left[:, pl.ds(pl.multiple_of(to * cols, cols), cols)], right[...]
            )

            @pl.when(i < b)
            def _():
                put(send, d, cols, part.astype(BF16))
                start(cut(send, d, cols), cut(recv, d, cols), base, d, up(d))

            @pl.when(i == b)
            def _():
                mine[...] = part

        loop(1, b + 1, step)

    loop(0, 4, feed)
    weight_grad(act, hs, gf, gr_send, gr_recv, gr_own, G_R)
    loop(1, b, lambda d: arrive(cut(red_w, down(d), hs), Z_R, d))
    ebias_acc[...] = jnp.zeros_like(ebias_acc)

    def feed_back(c2):
        grad_active = transposed_right(take(gf, c2, pair), red_w[...])
        grad_before = grad_active * take(slope, c2, pair)
        ebias_acc[...] += jnp.sum(grad_before, axis=0, keepdims=True)
        low_grad = grad_before.astype(BF16)
        put(gbl, c2, pair, low_grad)
        return [transposed_right(low_grad, exp_w[...]), dot(take(act, c2, pair), red_w[...])]

    reduce_loop([2, 1], feed_back, held=(1,))
    weight_grad(n2, kb, gbl, ge_send, ge_recv, ge_own, G_E)

    grad_n2 = reduce_finish(2)
    mid = middle[...]
    xhat2, rstd2 = norm_stats(mid)
    row_grad, grad_g2, grad_s2 = norm_back(xhat2, rstd2, grad_n2, vector(5))
    grad_final = cot[...].astype(F32) * live
    grad_mid = grad_final + row_grad
    gmid[...] = grad_mid
    place(gm, grad_mid.astype(BF16))
    gather_start(gm, AG_GM)
    seg = width // b

    def vec_put(row, value):
        for e in range(b):
            vs[e, row : row + 1, :] = value[:, e * seg : (e + 1) * seg]

    vs[...] = jnp.zeros_like(vs)
    vec_put(2, jnp.sum(grad_mid, axis=0, keepdims=True))
    vec_put(3, grad_g2)
    vec_put(4, grad_s2)
    vec_put(5, jnp.sum(grad_final, axis=0, keepdims=True))
    bias_acc[...] = jnp.zeros_like(bias_acc)

    def attend_back(c2):
        grad_ctx = transposed_right(take(gm, c2, pair), wout[...]).astype(BF16)
        held = take(qkv, c2, pair)
        blocks = []
        for half in range(2):
            at_row = slice(half * rows, (half + 1) * rows)
            gqs, gks, gvs = [], [], []
            for j in range(hl):
                at = slice(j * hd, (j + 1) * hd)
                q = held[at_row, j * hd : (j + 1) * hd]
                kk = held[at_row, fl + j * hd : fl + (j + 1) * hd]
                v = held[at_row, 2 * fl + j * hd : 2 * fl + (j + 1) * hd]
                prob = take(probs, (2 * c2 + half) * hl + j, rows)
                grad_prob = transposed_right(grad_ctx[at_row, at], v)
                gvs.append(transposed_left(prob.astype(BF16), grad_ctx[at_row, at]))
                centre = jnp.sum(prob * grad_prob, axis=-1, keepdims=True)
                grad_score = (prob * (grad_prob - centre) * scale).astype(BF16)
                gqs.append(dot(grad_score, kk))
                gks.append(transposed_left(grad_score, q))
            blocks.append(jnp.concatenate(gqs + gks + gvs, axis=1))
        packed = jnp.concatenate(blocks, axis=0)
        bias_acc[...] += jnp.sum(packed, axis=0, keepdims=True)
        low_grad = packed.astype(BF16)
        put(gpk, c2, pair, low_grad)
        return [transposed_right(low_grad, joint_w[...])]

    reduce_loop([3], attend_back, ready=lambda dc: gather_wait(gm, AG_GM, dc))
    loop(1, 4, lambda dc: send_hop(1, dc))
    weight_grad(n1, kb, gpk, gj_send, gj_recv, gj_own, G_J)
    grad_out = transposed_left(ctx[...], gm[...])
    evens = jnp.concatenate([grad_out[2 * j * br : (2 * j + 1) * br] for j in range(hl)], axis=0)
    odds = jnp.concatenate([grad_out[(2 * j + 1) * br : (2 * j + 2) * br] for j in range(hl)], axis=0)
    keep = jnp.where(k == 0, evens, odds)
    pass_on = jnp.where(k == 0, odds, evens)
    put(go_full, k, hl * br, keep.astype(BF16))
    go_sib[...] = pass_on.astype(BF16)
    start(go_sib, cut(go_full, k, hl * br), G_SIB, 0, sib)

    def collect(recv, mine, size, base):
        total = mine
        for d in range(1, b):
            arrive(cut(recv, d, size), base, d)
            total += recv[d * size : (d + 1) * size, :].astype(F32)
        return total

    def back(total, mine, landing, base):
        mine[...] = total.astype(BF16)
        put(landing, p, br, take(mine, p, br))

        def step(d):
            q = (p + d) % T
            start(cut(mine, q, br), cut(landing, p, br), base, d, z * T + q)

        loop(1, T, step)

    gred_out[...] = collect(gr_recv, gr_own[...], hs, G_R)

    back(collect(ge_recv, ge_own[...], kb, G_E), ge_low, ge_back, BACK_E)
    arrive(cut(go_full, 1 - k, hl * br), G_SIB, 0)

    def send_out(d):
        to = (z + d) % b
        start(cut(go_full, to, br), cut(go_recv, d, br), G_O, d, up(d))

    loop(1, b, send_out)
    grad_n1 = reduce_finish(3)
    xhat1, rstd1 = norm_stats(tok[...].astype(F32))
    row_grad, grad_g1, grad_s1 = norm_back(xhat1, rstd1, grad_n1, vector(0))
    gtok_out[...] = gmid[...] + row_grad
    vec_put(0, grad_g1)
    vec_put(1, grad_s1)
    for e in range(b):
        j = e % hl
        kept_row = jnp.concatenate(
            [bias_acc[:, j * hd : (j + 1) * hd], bias_acc[:, 2 * fl + j * hd : 2 * fl + (j + 1) * hd]], axis=1
        )
        vs[e, 6:7, :hs] = ebias_acc[:, e * hs : (e + 1) * hs]
        vs[e, 6:7, hs:] = jnp.where(k == e // hl, kept_row, 0.0)
    loop(1, b, lambda d: start(vs.at[(z + d) % b], vz_recv.at[d], VEC_Z, d, up(d)))

    layer_out[...] = (middle[...] + reduce_finish(1) + vector(7)).astype(BF16)

    total = vs[z]
    for d in range(1, b):
        arrive(vz_recv.at[d], VEC_Z, d)
        total += vz_recv[d]
    vp_own[...] = total
    vp[p] = total
    loop(1, T, lambda d: start(vp_own, vp.at[p], VEC_P, d, z * T + (p + d) % T))

    loop(1, T, lambda d: arrive(cut(ge_back, (p - d + T) % T, br), BACK_E, d))
    for q in range(T):
        for e in range(b):
            gexp_out[:, (e * T + q) * hs : (e * T + q + 1) * hs] = ge_back[
                q * br : (q + 1) * br, e * hs : (e + 1) * hs
            ].astype(F32)
    back(collect(gj_recv, gj_own[...], kb, G_J), gj_low, gj_back, BACK_J)
    gout_out[...] = collect(go_recv, take(go_full, z, br).astype(F32), br, G_O)
    loop(1, T, lambda d: arrive(vp.at[(p - d + T) % T], VEC_P, d))
    total = jnp.sum(vp[...], axis=0)
    picked = jnp.zeros((8, br), F32)
    for q in range(T):
        picked = jnp.where(p == q, total[:, q * br : (q + 1) * br], picked)
    vec_out[0:8, 0:br] = picked
    vec_out[6:7, :] = vp[p, 6:7, :hs]
    keeper = 2 * c + z // hl
    row = vp[keeper, 6:7, :]
    for i in range(2):
        at = hs + i * hl * br
        vec_out[8 + i : 9 + i, 0:br] = jnp.where(k == 0, row[:, at : at + br], row[:, at + br : at + 2 * br])
    loop(1, T, lambda d: arrive(cut(gj_back, (p - d + T) % T, br), BACK_J, d))
    for w in range(3):
        for j in range(hl):
            at = slice((w * hl + j) * hd, (w * hl + j + 1) * hd)
            for k2 in range(2):
                for half in range(2):
                    q0, q1 = 4 * half + k2, 4 * half + 2 + k2
                    head = 2 * half + 4 * (hl * k2 + j)
                    gjoint_out[:, w * width + head * hd : w * width + (head + 2) * hd] = (
                        jnp.concatenate(
                            [gj_back[q0 * br : (q0 + 1) * br, at], gj_back[q1 * br : (q1 + 1) * br, at]],
                            axis=1,
                        ).astype(F32)
                    )

    sent(small.at[p, z], SMALL_Z, 1, b)
    sent(small.at[p], SMALL_P, 1, T)
    sent(cut(jstage, 0, br), A2A_J, 1, T)
    sent(cut(estage, 0, br), A2A_E, 1, T)
    sent(cut(joint_w, 0, kb), Z_J, 1, b)
    sent(cut(exp_w, 0, kb), Z_E, 1, b)
    sent(reduce_in, Z_R, 1, b)
    sent(cut(wo_half, 0, br), Z_O, 1, b)
    sent(wo_sib, SIB_O, 0, 1)
    for base in (AG_N1, AG_GF, AG_N2, AG_GM):
        sent(cut(n1, 0, rows), base, 1, 8)
    for r in range(4):
        sent(cut(csend.at[0], 0, rows), RS_0 + 8 * r, 0, 4)
        sent(cut(csend.at[0], 0, rows), RS_0 + 8 * r, 5, 8)
    sent(cut(ge_send, 0, kb), G_E, 1, b)
    sent(cut(gr_send, 0, hs), G_R, 1, b)
    sent(cut(gj_send, 0, kb), G_J, 1, b)
    sent(go_sib, G_SIB, 0, 1)
    sent(cut(go_recv, 0, br), G_O, 1, b)
    sent(cut(ge_low, 0, br), BACK_E, 1, T)
    sent(cut(gj_low, 0, br), BACK_J, 1, T)
    sent(vs.at[0], VEC_Z, 1, b)
    sent(vp_own, VEC_P, 1, T)


def finish(count, vec, *refs):
    large_in, large_out, small_out = refs[:count], refs[count : 2 * count], refs[2 * count : -count - 2]
    held, sem_in, sem_out = refs[-count - 2 : -2], refs[-2], refs[-1]
    inward = [pltpu.make_async_copy(x, h, sem_in.at[i]) for i, (x, h) in enumerate(zip(large_in, held))]
    outward = [pltpu.make_async_copy(h, x, sem_out.at[i]) for i, (h, x) in enumerate(zip(held, large_out))]
    for copy in inward:
        copy.start()
    for r, out in zip((0, 1, 8, 9, 2, 3, 4, 5, 6), small_out):
        size = out.shape[0]
        out[...] = vec[r : r + 1, :size].reshape(size)
    for first, second in zip(inward, outward):
        first.wait()
        second.start()
    for copy in outward:
        copy.wait()


def fused(
    tokens, lengths, cotangent, norm1_gain, norm1_shift, joint_weight, query_bias, value_bias,
    output_weight, output_bias, norm2_gain, norm2_shift, expand_weight, expand_bias,
    reduce_weight, reduce_bias,
):
    n = lax.axis_size("dp")
    T = TENSOR
    b = n // T
    rows, width = tokens.shape
    br = joint_weight.shape[0]
    hs = reduce_weight.shape[0]
    fl = width // T
    hl = HEADS // T
    seqs = lengths.shape[1]
    kb, f, fj, tt = br * T, b * hs, 3 * fl, T * rows
    vm = pltpu.VMEM
    scratch = [
        vm((16, 128), F32), vm((T, b, 16, 128), BF16), vm((T, b, 16, 128), F32), vm((kb, fj), BF16), vm((kb, f), BF16), vm((width, fj), BF16),
        vm((width, f), BF16), vm((f, width), BF16), vm((b * br, width), BF16),
        vm((hl * br, width), BF16), vm((fl, width), BF16),
        vm((tt, width), BF16), vm((tt, width), BF16), vm((tt, width), BF16), vm((tt, width), BF16),
        vm((tt, fj), BF16), vm((tt * hl, rows), F32), vm((tt, fl), BF16),
        vm((tt, f), BF16), vm((tt, f), BF16), vm((tt, fj), BF16), vm((tt, f), F32),
        vm((4, 4 * rows, width), BF16), vm((4, 4 * rows, width), BF16),
        vm((4, 4 * rows, width), BF16), vm((4, 4 * rows, width), BF16),
        vm((4, 4 * rows, width), F32), vm((rows, width), F32), vm((rows, width), F32),
        vm((b * kb, f), BF16), vm((b * kb, f), BF16), vm((kb, f), F32),
        vm((b * hs, width), BF16), vm((b * hs, width), BF16), vm((hs, width), F32),
        vm((b * kb, fj), BF16), vm((b * kb, fj), BF16), vm((kb, fj), F32),
        vm((b * br, width), BF16), vm((hl * br, width), BF16), vm((hl * br, width), BF16), vm((b * br, width), BF16),
        vm((kb, f), BF16), vm((kb, fj), BF16), vm((kb, f), BF16), vm((kb, fj), BF16),
        vm((b, 8, width // b), F32), vm((b, 8, width // b), F32), vm((8, width // b), F32), vm((T, 8, width // b), F32),
        vm((1, fj), F32), vm((1, f), F32),
        pltpu.SemaphoreType.DMA((SEMS,)), pltpu.SemaphoreType.DMA((SEMS,)),
    ]
    sds = jax.ShapeDtypeStruct
    *large, vec = pl.pallas_call(
        functools.partial(kernel, seqs),
        out_shape=(
            sds((rows, width), BF16), sds((rows, width), F32), sds((br, 3 * width), F32),
            sds((br, width), F32), sds((br, expand_weight.shape[1]), F32), sds((hs, width), F32),
            sds((16, hs), F32),
        ),
        in_specs=[pl.BlockSpec(memory_space=pltpu.VMEM)] * 16,
        out_specs=tuple([pl.BlockSpec(memory_space=pltpu.VMEM)] * 7),
        scratch_shapes=scratch,
        compiler_params=pltpu.CompilerParams(
            collective_id=0, has_side_effects=True, vmem_limit_bytes=62 * 1024 * 1024
        ),
        name="layer",
    )(
        tokens, cotangent, joint_weight, output_weight, expand_weight, reduce_weight, lengths,
        norm1_gain, norm1_shift, query_bias, value_bias, output_bias, norm2_gain, norm2_shift,
        reduce_bias, expand_bias,
    )

    anywhere, inside = pl.BlockSpec(memory_space=pl.ANY), pl.BlockSpec(memory_space=pltpu.VMEM)
    done = pl.pallas_call(
        functools.partial(finish, len(large)),
        out_shape=tuple(sds(x.shape, x.dtype) for x in large)
        + tuple(sds((br,), F32) for _ in range(8)) + (sds((hs,), F32),),
        in_specs=[inside] + [anywhere] * len(large),
        out_specs=tuple([anywhere] * len(large) + [inside] * 9),
        scratch_shapes=[pltpu.VMEM(x.shape, x.dtype) for x in large]
        + [pltpu.SemaphoreType.DMA((len(large),))] * 2,
        name="finish",
    )(vec, *large)
    layer_output, grad_tokens, g_joint, g_out, g_exp, g_red = done[:6]
    g_g1, g_s1, g_qb, g_vb, g_ob, g_g2, g_s2, g_rb, g_eb = done[6:]
    return (
        layer_output, grad_tokens, g_g1, g_s1, g_joint, g_qb, g_vb, g_out,
        g_ob, g_g2, g_s2, g_exp, g_eb, g_red, g_rb,
    )


def fits(n, width):
    br = width // n
    return n % TENSOR == 0 and br % 16 == 0 and 2 * br * HEADS == width and n // TENSOR == 2 * (HEADS // TENSOR)


def whole(*args):
    n = lax.axis_size("dp")
    return fused(*args) if fits(n, args[0].shape[1]) else on_device(*args)


def solution(mesh):
    m, v = P("dp", None), P("dp")
    in_specs = (m, m, m, v, v, m, v, v, m, v, v, v, m, v, m, v)
    out_specs = (m, m, v, v, m, v, v, m, v, v, v, m, v, m, v)
    return jax.shard_map(
        whole, mesh=mesh, in_specs=in_specs, out_specs=out_specs, check_vma=False
    )
```

```python
import functools

import jax
import jax.numpy as jnp
from jax import lax
from jax.experimental import pallas as pl
from jax.experimental.pallas import tpu as pltpu
from jax.sharding import PartitionSpec as P

HEADS = 16
TENSOR = 8

EPSILON = 1e-05
TANH_SCALE = 0.7978845608028654
CUBIC_TERM = 0.044715

F32 = jnp.float32
BF16 = jnp.bfloat16


def layer_norm(row_data, gain_vector, shift_vector):
    average = jnp.mean(row_data, axis=-1, keepdims=True)
    centred = row_data - average
    spread = jnp.mean(centred * centred, axis=-1, keepdims=True)
    return centred * lax.rsqrt(spread + EPSILON) * gain_vector + shift_vector


def activation(values_in):
    return (
        0.5
        * values_in
        * (
            1.0
            + jnp.tanh(TANH_SCALE * (values_in + CUBIC_TERM * values_in * values_in * values_in))
        )
    )


def contract(pattern, first_op, second_op):
    return jnp.einsum(pattern, first_op, second_op, preferred_element_type=F32)


def dot(first_op, second_op):
    return jnp.dot(first_op, second_op, preferred_element_type=F32)


def transposed_left(first_op, second_op):
    return lax.dot_general(
        first_op, second_op, (((0,), (0,)), ((), ())), preferred_element_type=F32
    )


def transposed_right(first_op, second_op):
    return lax.dot_general(
        first_op, second_op, (((1,), (1,)), ((), ())), preferred_element_type=F32
    )


def slot_mask(lengths_row, row_count):
    position = jnp.arange(row_count, dtype=jnp.int32)
    segment = jnp.zeros((row_count,), jnp.int32)
    end = jnp.int32(0)
    for j in range(lengths_row.shape[0]):
        end = end + lengths_row[j]
        segment = segment + (position >= end).astype(jnp.int32)
    live_rows = position < end
    segment = jnp.where(live_rows, segment, row_count + position)
    allowed = (segment[:, None] == segment[None, :]) & (position[:, None] >= position[None, :])
    return (allowed, live_rows.astype(F32))


def on_device(
    tokens,
    lengths,
    cotangent,
    norm1_gain,
    norm1_shift,
    joint_weight,
    query_bias,
    value_bias,
    output_weight,
    output_bias,
    norm2_gain,
    norm2_shift,
    expand_weight,
    expand_bias,
    reduce_weight,
    reduce_bias,
):
    n = lax.axis_size("dp")
    t = TENSOR if n % TENSOR == 0 else 1
    b = n // t
    rows, width = tokens.shape
    hid = expand_weight.shape[1]
    br = joint_weight.shape[0]
    hs = reduce_weight.shape[0]
    head_size = width // HEADS
    hl = HEADS // t
    fl = width // t
    me = lax.axis_index("dp")
    mine = me % t
    plane = [[z * t + p for p in range(t)] for z in range(b)]
    column = [[z * t + p for z in range(b)] for p in range(t)]
    swap = [(z * t + p, p * b + z) for z in range(b) for p in range(t)]

    def gather(x, groups):
        return lax.all_gather(x, "dp", axis=0, tiled=True, axis_index_groups=groups)

    def scatter(x, groups):
        return lax.psum_scatter(
            x, "dp", scatter_dimension=0, tiled=True, axis_index_groups=groups
        )

    def exchange(x):
        return lax.all_to_all(
            x, "dp", split_axis=0, concat_axis=0, tiled=True, axis_index_groups=plane
        )

    vecs = [
        norm1_gain, norm1_shift, query_bias, value_bias, output_bias,
        norm2_gain, norm2_shift, expand_bias, reduce_bias,
    ]
    sizes = [v.shape[0] for v in vecs]
    small = lax.all_gather(jnp.concatenate(vecs)[None, :], "dp", axis=0, tiled=True)
    whole, at = [], 0
    for s in sizes:
        whole.append(small[:, at : at + s].reshape(-1).astype(F32))
        at += s
    gain1, shift1, qb, vb, ob, gain2, shift2, eb, rb = whole
    eb = lax.dynamic_slice_in_dim(eb.reshape(b, t, hs), mine, 1, 1).reshape(-1)
    qb = lax.dynamic_slice_in_dim(qb, mine * fl, fl, 0)
    vb = lax.dynamic_slice_in_dim(vb, mine * fl, fl, 0)

    joint_cut = joint_weight.reshape(br, 3, t, fl).transpose(2, 0, 1, 3).reshape(t * br, 3 * fl)
    expand_cut = expand_weight.reshape(br, b, t, hs).transpose(2, 0, 1, 3).reshape(t * br, b * hs)
    out_mine = lax.ppermute(output_weight, "dp", [(d, s) for s, d in swap])
    wout = gather(out_mine, column)
    joint = gather(exchange(joint_cut), column)
    expand = gather(exchange(expand_cut), column)
    reduce = gather(reduce_weight, column)

    lens = gather(lengths, plane)
    allowed, _ = jax.vmap(lambda r: slot_mask(r, rows))(lens)
    _, live = slot_mask(lengths[0], rows)

    residual = tokens.astype(F32)
    n1 = gather(layer_norm(residual, gain1, shift1).astype(BF16), plane)
    grad_final = cotangent.astype(F32) * live[:, None]
    gf = gather(grad_final.astype(BF16), plane)

    packed = dot(n1, joint)
    shape4 = (t, rows, hl, head_size)
    q = (packed[:, :fl] + qb).astype(BF16).reshape(shape4)
    k = packed[:, fl : 2 * fl].astype(BF16).reshape(shape4)
    v = (packed[:, 2 * fl :] + vb).astype(BF16).reshape(shape4)
    scale = head_size ** (-0.5)
    scores = contract("gqhd,gkhd->ghqk", q, k) * scale
    scores = jnp.where(allowed[:, None], scores, -1e30)
    top = jnp.max(scores, axis=-1, keepdims=True)
    logsum = top + jnp.log(jnp.sum(jnp.exp(scores - top), axis=-1, keepdims=True))
    probs = jnp.exp(scores - logsum)
    weights = probs.astype(BF16)
    context = contract("ghqk,gkhd->gqhd", weights, v).astype(BF16).reshape(t * rows, fl)
    middle = (
        residual + scatter(dot(context, wout).astype(BF16), plane).astype(F32) + ob
    )
    n2 = gather(layer_norm(middle, gain2, shift2).astype(BF16), plane)
    before = dot(n2, expand) + eb
    active = activation(before).astype(BF16)
    final = middle + scatter(dot(active, reduce).astype(BF16), plane).astype(F32) + rb
    layer_output = final.astype(BF16)

    grad_rb = jnp.sum(grad_final, axis=0)
    g_reduce = transposed_left(active, gf)
    _, curve_back = jax.vjp(activation, before)
    gb = curve_back(transposed_right(gf, reduce))[0]
    grad_eb = jnp.sum(gb, axis=0)
    gbl = gb.astype(BF16)
    g_expand = transposed_left(n2, gbl)
    gn2 = scatter(transposed_right(gbl, expand).astype(BF16), plane).astype(F32)
    _, back2 = jax.vjp(layer_norm, middle, gain2, shift2)
    gmn, grad_g2, grad_s2 = back2(gn2)
    gm_own = grad_final + gmn
    grad_ob = jnp.sum(gm_own, axis=0)
    gm = gather(gm_own.astype(BF16), plane)
    g_out = transposed_left(context, gm)
    gctx = transposed_right(gm, wout).astype(BF16).reshape(shape4)
    gp = contract("gqhd,gkhd->ghqk", gctx, v)
    gv = contract("ghqk,gqhd->gkhd", weights, gctx).reshape(t * rows, fl)
    centre = jnp.sum(probs * gp, axis=-1, keepdims=True)
    gs = (probs * (gp - centre) * scale).astype(BF16)
    gq = contract("ghqk,gkhd->gqhd", gs, k).reshape(t * rows, fl)
    gk = contract("ghqk,gqhd->gkhd", gs, q).reshape(t * rows, fl)
    grad_qb = jnp.sum(gq, axis=0)
    grad_vb = jnp.sum(gv, axis=0)
    gpacked = jnp.concatenate([gq, gk, gv], axis=1).astype(BF16)
    g_joint = transposed_left(n1, gpacked)
    gn1 = scatter(transposed_right(gpacked, joint).astype(BF16), plane).astype(F32)
    _, back1 = jax.vjp(layer_norm, residual, gain1, shift1)
    gtn, grad_g1, grad_s1 = back1(gn1)
    grad_tokens = gm_own + gtn

    reduce_out = scatter(g_reduce.astype(BF16), column).astype(F32)
    expand_out = (
        exchange(scatter(g_expand.astype(BF16), column))
        .reshape(t, br, b, hs).transpose(1, 2, 0, 3).reshape(br, hid).astype(F32)
    )
    joint_out = (
        exchange(scatter(g_joint.astype(BF16), column))
        .reshape(t, br, 3, fl).transpose(1, 2, 0, 3).reshape(br, 3 * width).astype(F32)
    )
    out_out = lax.ppermute(scatter(g_out.astype(BF16), column), "dp", swap).astype(F32)

    def place(x):
        return lax.dynamic_update_slice_in_dim(jnp.zeros((width,), F32), x, mine * fl, 0)

    full_eb = lax.dynamic_update_slice_in_dim(
        jnp.zeros((b, t, hs), F32), grad_eb.reshape(b, 1, hs), mine, 1
    )
    grads = [grad_g1, grad_s1, place(grad_qb), place(grad_vb), grad_ob, grad_g2, grad_s2, full_eb, grad_rb]
    sums = lax.psum_scatter(
        jnp.concatenate([g.reshape(n, -1) for g in grads], axis=1),
        "dp", scatter_dimension=0, tiled=True,
    )[0]
    pieces, at = [], 0
    for s in sizes:
        pieces.append(sums[at : at + s])
        at += s
    return (
        layer_output, grad_tokens, pieces[0], pieces[1], joint_out, pieces[2], pieces[3],
        out_out, pieces[4], pieces[5], pieces[6], expand_out, pieces[7], reduce_out, pieces[8],
    )


def cut(ref, index, size):
    return ref.at[pl.ds(pl.multiple_of(index * size, size), size)]


def take(ref, index, size):
    return ref[pl.ds(pl.multiple_of(index * size, size), size), :]


def put(ref, index, size, value):
    ref[pl.ds(pl.multiple_of(index * size, size), size), :] = value


def loop(low, high, step):
    def body(i, carry):
        step(i)
        return carry

    lax.fori_loop(low, high, body, 0)


def norm_stats(x):
    average = jnp.mean(x, axis=-1, keepdims=True)
    centred = x - average
    spread = jnp.mean(centred * centred, axis=-1, keepdims=True)
    rstd = lax.rsqrt(spread + EPSILON)
    return centred * rstd, rstd


def norm_back(xhat, rstd, grad_out, gain):
    scaled = grad_out * gain
    first = jnp.mean(scaled, axis=-1, keepdims=True)
    second = jnp.mean(scaled * xhat, axis=-1, keepdims=True)
    grad_gain = jnp.sum(grad_out * xhat, axis=0, keepdims=True)
    grad_shift = jnp.sum(grad_out, axis=0, keepdims=True)
    return rstd * (scaled - first - xhat * second), grad_gain, grad_shift


SMALL_P, SMALL_Z = 0, 8
A2A_J, A2A_E = 12, 20
Z_J, Z_E, Z_R, Z_O, SIB_O = 28, 32, 36, 40, 44
AG_N1, AG_GF, AG_N2, AG_GM = 48, 56, 64, 72
RS_0 = 80
G_E, G_R, G_J, G_O, G_SIB = 112, 116, 120, 124, 128
BACK_E, BACK_J = 132, 140
VEC_P, VEC_Z = 148, 156
SEMS = 160


def kernel(
    seqs,
    tok, cot, joint_in, out_in, expand_in, reduce_in, lens,
    v_g1, v_s1, v_qb, v_vb, v_ob, v_g2, v_s2, v_rb, v_eb,
    layer_out, gtok_out, gjoint_out, gout_out, gexp_out, gred_out, vec_out,
    line, small, small32, jstage, estage, joint_w, exp_w, red_w, wo_half, wo_sib, wout,
    n1, n2, gf, gm, qkv, probs, ctx, act, gbl, gpk,
    slope, csend, crecv, hsend, hrecv, part, middle, gmid,
    ge_send, ge_recv, ge_own, gr_send, gr_recv, gr_own,
    gj_send, gj_recv, gj_own, go_full, go_sib, go_send, go_recv,
    ge_low, gj_low, ge_back, gj_back, vs, vz_recv, vp_own, vp, bias_acc, ebias_acc,
    ssem, rsem,
):
    T = TENSOR
    rows, width = tok.shape
    br = joint_in.shape[0]
    me = lax.axis_index("dp")
    n = lax.axis_size("dp")
    b = n // T
    z = me // T
    p = me % T
    c = p // 2
    k = p % 2
    sib = z * T + 2 * c + (1 - k)
    hs = reduce_in.shape[0]
    fl = width // T
    hd = width // HEADS
    hl = HEADS // T
    kb = br * T

    def chip(dc):
        return ((c // 2 + dc // 2) % 2) * 2 + (c % 2 + dc % 2) % 2

    def dev(c2, k2):
        return z * T + 2 * c2 + k2

    def up(d):
        return ((z + d) % b) * T + p

    def down(d):
        return (z - d + b) % b

    def rc(src, dst, base, i, device):
        return pltpu.make_async_remote_copy(
            src_ref=src, dst_ref=dst, send_sem=ssem.at[base + i], recv_sem=rsem.at[base + i],
            device_id=(device,), device_id_type=pl.DeviceIdType.MESH,
        )

    def start(src, dst, base, i, device):
        rc(src, dst, base, i, device).start()

    def arrive(dst, base, i):
        rc(dst, dst, base, i, sib).wait_recv()

    def sent(src, base, low, high):
        loop(low, high, lambda i: rc(src, src, base, i, sib).wait_send())

    barrier = pltpu.get_barrier_semaphore()
    loop(1, T, lambda d: pl.semaphore_signal(
        barrier, inc=1, device_id=(z * T + (p + d) % T,), device_id_type=pl.DeviceIdType.MESH))
    loop(1, b, lambda d: pl.semaphore_signal(
        barrier, inc=1, device_id=(up(d),), device_id_type=pl.DeviceIdType.MESH))
    pl.semaphore_wait(barrier, T - 1 + b - 1)

    loop(1, b, lambda d: start(out_in, cut(wo_half, z, br), Z_O, d, up(d)))
    lane = lax.broadcasted_iota(jnp.int32, (1, 128), 1)
    plain = (me % (128 // br)) * br
    headed = ((z % hl) * 2 + k) * br
    line[...] = jnp.zeros_like(line)
    for r, v in enumerate((v_g1, v_s1, v_qb, v_vb, v_ob, v_g2, v_s2, v_rb)):
        at = headed if r in (2, 3) else plain
        tiled = jnp.concatenate([v[...].astype(F32).reshape(1, br)] * (128 // br), axis=1)
        line[r : r + 1, :] = jnp.where((lane >= at) & (lane < at + br), tiled, 0.0)
    line[8:9, :] = v_eb[...].astype(F32).reshape(1, hs)
    running = jnp.zeros((1, 1), F32)
    marks = jnp.zeros((1, 128), F32)
    for j in range(seqs):
        running = running + lens[:, j : j + 1].astype(F32)
        marks = jnp.where(lane == j, running, marks)
    line[9:10, :] = marks
    small[p, z] = line[...].astype(BF16)
    loop(1, b, lambda d: start(small.at[p, z], small.at[p, z], SMALL_Z, d, up(d)))

    for q in range(T):
        c2, k2 = q // 2, q % 2
        pieces = [
            joint_in[:, w * width + (c2 + 4 * (hl * k2 + j)) * hd : w * width + (c2 + 4 * (hl * k2 + j) + 1) * hd]
            for w in range(3) for j in range(hl)
        ]
        jstage[q * br : (q + 1) * br, :] = jnp.concatenate(pieces, axis=1)
    put(joint_w, z * T + p, br, take(jstage, p, br))

    def send_joint(d):
        q = (p + d) % T
        start(cut(jstage, q, br), cut(joint_w, z * T + p, br), A2A_J, d, z * T + q)

    loop(1, T, send_joint)
    loop(1, b, lambda d: arrive(small.at[p, down(d)], SMALL_Z, d))
    loop(1, T, lambda d: start(small.at[p], small.at[p], SMALL_P, d, z * T + (p + d) % T))
    for q in range(T):
        pieces = [expand_in[:, (e * T + q) * hs : (e * T + q + 1) * hs] for e in range(b)]
        estage[q * br : (q + 1) * br, :] = jnp.concatenate(pieces, axis=1)
    put(exp_w, z * T + p, br, take(estage, p, br))

    def send_expand(d):
        q = (p + d) % T
        start(cut(estage, q, br), cut(exp_w, z * T + p, br), A2A_E, d, z * T + q)

    loop(1, T, send_expand)
    put(red_w, z, hs, reduce_in[...])
    put(wo_half, z, br, out_in[...])

    loop(1, T, lambda d: arrive(cut(joint_w, z * T + (p - d + T) % T, br), A2A_J, d))
    loop(1, b, lambda d: start(cut(joint_w, z, kb), cut(joint_w, z, kb), Z_J, d, up(d)))
    xhat1, rstd1 = norm_stats(tok[...].astype(F32))
    loop(1, T, lambda d: arrive(small.at[(p - d + T) % T], SMALL_P, d))
    small32[...] = small[...].astype(F32)
    fold = 128 // br
    halves = [
        sum(small32[h * fold + i] for i in range(1, fold)) + small32[h * fold]
        for h in range(T // fold)
    ]

    def vector(r):
        return jnp.concatenate(
            [half[e, r : r + 1, :] for e in range(b) for half in halves], axis=1
        )

    def place(ref, value):
        put(ref, p, rows, value)

    def gather_start(ref, base):
        mine = cut(ref, p, rows)
        loop(1, 4, lambda dc: start(mine, mine, base, dc, dev(chip(dc), k)))
        start(mine, mine, base + 4, 0, sib)

    def gather_wait(ref, base, dc):
        c2 = chip(dc)

        @pl.when(dc > 0)
        def _():
            block = cut(ref, 2 * c2 + k, rows)
            arrive(block, base, dc)
            start(block, block, base + 4, dc, sib)

        arrive(cut(ref, 2 * c2 + 1 - k, rows), base + 4, dc)

    def gather_finish(ref, base):
        def forward(dc):
            block = cut(ref, 2 * chip(dc) + k, rows)
            arrive(block, base, dc)
            start(block, block, base + 4, dc, sib)

        loop(1, 4, forward)
        loop(0, 4, lambda dc: arrive(cut(ref, 2 * chip(dc) + 1 - k, rows), base + 4, dc))

    place(n1, (xhat1 * vector(0) + vector(1)).astype(BF16))
    gather_start(n1, AG_N1)

    loop(1, T, lambda d: arrive(cut(exp_w, z * T + (p - d + T) % T, br), A2A_E, d))
    loop(1, b, lambda d: start(cut(exp_w, z, kb), cut(exp_w, z, kb), Z_E, d, up(d)))
    loop(1, b, lambda d: start(reduce_in, cut(red_w, z, hs), Z_R, d, up(d)))

    ends = line[9:10, :]
    column_pos = lax.broadcasted_iota(jnp.int32, (rows, 1), 0).astype(F32)
    row_pos = lax.broadcasted_iota(jnp.int32, (1, rows), 1).astype(F32)
    live = (column_pos < ends[:, seqs - 1 : seqs]).astype(F32)
    grad_final = cot[...].astype(F32) * live
    place(gf, grad_final.astype(BF16))

    def feature_bias(r):
        total = jnp.zeros((1, 128), F32)
        for j in range(hl):
            for k2 in range(2):
                total += small32[2 * c + k2, hl * k + j, r : r + 1, :]
        return total

    qb, vb = feature_bias(2), feature_bias(3)
    eb = jnp.concatenate([small32[p, e, 8:9, :] for e in range(b)], axis=1)

    gather_finish(n1, AG_N1)
    gather_start(gf, AG_GF)
    loop(1, b, lambda d: arrive(cut(wo_half, down(d), br), Z_O, d))
    give = cut(wo_half, 1 - k, hl * br)
    start(give, wo_sib, SIB_O, 0, sib)
    loop(1, b, lambda d: arrive(cut(joint_w, down(d), kb), Z_J, d))
    arrive(wo_sib, SIB_O, 0)
    kept = take(wo_half, k, hl * br)
    other = wo_sib[...]
    low = jnp.where(k == 0, kept, other)
    high = jnp.where(k == 0, other, kept)
    for j in range(hl):
        wout[2 * j * br : (2 * j + 1) * br, :] = low[j * br : (j + 1) * br]
        wout[(2 * j + 1) * br : (2 * j + 2) * br, :] = high[j * br : (j + 1) * br]

    scale = hd ** (-0.5)

    def send_hop(r, dc):
        start(cut(hsend.at[r], dc, rows), cut(hrecv.at[r], dc, rows), RS_0 + 8 * r + 4, dc, dev(chip(dc), k))

    def reduce_loop(slots, compute, ready=None, held=(), turn=1):
        def step(i):
            @pl.when(i < 4)
            def _():
                now = (i * turn) % 4
                c2 = chip(now)
                if ready is not None:
                    ready(now)
                for r, value in zip(slots, compute(c2)):
                    first, second = value[:rows], value[rows:]
                    put(csend.at[r], c2, rows, jnp.where(k == 0, second, first).astype(BF16))
                    start(cut(csend.at[r], c2, rows), cut(crecv.at[r], c2, rows), RS_0 + 8 * r, c2, sib)
                    put(part.at[r], now, rows, jnp.where(k == 0, first, second))

            @pl.when(i > 0)
            def _():
                dc = ((i - 1) * turn) % 4
                c2 = chip(dc)
                for r in slots:
                    arrive(cut(crecv.at[r], c2, rows), RS_0 + 8 * r, c2)
                    total = take(part.at[r], dc, rows) + take(crecv.at[r], c2, rows).astype(F32)

                    @pl.when(dc == 0)
                    def _():
                        put(part.at[r], 0, rows, total)

                    @pl.when(dc > 0)
                    def _():
                        put(hsend.at[r], dc, rows, total.astype(BF16))
                        if r not in held:
                            send_hop(r, dc)

        loop(0, 5, step)

    def reduce_finish(r):
        total = part[r, 0:rows, :]
        for dc in range(1, 4):
            arrive(cut(hrecv.at[r], dc, rows), RS_0 + 8 * r + 4, dc)
            total += hrecv[r, dc * rows : (dc + 1) * rows, :].astype(F32)
        return total

    pair = 2 * rows

    def attend(c2):
        packed = dot(take(n1, c2, pair), joint_w[...])
        q = (packed[:, :fl] + qb).astype(BF16)
        kk = packed[:, fl : 2 * fl].astype(BF16)
        v = (packed[:, 2 * fl :] + vb).astype(BF16)
        put(qkv, c2, pair, jnp.concatenate([q, kk, v], axis=1))
        blocks = []
        for half in range(2):
            at_row = slice(half * rows, (half + 1) * rows)
            bounds = small32[2 * c2 + half, z, 9:10, :]
            seg_q = jnp.zeros((rows, 1), F32)
            seg_k = jnp.zeros((1, rows), F32)
            for j in range(seqs):
                end = bounds[:, j : j + 1]
                seg_q += (column_pos >= end).astype(F32)
                seg_k += (row_pos >= end).astype(F32)
            last = bounds[:, seqs - 1 : seqs]
            seg_q = jnp.where(column_pos < last, seg_q, rows + column_pos)
            seg_k = jnp.where(row_pos < last, seg_k, rows + row_pos)
            allowed = (seg_q == seg_k) & (column_pos >= row_pos)
            outs = []
            for j in range(hl):
                at = slice(j * hd, (j + 1) * hd)
                scores = transposed_right(q[at_row, at], kk[at_row, at]) * scale
                scores = jnp.where(allowed, scores, -1e30)
                top = jnp.max(scores, axis=-1, keepdims=True)
                logsum = top + jnp.log(jnp.sum(jnp.exp(scores - top), axis=-1, keepdims=True))
                prob = jnp.exp(scores - logsum)
                put(probs, (2 * c2 + half) * hl + j, rows, prob)
                outs.append(dot(prob.astype(BF16), v[at_row, at]))
            blocks.append(jnp.concatenate(outs, axis=1))
        context = jnp.concatenate(blocks, axis=0).astype(BF16)
        put(ctx, c2, pair, context)
        return [dot(context, wout[...])]

    reduce_loop([0], attend, turn=3)
    gather_finish(gf, AG_GF)
    mid = tok[...].astype(F32) + reduce_finish(0) + vector(4)
    middle[...] = mid
    xhat2, rstd2 = norm_stats(mid)
    place(n2, (xhat2 * vector(5) + vector(6)).astype(BF16))
    gather_start(n2, AG_N2)
    loop(1, b, lambda d: arrive(cut(exp_w, down(d), kb), Z_E, d))

    def feed(dc):
        c2 = chip(dc)
        gather_wait(n2, AG_N2, dc)
        before = dot(take(n2, c2, pair), exp_w[...]) + eb
        square = before * before
        curve = jnp.tanh(TANH_SCALE * (before + CUBIC_TERM * before * square))
        put(act, c2, pair, (0.5 * before * (1.0 + curve)).astype(BF16))
        put(slope, c2, pair, 0.5 * (1.0 + curve) + 0.5 * before * (1.0 - curve * curve) * TANH_SCALE * (
            1.0 + 3.0 * CUBIC_TERM * square
        ))

    def weight_grad(left, cols, right, send, recv, mine, base):
        def step(i):
            d = i % b
            to = (z + d) % b
            part = transposed_left(
                left[:, pl.ds(pl.multiple_of(to * cols, cols), cols)], right[...]
            )

            @pl.when(i < b)
            def _():
                put(send, d, cols, part.astype(BF16))
                start(cut(send, d, cols), cut(recv, d, cols), base, d, up(d))

            @pl.when(i == b)
            def _():
                mine[...] = part

        loop(1, b + 1, step)

    loop(0, 4, feed)
    weight_grad(act, hs, gf, gr_send, gr_recv, gr_own, G_R)
    loop(1, b, lambda d: arrive(cut(red_w, down(d), hs), Z_R, d))
    ebias_acc[...] = jnp.zeros_like(ebias_acc)

    def feed_back(c2):
        grad_active = transposed_right(take(gf, c2, pair), red_w[...])
        grad_before = grad_active * take(slope, c2, pair)
        ebias_acc[...] += jnp.sum(grad_before, axis=0, keepdims=True)
        low_grad = grad_before.astype(BF16)
        put(gbl, c2, pair, low_grad)
        return [transposed_right(low_grad, exp_w[...]), dot(take(act, c2, pair), red_w[...])]

    reduce_loop([2, 1], feed_back, held=(1,), turn=3)
    weight_grad(n2, kb, gbl, ge_send, ge_recv, ge_own, G_E)

    grad_n2 = reduce_finish(2)
    mid = middle[...]
    xhat2, rstd2 = norm_stats(mid)
    row_grad, grad_g2, grad_s2 = norm_back(xhat2, rstd2, grad_n2, vector(5))
    grad_final = cot[...].astype(F32) * live
    grad_mid = grad_final + row_grad
    gmid[...] = grad_mid
    place(gm, grad_mid.astype(BF16))
    gather_start(gm, AG_GM)
    seg = width // b

    def vec_put(row, value):
        for e in range(b):
            vs[e, row : row + 1, :] = value[:, e * seg : (e + 1) * seg]

    vs[...] = jnp.zeros_like(vs)
    vec_put(2, jnp.sum(grad_mid, axis=0, keepdims=True))
    vec_put(3, grad_g2)
    vec_put(4, grad_s2)
    vec_put(5, jnp.sum(grad_final, axis=0, keepdims=True))
    bias_acc[...] = jnp.zeros_like(bias_acc)

    def attend_back(c2):
        grad_ctx = transposed_right(take(gm, c2, pair), wout[...]).astype(BF16)
        held = take(qkv, c2, pair)
        blocks = []
        for half in range(2):
            at_row = slice(half * rows, (half + 1) * rows)
            gqs, gks, gvs = [], [], []
            for j in range(hl):
                at = slice(j * hd, (j + 1) * hd)
                q = held[at_row, j * hd : (j + 1) * hd]
                kk = held[at_row, fl + j * hd : fl + (j + 1) * hd]
                v = held[at_row, 2 * fl + j * hd : 2 * fl + (j + 1) * hd]
                prob = take(probs, (2 * c2 + half) * hl + j, rows)
                grad_prob = transposed_right(grad_ctx[at_row, at], v)
                gvs.append(transposed_left(prob.astype(BF16), grad_ctx[at_row, at]))
                centre = jnp.sum(prob * grad_prob, axis=-1, keepdims=True)
                grad_score = (prob * (grad_prob - centre) * scale).astype(BF16)
                gqs.append(dot(grad_score, kk))
                gks.append(transposed_left(grad_score, q))
            blocks.append(jnp.concatenate(gqs + gks + gvs, axis=1))
        packed = jnp.concatenate(blocks, axis=0)
        bias_acc[...] += jnp.sum(packed, axis=0, keepdims=True)
        low_grad = packed.astype(BF16)
        put(gpk, c2, pair, low_grad)
        return [transposed_right(low_grad, joint_w[...])]

    def gm_ready(dc):
        gather_wait(gm, AG_GM, dc)

        @pl.when(dc == 3)
        def _():
            loop(1, 4, lambda d: send_hop(1, d))

    reduce_loop([3], attend_back, ready=gm_ready)
    weight_grad(n1, kb, gpk, gj_send, gj_recv, gj_own, G_J)
    grad_out = transposed_left(ctx[...], gm[...])
    evens = jnp.concatenate([grad_out[2 * j * br : (2 * j + 1) * br] for j in range(hl)], axis=0)
    odds = jnp.concatenate([grad_out[(2 * j + 1) * br : (2 * j + 2) * br] for j in range(hl)], axis=0)
    keep = jnp.where(k == 0, evens, odds)
    pass_on = jnp.where(k == 0, odds, evens)
    put(go_full, k, hl * br, keep.astype(BF16))
    go_sib[...] = pass_on.astype(BF16)
    start(go_sib, cut(go_full, k, hl * br), G_SIB, 0, sib)

    def collect(recv, mine, size, base):
        total = mine
        for d in range(1, b):
            arrive(cut(recv, d, size), base, d)
            total += recv[d * size : (d + 1) * size, :].astype(F32)
        return total

    def back(mine, landing, base):
        put(landing, p, br, take(mine, p, br))

        def step(d):
            q = (p + d) % T
            start(cut(mine, q, br), cut(landing, p, br), base, d, z * T + q)

        loop(1, T, step)

    gred_out[...] = collect(gr_recv, gr_own[...], hs, G_R)

    ge_low[...] = collect(ge_recv, ge_own[...], kb, G_E).astype(BF16)
    arrive(cut(go_full, 1 - k, hl * br), G_SIB, 0)

    def send_out(d):
        to = (z + d) % b
        start(cut(go_full, to, br), cut(go_recv, d, br), G_O, d, up(d))

    loop(1, b, send_out)
    grad_n1 = reduce_finish(3)
    xhat1, rstd1 = norm_stats(tok[...].astype(F32))
    row_grad, grad_g1, grad_s1 = norm_back(xhat1, rstd1, grad_n1, vector(0))
    gtok_out[...] = gmid[...] + row_grad
    vec_put(0, grad_g1)
    vec_put(1, grad_s1)
    for e in range(b):
        j = e % hl
        kept_row = jnp.concatenate(
            [bias_acc[:, j * hd : (j + 1) * hd], bias_acc[:, 2 * fl + j * hd : 2 * fl + (j + 1) * hd]], axis=1
        )
        vs[e, 6:7, :hs] = ebias_acc[:, e * hs : (e + 1) * hs]
        vs[e, 6:7, hs:] = jnp.where(k == e // hl, kept_row, 0.0)
    loop(1, b, lambda d: start(vs.at[(z + d) % b], vz_recv.at[d], VEC_Z, d, up(d)))

    back(ge_low, ge_back, BACK_E)
    total = vs[z]
    for d in range(1, b):
        arrive(vz_recv.at[d], VEC_Z, d)
        total += vz_recv[d]
    vp_own[...] = total
    vp[p] = total
    loop(1, T, lambda d: start(vp_own, vp.at[p], VEC_P, d, z * T + (p + d) % T))

    loop(1, T, lambda d: arrive(cut(ge_back, (p - d + T) % T, br), BACK_E, d))
    for q in range(T):
        for e in range(b):
            gexp_out[:, (e * T + q) * hs : (e * T + q + 1) * hs] = ge_back[
                q * br : (q + 1) * br, e * hs : (e + 1) * hs
            ].astype(F32)
    gj_low[...] = collect(gj_recv, gj_own[...], kb, G_J).astype(BF16)
    back(gj_low, gj_back, BACK_J)
    layer_out[...] = (middle[...] + reduce_finish(1) + vector(7)).astype(BF16)
    gout_out[...] = collect(go_recv, take(go_full, z, br).astype(F32), br, G_O)
    loop(1, T, lambda d: arrive(vp.at[(p - d + T) % T], VEC_P, d))
    total = jnp.sum(vp[...], axis=0)
    picked = jnp.zeros((8, br), F32)
    for q in range(T):
        picked = jnp.where(p == q, total[:, q * br : (q + 1) * br], picked)
    vec_out[0:8, 0:br] = picked
    vec_out[6:7, :] = vp[p, 6:7, :hs]
    keeper = 2 * c + z // hl
    row = vp[keeper, 6:7, :]
    for i in range(2):
        at = hs + i * hl * br
        vec_out[8 + i : 9 + i, 0:br] = jnp.where(k == 0, row[:, at : at + br], row[:, at + br : at + 2 * br])
    loop(1, T, lambda d: arrive(cut(gj_back, (p - d + T) % T, br), BACK_J, d))
    for w in range(3):
        for j in range(hl):
            at = slice((w * hl + j) * hd, (w * hl + j + 1) * hd)
            for k2 in range(2):
                for half in range(2):
                    q0, q1 = 4 * half + k2, 4 * half + 2 + k2
                    head = 2 * half + 4 * (hl * k2 + j)
                    gjoint_out[:, w * width + head * hd : w * width + (head + 2) * hd] = (
                        jnp.concatenate(
                            [gj_back[q0 * br : (q0 + 1) * br, at], gj_back[q1 * br : (q1 + 1) * br, at]],
                            axis=1,
                        ).astype(F32)
                    )

    sent(small.at[p, z], SMALL_Z, 1, b)
    sent(small.at[p], SMALL_P, 1, T)
    sent(cut(jstage, 0, br), A2A_J, 1, T)
    sent(cut(estage, 0, br), A2A_E, 1, T)
    sent(cut(joint_w, 0, kb), Z_J, 1, b)
    sent(cut(exp_w, 0, kb), Z_E, 1, b)
    sent(reduce_in, Z_R, 1, b)
    sent(out_in, Z_O, 1, b)
    sent(wo_sib, SIB_O, 0, 1)
    for base in (AG_N1, AG_GF, AG_N2, AG_GM):
        sent(cut(n1, 0, rows), base, 1, 8)
    for r in range(4):
        sent(cut(csend.at[0], 0, rows), RS_0 + 8 * r, 0, 4)
        sent(cut(csend.at[0], 0, rows), RS_0 + 8 * r, 5, 8)
    sent(cut(ge_send, 0, kb), G_E, 1, b)
    sent(cut(gr_send, 0, hs), G_R, 1, b)
    sent(cut(gj_send, 0, kb), G_J, 1, b)
    sent(go_sib, G_SIB, 0, 1)
    sent(cut(go_recv, 0, br), G_O, 1, b)
    sent(cut(ge_low, 0, br), BACK_E, 1, T)
    sent(cut(gj_low, 0, br), BACK_J, 1, T)
    sent(vs.at[0], VEC_Z, 1, b)
    sent(vp_own, VEC_P, 1, T)


def finish(count, vec, *refs):
    large_in, large_out, small_out = refs[:count], refs[count : 2 * count], refs[2 * count : -count - 2]
    held, sem_in, sem_out = refs[-count - 2 : -2], refs[-2], refs[-1]
    inward = [pltpu.make_async_copy(x, h, sem_in.at[i]) for i, (x, h) in enumerate(zip(large_in, held))]
    outward = [pltpu.make_async_copy(h, x, sem_out.at[i]) for i, (h, x) in enumerate(zip(held, large_out))]
    for copy in inward:
        copy.start()
    for r, out in zip((0, 1, 8, 9, 2, 3, 4, 5, 6), small_out):
        size = out.shape[0]
        out[...] = vec[r : r + 1, :size].reshape(size)
    for first, second in zip(inward, outward):
        first.wait()
        second.start()
    for copy in outward:
        copy.wait()


def fused(
    tokens, lengths, cotangent, norm1_gain, norm1_shift, joint_weight, query_bias, value_bias,
    output_weight, output_bias, norm2_gain, norm2_shift, expand_weight, expand_bias,
    reduce_weight, reduce_bias,
):
    n = lax.axis_size("dp")
    T = TENSOR
    b = n // T
    rows, width = tokens.shape
    br = joint_weight.shape[0]
    hs = reduce_weight.shape[0]
    fl = width // T
    hl = HEADS // T
    seqs = lengths.shape[1]
    kb, f, fj, tt = br * T, b * hs, 3 * fl, T * rows
    vm = pltpu.VMEM
    scratch = [
        vm((16, 128), F32), vm((T, b, 16, 128), BF16), vm((T, b, 16, 128), F32), vm((kb, fj), BF16), vm((kb, f), BF16), vm((width, fj), BF16),
        vm((width, f), BF16), vm((f, width), BF16), vm((b * br, width), BF16),
        vm((hl * br, width), BF16), vm((fl, width), BF16),
        vm((tt, width), BF16), vm((tt, width), BF16), vm((tt, width), BF16), vm((tt, width), BF16),
        vm((tt, fj), BF16), vm((tt * hl, rows), F32), vm((tt, fl), BF16),
        vm((tt, f), BF16), vm((tt, f), BF16), vm((tt, fj), BF16), vm((tt, f), F32),
        vm((4, 4 * rows, width), BF16), vm((4, 4 * rows, width), BF16),
        vm((4, 4 * rows, width), BF16), vm((4, 4 * rows, width), BF16),
        vm((4, 4 * rows, width), F32), vm((rows, width), F32), vm((rows, width), F32),
        vm((b * kb, f), BF16), vm((b * kb, f), BF16), vm((kb, f), F32),
        vm((b * hs, width), BF16), vm((b * hs, width), BF16), vm((hs, width), F32),
        vm((b * kb, fj), BF16), vm((b * kb, fj), BF16), vm((kb, fj), F32),
        vm((b * br, width), BF16), vm((hl * br, width), BF16), vm((hl * br, width), BF16), vm((b * br, width), BF16),
        vm((kb, f), BF16), vm((kb, fj), BF16), vm((kb, f), BF16), vm((kb, fj), BF16),
        vm((b, 8, width // b), F32), vm((b, 8, width // b), F32), vm((8, width // b), F32), vm((T, 8, width // b), F32),
        vm((1, fj), F32), vm((1, f), F32),
        pltpu.SemaphoreType.DMA((SEMS,)), pltpu.SemaphoreType.DMA((SEMS,)),
    ]
    sds = jax.ShapeDtypeStruct
    *large, vec = pl.pallas_call(
        functools.partial(kernel, seqs),
        out_shape=(
            sds((rows, width), BF16), sds((rows, width), F32), sds((br, 3 * width), F32),
            sds((br, width), F32), sds((br, expand_weight.shape[1]), F32), sds((hs, width), F32),
            sds((16, hs), F32),
        ),
        in_specs=[pl.BlockSpec(memory_space=pltpu.VMEM)] * 16,
        out_specs=tuple([pl.BlockSpec(memory_space=pltpu.VMEM)] * 7),
        scratch_shapes=scratch,
        compiler_params=pltpu.CompilerParams(
            collective_id=0, has_side_effects=True, vmem_limit_bytes=62 * 1024 * 1024
        ),
        name="layer",
    )(
        tokens, cotangent, joint_weight, output_weight, expand_weight, reduce_weight, lengths,
        norm1_gain, norm1_shift, query_bias, value_bias, output_bias, norm2_gain, norm2_shift,
        reduce_bias, expand_bias,
    )

    anywhere, inside = pl.BlockSpec(memory_space=pl.ANY), pl.BlockSpec(memory_space=pltpu.VMEM)
    done = pl.pallas_call(
        functools.partial(finish, len(large)),
        out_shape=tuple(sds(x.shape, x.dtype) for x in large)
        + tuple(sds((br,), F32) for _ in range(8)) + (sds((hs,), F32),),
        in_specs=[inside] + [anywhere] * len(large),
        out_specs=tuple([anywhere] * len(large) + [inside] * 9),
        scratch_shapes=[pltpu.VMEM(x.shape, x.dtype) for x in large]
        + [pltpu.SemaphoreType.DMA((len(large),))] * 2,
        name="finish",
    )(vec, *large)
    layer_output, grad_tokens, g_joint, g_out, g_exp, g_red = done[:6]
    g_g1, g_s1, g_qb, g_vb, g_ob, g_g2, g_s2, g_rb, g_eb = done[6:]
    return (
        layer_output, grad_tokens, g_g1, g_s1, g_joint, g_qb, g_vb, g_out,
        g_ob, g_g2, g_s2, g_exp, g_eb, g_red, g_rb,
    )


def fits(n, width):
    br = width // n
    return n % TENSOR == 0 and br % 16 == 0 and 2 * br * HEADS == width and n // TENSOR == 2 * (HEADS // TENSOR)


def whole(*args):
    n = lax.axis_size("dp")
    return fused(*args) if fits(n, args[0].shape[1]) else on_device(*args)


def solution(mesh):
    m, v = P("dp", None), P("dp")
    in_specs = (m, m, m, v, v, m, v, v, m, v, v, v, m, v, m, v)
    out_specs = (m, m, v, v, m, v, v, m, v, v, v, m, v, m, v)
    return jax.shard_map(
        whole, mesh=mesh, in_specs=in_specs, out_specs=out_specs, check_vma=False
    )
```

```python
import functools

import jax
import jax.numpy as jnp
from jax import lax
from jax.experimental import pallas as pl
from jax.experimental.pallas import tpu as pltpu
from jax.sharding import PartitionSpec as P

HEADS = 16
TENSOR = 8

EPSILON = 1e-05
TANH_SCALE = 0.7978845608028654
CUBIC_TERM = 0.044715

F32 = jnp.float32
BF16 = jnp.bfloat16


def layer_norm(row_data, gain_vector, shift_vector):
    average = jnp.mean(row_data, axis=-1, keepdims=True)
    centred = row_data - average
    spread = jnp.mean(centred * centred, axis=-1, keepdims=True)
    return centred * lax.rsqrt(spread + EPSILON) * gain_vector + shift_vector


def activation(values_in):
    return (
        0.5
        * values_in
        * (
            1.0
            + jnp.tanh(TANH_SCALE * (values_in + CUBIC_TERM * values_in * values_in * values_in))
        )
    )


def contract(pattern, first_op, second_op):
    return jnp.einsum(pattern, first_op, second_op, preferred_element_type=F32)


def dot(first_op, second_op):
    return jnp.dot(first_op, second_op, preferred_element_type=F32)


def transposed_left(first_op, second_op):
    return lax.dot_general(
        first_op, second_op, (((0,), (0,)), ((), ())), preferred_element_type=F32
    )


def transposed_right(first_op, second_op):
    return lax.dot_general(
        first_op, second_op, (((1,), (1,)), ((), ())), preferred_element_type=F32
    )


def slot_mask(lengths_row, row_count):
    position = jnp.arange(row_count, dtype=jnp.int32)
    segment = jnp.zeros((row_count,), jnp.int32)
    end = jnp.int32(0)
    for j in range(lengths_row.shape[0]):
        end = end + lengths_row[j]
        segment = segment + (position >= end).astype(jnp.int32)
    live_rows = position < end
    segment = jnp.where(live_rows, segment, row_count + position)
    allowed = (segment[:, None] == segment[None, :]) & (position[:, None] >= position[None, :])
    return (allowed, live_rows.astype(F32))


def on_device(
    tokens,
    lengths,
    cotangent,
    norm1_gain,
    norm1_shift,
    joint_weight,
    query_bias,
    value_bias,
    output_weight,
    output_bias,
    norm2_gain,
    norm2_shift,
    expand_weight,
    expand_bias,
    reduce_weight,
    reduce_bias,
):
    n = lax.axis_size("dp")
    t = TENSOR if n % TENSOR == 0 else 1
    b = n // t
    rows, width = tokens.shape
    hid = expand_weight.shape[1]
    br = joint_weight.shape[0]
    hs = reduce_weight.shape[0]
    head_size = width // HEADS
    hl = HEADS // t
    fl = width // t
    me = lax.axis_index("dp")
    mine = me % t
    plane = [[z * t + p for p in range(t)] for z in range(b)]
    column = [[z * t + p for z in range(b)] for p in range(t)]
    swap = [(z * t + p, p * b + z) for z in range(b) for p in range(t)]

    def gather(x, groups):
        return lax.all_gather(x, "dp", axis=0, tiled=True, axis_index_groups=groups)

    def scatter(x, groups):
        return lax.psum_scatter(
            x, "dp", scatter_dimension=0, tiled=True, axis_index_groups=groups
        )

    def exchange(x):
        return lax.all_to_all(
            x, "dp", split_axis=0, concat_axis=0, tiled=True, axis_index_groups=plane
        )

    vecs = [
        norm1_gain, norm1_shift, query_bias, value_bias, output_bias,
        norm2_gain, norm2_shift, expand_bias, reduce_bias,
    ]
    sizes = [v.shape[0] for v in vecs]
    small = lax.all_gather(jnp.concatenate(vecs)[None, :], "dp", axis=0, tiled=True)
    whole, at = [], 0
    for s in sizes:
        whole.append(small[:, at : at + s].reshape(-1).astype(F32))
        at += s
    gain1, shift1, qb, vb, ob, gain2, shift2, eb, rb = whole
    eb = lax.dynamic_slice_in_dim(eb.reshape(b, t, hs), mine, 1, 1).reshape(-1)
    qb = lax.dynamic_slice_in_dim(qb, mine * fl, fl, 0)
    vb = lax.dynamic_slice_in_dim(vb, mine * fl, fl, 0)

    joint_cut = joint_weight.reshape(br, 3, t, fl).transpose(2, 0, 1, 3).reshape(t * br, 3 * fl)
    expand_cut = expand_weight.reshape(br, b, t, hs).transpose(2, 0, 1, 3).reshape(t * br, b * hs)
    out_mine = lax.ppermute(output_weight, "dp", [(d, s) for s, d in swap])
    wout = gather(out_mine, column)
    joint = gather(exchange(joint_cut), column)
    expand = gather(exchange(expand_cut), column)
    reduce = gather(reduce_weight, column)

    lens = gather(lengths, plane)
    allowed, _ = jax.vmap(lambda r: slot_mask(r, rows))(lens)
    _, live = slot_mask(lengths[0], rows)

    residual = tokens.astype(F32)
    n1 = gather(layer_norm(residual, gain1, shift1).astype(BF16), plane)
    grad_final = cotangent.astype(F32) * live[:, None]
    gf = gather(grad_final.astype(BF16), plane)

    packed = dot(n1, joint)
    shape4 = (t, rows, hl, head_size)
    q = (packed[:, :fl] + qb).astype(BF16).reshape(shape4)
    k = packed[:, fl : 2 * fl].astype(BF16).reshape(shape4)
    v = (packed[:, 2 * fl :] + vb).astype(BF16).reshape(shape4)
    scale = head_size ** (-0.5)
    scores = contract("gqhd,gkhd->ghqk", q, k) * scale
    scores = jnp.where(allowed[:, None], scores, -1e30)
    top = jnp.max(scores, axis=-1, keepdims=True)
    logsum = top + jnp.log(jnp.sum(jnp.exp(scores - top), axis=-1, keepdims=True))
    probs = jnp.exp(scores - logsum)
    weights = probs.astype(BF16)
    context = contract("ghqk,gkhd->gqhd", weights, v).astype(BF16).reshape(t * rows, fl)
    middle = (
        residual + scatter(dot(context, wout).astype(BF16), plane).astype(F32) + ob
    )
    n2 = gather(layer_norm(middle, gain2, shift2).astype(BF16), plane)
    before = dot(n2, expand) + eb
    active = activation(before).astype(BF16)
    final = middle + scatter(dot(active, reduce).astype(BF16), plane).astype(F32) + rb
    layer_output = final.astype(BF16)

    grad_rb = jnp.sum(grad_final, axis=0)
    g_reduce = transposed_left(active, gf)
    _, curve_back = jax.vjp(activation, before)
    gb = curve_back(transposed_right(gf, reduce))[0]
    grad_eb = jnp.sum(gb, axis=0)
    gbl = gb.astype(BF16)
    g_expand = transposed_left(n2, gbl)
    gn2 = scatter(transposed_right(gbl, expand).astype(BF16), plane).astype(F32)
    _, back2 = jax.vjp(layer_norm, middle, gain2, shift2)
    gmn, grad_g2, grad_s2 = back2(gn2)
    gm_own = grad_final + gmn
    grad_ob = jnp.sum(gm_own, axis=0)
    gm = gather(gm_own.astype(BF16), plane)
    g_out = transposed_left(context, gm)
    gctx = transposed_right(gm, wout).astype(BF16).reshape(shape4)
    gp = contract("gqhd,gkhd->ghqk", gctx, v)
    gv = contract("ghqk,gqhd->gkhd", weights, gctx).reshape(t * rows, fl)
    centre = jnp.sum(probs * gp, axis=-1, keepdims=True)
    gs = (probs * (gp - centre) * scale).astype(BF16)
    gq = contract("ghqk,gkhd->gqhd", gs, k).reshape(t * rows, fl)
    gk = contract("ghqk,gqhd->gkhd", gs, q).reshape(t * rows, fl)
    grad_qb = jnp.sum(gq, axis=0)
    grad_vb = jnp.sum(gv, axis=0)
    gpacked = jnp.concatenate([gq, gk, gv], axis=1).astype(BF16)
    g_joint = transposed_left(n1, gpacked)
    gn1 = scatter(transposed_right(gpacked, joint).astype(BF16), plane).astype(F32)
    _, back1 = jax.vjp(layer_norm, residual, gain1, shift1)
    gtn, grad_g1, grad_s1 = back1(gn1)
    grad_tokens = gm_own + gtn

    reduce_out = scatter(g_reduce.astype(BF16), column).astype(F32)
    expand_out = (
        exchange(scatter(g_expand.astype(BF16), column))
        .reshape(t, br, b, hs).transpose(1, 2, 0, 3).reshape(br, hid).astype(F32)
    )
    joint_out = (
        exchange(scatter(g_joint.astype(BF16), column))
        .reshape(t, br, 3, fl).transpose(1, 2, 0, 3).reshape(br, 3 * width).astype(F32)
    )
    out_out = lax.ppermute(scatter(g_out.astype(BF16), column), "dp", swap).astype(F32)

    def place(x):
        return lax.dynamic_update_slice_in_dim(jnp.zeros((width,), F32), x, mine * fl, 0)

    full_eb = lax.dynamic_update_slice_in_dim(
        jnp.zeros((b, t, hs), F32), grad_eb.reshape(b, 1, hs), mine, 1
    )
    grads = [grad_g1, grad_s1, place(grad_qb), place(grad_vb), grad_ob, grad_g2, grad_s2, full_eb, grad_rb]
    sums = lax.psum_scatter(
        jnp.concatenate([g.reshape(n, -1) for g in grads], axis=1),
        "dp", scatter_dimension=0, tiled=True,
    )[0]
    pieces, at = [], 0
    for s in sizes:
        pieces.append(sums[at : at + s])
        at += s
    return (
        layer_output, grad_tokens, pieces[0], pieces[1], joint_out, pieces[2], pieces[3],
        out_out, pieces[4], pieces[5], pieces[6], expand_out, pieces[7], reduce_out, pieces[8],
    )


def cut(ref, index, size):
    return ref.at[pl.ds(pl.multiple_of(index * size, size), size)]


def take(ref, index, size):
    return ref[pl.ds(pl.multiple_of(index * size, size), size), :]


def put(ref, index, size, value):
    ref[pl.ds(pl.multiple_of(index * size, size), size), :] = value


def loop(low, high, step):
    def body(i, carry):
        step(i)
        return carry

    lax.fori_loop(low, high, body, 0)


def norm_stats(x):
    average = jnp.mean(x, axis=-1, keepdims=True)
    centred = x - average
    spread = jnp.mean(centred * centred, axis=-1, keepdims=True)
    rstd = lax.rsqrt(spread + EPSILON)
    return centred * rstd, rstd


def norm_back(xhat, rstd, grad_out, gain):
    scaled = grad_out * gain
    first = jnp.mean(scaled, axis=-1, keepdims=True)
    second = jnp.mean(scaled * xhat, axis=-1, keepdims=True)
    grad_gain = jnp.sum(grad_out * xhat, axis=0, keepdims=True)
    grad_shift = jnp.sum(grad_out, axis=0, keepdims=True)
    return rstd * (scaled - first - xhat * second), grad_gain, grad_shift


SMALL_P, SMALL_Z = 0, 8
A2A_J, A2A_E = 12, 20
Z_J, Z_E, Z_R, Z_O, SIB_O = 28, 32, 36, 40, 44
AG_N1, AG_GF, AG_N2, AG_GM = 48, 56, 64, 72
RS_0 = 80
G_E, G_R, G_J, G_O, G_SIB = 112, 116, 120, 124, 128
BACK_E, BACK_J = 132, 140
VEC_P, VEC_Z = 148, 156
RELAY_E, RELAY_R = 160, 161
SEMS = 164


def kernel(
    seqs,
    tok, cot, joint_in, out_in, expand_in, reduce_in, lens,
    v_g1, v_s1, v_qb, v_vb, v_ob, v_g2, v_s2, v_rb, v_eb,
    layer_out, gtok_out, gjoint_out, gout_out, gexp_out, gred_out, vec_out,
    line, small, small32, jstage, estage, joint_w, exp_w, red_w, wo_half, wo_sib, wout,
    n1, n2, gf, gm, qkv, probs, ctx, act, gbl, gpk,
    slope, csend, crecv, hsend, hrecv, part, middle, gmid,
    ge_send, ge_recv, ge_own, gr_send, gr_recv, gr_own,
    gj_send, gj_recv, gj_own, go_full, go_sib, go_send, go_recv,
    ge_low, gj_low, ge_back, gj_back, vs, vz_recv, vp_own, vp, bias_acc, ebias_acc,
    ssem, rsem,
):
    T = TENSOR
    rows, width = tok.shape
    br = joint_in.shape[0]
    me = lax.axis_index("dp")
    n = lax.axis_size("dp")
    b = n // T
    z = me // T
    p = me % T
    c = p // 2
    k = p % 2
    sib = z * T + 2 * c + (1 - k)
    hs = reduce_in.shape[0]
    fl = width // T
    hd = width // HEADS
    hl = HEADS // T
    kb = br * T

    def chip(dc):
        return ((c // 2 + dc // 2) % 2) * 2 + (c % 2 + dc % 2) % 2

    def dev(c2, k2):
        return z * T + 2 * c2 + k2

    def up(d):
        return ((z + d) % b) * T + p

    def down(d):
        return (z - d + b) % b

    def rc(src, dst, base, i, device):
        return pltpu.make_async_remote_copy(
            src_ref=src, dst_ref=dst, send_sem=ssem.at[base + i], recv_sem=rsem.at[base + i],
            device_id=(device,), device_id_type=pl.DeviceIdType.MESH,
        )

    def start(src, dst, base, i, device):
        rc(src, dst, base, i, device).start()

    def arrive(dst, base, i):
        rc(dst, dst, base, i, sib).wait_recv()

    def sent(src, base, low, high):
        loop(low, high, lambda i: rc(src, src, base, i, sib).wait_send())

    far = jnp.where(z == 0, b - 1, jnp.where(z == b - 1, 1, 0))
    middle_z = (z == 1) | (z == b - 2)
    source = jnp.where(z == 1, b - 1, 0)
    target = b - 1 - source

    def spread(src, dst, base):
        def step(i):
            d = 1 + i % (b - 1)

            @pl.when(d != far)
            def _():
                start(src, dst, base, d, up(d))

        loop(1, b, step)

    def passing(ref, size, base, slot):
        block = cut(ref, source, size)
        return pltpu.make_async_remote_copy(
            src_ref=block, dst_ref=block, send_sem=ssem.at[slot],
            recv_sem=rsem.at[base + (target - source + b) % b],
            device_id=(target * T + p,), device_id_type=pl.DeviceIdType.MESH,
        )

    def relay(ref, size, base, slot):
        @pl.when(middle_z)
        def _():
            arrive(cut(ref, source, size), base, 2)
            passing(ref, size, base, slot).start()

    def spread_arrive(ref, size, base):
        def step(d):
            @pl.when(jnp.logical_not(middle_z & (d == 2)))
            def _():
                arrive(cut(ref, down(d), size), base, d)

        loop(1, b, step)

    def spread_sent(ref, size, base, slot):
        def step(d):
            @pl.when(d != far)
            def _():
                rc(cut(ref, 0, size), cut(ref, 0, size), base, d, sib).wait_send()

        loop(1, b, step)

        @pl.when(middle_z)
        def _():
            passing(ref, size, base, slot).wait_send()

    barrier = pltpu.get_barrier_semaphore()
    loop(1, T, lambda d: pl.semaphore_signal(
        barrier, inc=1, device_id=(z * T + (p + d) % T,), device_id_type=pl.DeviceIdType.MESH))
    loop(1, b, lambda d: pl.semaphore_signal(
        barrier, inc=1, device_id=(up(d),), device_id_type=pl.DeviceIdType.MESH))
    pl.semaphore_wait(barrier, T - 1 + b - 1)

    loop(1, b, lambda d: start(out_in, cut(wo_half, z, br), Z_O, d, up(d)))
    lane = lax.broadcasted_iota(jnp.int32, (1, 128), 1)
    plain = (me % (128 // br)) * br
    headed = ((z % hl) * 2 + k) * br
    line[...] = jnp.zeros_like(line)
    for r, v in enumerate((v_g1, v_s1, v_qb, v_vb, v_ob, v_g2, v_s2, v_rb)):
        at = headed if r in (2, 3) else plain
        tiled = jnp.concatenate([v[...].astype(F32).reshape(1, br)] * (128 // br), axis=1)
        line[r : r + 1, :] = jnp.where((lane >= at) & (lane < at + br), tiled, 0.0)
    line[8:9, :] = v_eb[...].astype(F32).reshape(1, hs)
    running = jnp.zeros((1, 1), F32)
    marks = jnp.zeros((1, 128), F32)
    for j in range(seqs):
        running = running + lens[:, j : j + 1].astype(F32)
        marks = jnp.where(lane == j, running, marks)
    line[9:10, :] = marks
    small[p, z] = line[...].astype(BF16)
    loop(1, b, lambda d: start(small.at[p, z], small.at[p, z], SMALL_Z, d, up(d)))

    for q in range(T):
        c2, k2 = q // 2, q % 2
        pieces = [
            joint_in[:, w * width + (c2 + 4 * (hl * k2 + j)) * hd : w * width + (c2 + 4 * (hl * k2 + j) + 1) * hd]
            for w in range(3) for j in range(hl)
        ]
        jstage[q * br : (q + 1) * br, :] = jnp.concatenate(pieces, axis=1)
    put(joint_w, z * T + p, br, take(jstage, p, br))

    def send_joint(d):
        q = (p + d) % T
        start(cut(jstage, q, br), cut(joint_w, z * T + p, br), A2A_J, d, z * T + q)

    loop(1, T, send_joint)
    loop(1, b, lambda d: arrive(small.at[p, down(d)], SMALL_Z, d))
    loop(1, T, lambda d: start(small.at[p], small.at[p], SMALL_P, d, z * T + (p + d) % T))
    for q in range(T):
        pieces = [expand_in[:, (e * T + q) * hs : (e * T + q + 1) * hs] for e in range(b)]
        estage[q * br : (q + 1) * br, :] = jnp.concatenate(pieces, axis=1)
    put(exp_w, z * T + p, br, take(estage, p, br))

    def send_expand(d):
        q = (p + d) % T
        start(cut(estage, q, br), cut(exp_w, z * T + p, br), A2A_E, d, z * T + q)

    loop(1, T, send_expand)
    put(red_w, z, hs, reduce_in[...])
    put(wo_half, z, br, out_in[...])

    loop(1, T, lambda d: arrive(cut(joint_w, z * T + (p - d + T) % T, br), A2A_J, d))
    loop(1, b, lambda d: start(cut(joint_w, z, kb), cut(joint_w, z, kb), Z_J, d, up(d)))
    xhat1, rstd1 = norm_stats(tok[...].astype(F32))
    loop(1, T, lambda d: arrive(small.at[(p - d + T) % T], SMALL_P, d))
    small32[...] = small[...].astype(F32)
    fold = 128 // br
    halves = [
        sum(small32[h * fold + i] for i in range(1, fold)) + small32[h * fold]
        for h in range(T // fold)
    ]

    def vector(r):
        return jnp.concatenate(
            [half[e, r : r + 1, :] for e in range(b) for half in halves], axis=1
        )

    def place(ref, value):
        put(ref, p, rows, value)

    def gather_start(ref, base):
        mine = cut(ref, p, rows)
        loop(1, 4, lambda dc: start(mine, mine, base, dc, dev(chip(dc), k)))
        start(mine, mine, base + 4, 0, sib)

    def gather_wait(ref, base, dc):
        c2 = chip(dc)

        @pl.when(dc > 0)
        def _():
            block = cut(ref, 2 * c2 + k, rows)
            arrive(block, base, dc)
            start(block, block, base + 4, dc, sib)

        arrive(cut(ref, 2 * c2 + 1 - k, rows), base + 4, dc)

    def gather_finish(ref, base):
        def forward(dc):
            block = cut(ref, 2 * chip(dc) + k, rows)
            arrive(block, base, dc)
            start(block, block, base + 4, dc, sib)

        loop(1, 4, forward)
        loop(0, 4, lambda dc: arrive(cut(ref, 2 * chip(dc) + 1 - k, rows), base + 4, dc))

    place(n1, (xhat1 * vector(0) + vector(1)).astype(BF16))
    gather_start(n1, AG_N1)

    loop(1, T, lambda d: arrive(cut(exp_w, z * T + (p - d + T) % T, br), A2A_E, d))
    spread(cut(exp_w, z, kb), cut(exp_w, z, kb), Z_E)
    loop(1, b, lambda d: start(reduce_in, cut(red_w, z, hs), Z_R, d, up(d)))

    ends = line[9:10, :]
    column_pos = lax.broadcasted_iota(jnp.int32, (rows, 1), 0).astype(F32)
    row_pos = lax.broadcasted_iota(jnp.int32, (1, rows), 1).astype(F32)
    live = (column_pos < ends[:, seqs - 1 : seqs]).astype(F32)
    grad_final = cot[...].astype(F32) * live
    place(gf, grad_final.astype(BF16))

    def feature_bias(r):
        total = jnp.zeros((1, 128), F32)
        for j in range(hl):
            for k2 in range(2):
                total += small32[2 * c + k2, hl * k + j, r : r + 1, :]
        return total

    qb, vb = feature_bias(2), feature_bias(3)
    eb = jnp.concatenate([small32[p, e, 8:9, :] for e in range(b)], axis=1)

    gather_finish(n1, AG_N1)
    gather_start(gf, AG_GF)
    loop(1, b, lambda d: arrive(cut(wo_half, down(d), br), Z_O, d))
    give = cut(wo_half, 1 - k, hl * br)
    start(give, wo_sib, SIB_O, 0, sib)
    loop(1, b, lambda d: arrive(cut(joint_w, down(d), kb), Z_J, d))
    arrive(wo_sib, SIB_O, 0)
    kept = take(wo_half, k, hl * br)
    other = wo_sib[...]
    low = jnp.where(k == 0, kept, other)
    high = jnp.where(k == 0, other, kept)
    for j in range(hl):
        wout[2 * j * br : (2 * j + 1) * br, :] = low[j * br : (j + 1) * br]
        wout[(2 * j + 1) * br : (2 * j + 2) * br, :] = high[j * br : (j + 1) * br]

    scale = hd ** (-0.5)

    def send_hop(r, dc):
        start(cut(hsend.at[r], dc, rows), cut(hrecv.at[r], dc, rows), RS_0 + 8 * r + 4, dc, dev(chip(dc), k))

    def reduce_loop(slots, compute, ready=None, held=(), turn=1):
        def step(i):
            @pl.when(i < 4)
            def _():
                now = (i * turn) % 4
                c2 = chip(now)
                if ready is not None:
                    ready(now)
                for r, value in zip(slots, compute(c2)):
                    first, second = value[:rows], value[rows:]
                    put(csend.at[r], c2, rows, jnp.where(k == 0, second, first).astype(BF16))
                    start(cut(csend.at[r], c2, rows), cut(crecv.at[r], c2, rows), RS_0 + 8 * r, c2, sib)
                    put(part.at[r], now, rows, jnp.where(k == 0, first, second))

            @pl.when(i > 0)
            def _():
                dc = ((i - 1) * turn) % 4
                c2 = chip(dc)
                for r in slots:
                    arrive(cut(crecv.at[r], c2, rows), RS_0 + 8 * r, c2)
                    total = take(part.at[r], dc, rows) + take(crecv.at[r], c2, rows).astype(F32)

                    @pl.when(dc == 0)
                    def _():
                        put(part.at[r], 0, rows, total)

                    @pl.when(dc > 0)
                    def _():
                        put(hsend.at[r], dc, rows, total.astype(BF16))
                        if r not in held:
                            send_hop(r, dc)

        loop(0, 5, step)

    def reduce_finish(r):
        total = part[r, 0:rows, :]
        for dc in range(1, 4):
            arrive(cut(hrecv.at[r], dc, rows), RS_0 + 8 * r + 4, dc)
            total += hrecv[r, dc * rows : (dc + 1) * rows, :].astype(F32)
        return total

    pair = 2 * rows

    def attend(c2):
        packed = dot(take(n1, c2, pair), joint_w[...])
        q = (packed[:, :fl] + qb).astype(BF16)
        kk = packed[:, fl : 2 * fl].astype(BF16)
        v = (packed[:, 2 * fl :] + vb).astype(BF16)
        put(qkv, c2, pair, jnp.concatenate([q, kk, v], axis=1))
        blocks = []
        for half in range(2):
            at_row = slice(half * rows, (half + 1) * rows)
            bounds = small32[2 * c2 + half, z, 9:10, :]
            seg_q = jnp.zeros((rows, 1), F32)
            seg_k = jnp.zeros((1, rows), F32)
            for j in range(seqs):
                end = bounds[:, j : j + 1]
                seg_q += (column_pos >= end).astype(F32)
                seg_k += (row_pos >= end).astype(F32)
            last = bounds[:, seqs - 1 : seqs]
            seg_q = jnp.where(column_pos < last, seg_q, rows + column_pos)
            seg_k = jnp.where(row_pos < last, seg_k, rows + row_pos)
            allowed = (seg_q == seg_k) & (column_pos >= row_pos)
            outs = []
            for j in range(hl):
                at = slice(j * hd, (j + 1) * hd)
                scores = transposed_right(q[at_row, at], kk[at_row, at]) * scale
                scores = jnp.where(allowed, scores, -1e30)
                top = jnp.max(scores, axis=-1, keepdims=True)
                logsum = top + jnp.log(jnp.sum(jnp.exp(scores - top), axis=-1, keepdims=True))
                prob = jnp.exp(scores - logsum)
                put(probs, (2 * c2 + half) * hl + j, rows, prob)
                outs.append(dot(prob.astype(BF16), v[at_row, at]))
            blocks.append(jnp.concatenate(outs, axis=1))
        context = jnp.concatenate(blocks, axis=0).astype(BF16)
        put(ctx, c2, pair, context)
        return [dot(context, wout[...])]

    reduce_loop([0], attend, turn=3)
    relay(exp_w, kb, Z_E, RELAY_E)
    gather_finish(gf, AG_GF)
    mid = tok[...].astype(F32) + reduce_finish(0) + vector(4)
    middle[...] = mid
    xhat2, rstd2 = norm_stats(mid)
    place(n2, (xhat2 * vector(5) + vector(6)).astype(BF16))
    gather_start(n2, AG_N2)
    spread_arrive(exp_w, kb, Z_E)

    def feed(dc):
        c2 = chip(dc)
        gather_wait(n2, AG_N2, dc)
        before = dot(take(n2, c2, pair), exp_w[...]) + eb
        square = before * before
        curve = jnp.tanh(TANH_SCALE * (before + CUBIC_TERM * before * square))
        put(act, c2, pair, (0.5 * before * (1.0 + curve)).astype(BF16))
        put(slope, c2, pair, 0.5 * (1.0 + curve) + 0.5 * before * (1.0 - curve * curve) * TANH_SCALE * (
            1.0 + 3.0 * CUBIC_TERM * square
        ))

    def weight_grad(left, cols, right, send, recv, mine, base):
        def step(i):
            d = i % b
            to = (z + d) % b
            part = transposed_left(
                left[:, pl.ds(pl.multiple_of(to * cols, cols), cols)], right[...]
            )

            @pl.when(i < b)
            def _():
                put(send, d, cols, part.astype(BF16))
                start(cut(send, d, cols), cut(recv, d, cols), base, d, up(d))

            @pl.when(i == b)
            def _():
                mine[...] = part

        loop(1, b + 1, step)

    loop(0, 4, feed)
    loop(1, b, lambda d: arrive(cut(red_w, down(d), hs), Z_R, d))
    weight_grad(act, hs, gf, gr_send, gr_recv, gr_own, G_R)
    ebias_acc[...] = jnp.zeros_like(ebias_acc)

    def feed_back(c2):
        grad_active = transposed_right(take(gf, c2, pair), red_w[...])
        grad_before = grad_active * take(slope, c2, pair)
        ebias_acc[...] += jnp.sum(grad_before, axis=0, keepdims=True)
        low_grad = grad_before.astype(BF16)
        put(gbl, c2, pair, low_grad)
        return [transposed_right(low_grad, exp_w[...]), dot(take(act, c2, pair), red_w[...])]

    reduce_loop([2, 1], feed_back, held=(1,), turn=3)
    weight_grad(n2, kb, gbl, ge_send, ge_recv, ge_own, G_E)

    grad_n2 = reduce_finish(2)
    mid = middle[...]
    xhat2, rstd2 = norm_stats(mid)
    row_grad, grad_g2, grad_s2 = norm_back(xhat2, rstd2, grad_n2, vector(5))
    grad_final = cot[...].astype(F32) * live
    grad_mid = grad_final + row_grad
    gmid[...] = grad_mid
    place(gm, grad_mid.astype(BF16))
    gather_start(gm, AG_GM)
    seg = width // b

    def vec_put(row, value):
        for e in range(b):
            vs[e, row : row + 1, :] = value[:, e * seg : (e + 1) * seg]

    vs[...] = jnp.zeros_like(vs)
    vec_put(2, jnp.sum(grad_mid, axis=0, keepdims=True))
    vec_put(3, grad_g2)
    vec_put(4, grad_s2)
    vec_put(5, jnp.sum(grad_final, axis=0, keepdims=True))
    bias_acc[...] = jnp.zeros_like(bias_acc)

    def attend_back(c2):
        grad_ctx = transposed_right(take(gm, c2, pair), wout[...]).astype(BF16)
        held = take(qkv, c2, pair)
        blocks = []
        for half in range(2):
            at_row = slice(half * rows, (half + 1) * rows)
            gqs, gks, gvs = [], [], []
            for j in range(hl):
                at = slice(j * hd, (j + 1) * hd)
                q = held[at_row, j * hd : (j + 1) * hd]
                kk = held[at_row, fl + j * hd : fl + (j + 1) * hd]
                v = held[at_row, 2 * fl + j * hd : 2 * fl + (j + 1) * hd]
                prob = take(probs, (2 * c2 + half) * hl + j, rows)
                grad_prob = transposed_right(grad_ctx[at_row, at], v)
                gvs.append(transposed_left(prob.astype(BF16), grad_ctx[at_row, at]))
                centre = jnp.sum(prob * grad_prob, axis=-1, keepdims=True)
                grad_score = (prob * (grad_prob - centre) * scale).astype(BF16)
                gqs.append(dot(grad_score, kk))
                gks.append(transposed_left(grad_score, q))
            blocks.append(jnp.concatenate(gqs + gks + gvs, axis=1))
        packed = jnp.concatenate(blocks, axis=0)
        bias_acc[...] += jnp.sum(packed, axis=0, keepdims=True)
        low_grad = packed.astype(BF16)
        put(gpk, c2, pair, low_grad)
        return [transposed_right(low_grad, joint_w[...])]

    def gm_ready(dc):
        gather_wait(gm, AG_GM, dc)

        @pl.when(dc == 3)
        def _():
            loop(1, 4, lambda d: send_hop(1, d))

    reduce_loop([3], attend_back, ready=gm_ready)
    weight_grad(n1, kb, gpk, gj_send, gj_recv, gj_own, G_J)
    grad_out = transposed_left(ctx[...], gm[...])
    evens = jnp.concatenate([grad_out[2 * j * br : (2 * j + 1) * br] for j in range(hl)], axis=0)
    odds = jnp.concatenate([grad_out[(2 * j + 1) * br : (2 * j + 2) * br] for j in range(hl)], axis=0)
    keep = jnp.where(k == 0, evens, odds)
    pass_on = jnp.where(k == 0, odds, evens)
    put(go_full, k, hl * br, keep.astype(BF16))
    go_sib[...] = pass_on.astype(BF16)
    start(go_sib, cut(go_full, k, hl * br), G_SIB, 0, sib)

    def collect(recv, mine, size, base):
        total = mine
        for d in range(1, b):
            arrive(cut(recv, d, size), base, d)
            total += recv[d * size : (d + 1) * size, :].astype(F32)
        return total

    def back(mine, landing, base):
        put(landing, p, br, take(mine, p, br))

        def step(d):
            q = (p + d) % T
            start(cut(mine, q, br), cut(landing, p, br), base, d, z * T + q)

        loop(1, T, step)

    gred_out[...] = collect(gr_recv, gr_own[...], hs, G_R)

    ge_low[...] = collect(ge_recv, ge_own[...], kb, G_E).astype(BF16)
    arrive(cut(go_full, 1 - k, hl * br), G_SIB, 0)

    def send_out(d):
        to = (z + d) % b
        start(cut(go_full, to, br), cut(go_recv, d, br), G_O, d, up(d))

    loop(1, b, send_out)
    grad_n1 = reduce_finish(3)
    xhat1, rstd1 = norm_stats(tok[...].astype(F32))
    row_grad, grad_g1, grad_s1 = norm_back(xhat1, rstd1, grad_n1, vector(0))
    gtok_out[...] = gmid[...] + row_grad
    vec_put(0, grad_g1)
    vec_put(1, grad_s1)
    for e in range(b):
        j = e % hl
        kept_row = jnp.concatenate(
            [bias_acc[:, j * hd : (j + 1) * hd], bias_acc[:, 2 * fl + j * hd : 2 * fl + (j + 1) * hd]], axis=1
        )
        vs[e, 6:7, :hs] = ebias_acc[:, e * hs : (e + 1) * hs]
        vs[e, 6:7, hs:] = jnp.where(k == e // hl, kept_row, 0.0)
    loop(1, b, lambda d: start(vs.at[(z + d) % b], vz_recv.at[d], VEC_Z, d, up(d)))

    back(ge_low, ge_back, BACK_E)
    total = vs[z]
    for d in range(1, b):
        arrive(vz_recv.at[d], VEC_Z, d)
        total += vz_recv[d]
    vp_own[...] = total
    vp[p] = total
    loop(1, T, lambda d: start(vp_own, vp.at[p], VEC_P, d, z * T + (p + d) % T))

    loop(1, T, lambda d: arrive(cut(ge_back, (p - d + T) % T, br), BACK_E, d))
    for q in range(T):
        for e in range(b):
            gexp_out[:, (e * T + q) * hs : (e * T + q + 1) * hs] = ge_back[
                q * br : (q + 1) * br, e * hs : (e + 1) * hs
            ].astype(F32)
    gj_low[...] = collect(gj_recv, gj_own[...], kb, G_J).astype(BF16)
    back(gj_low, gj_back, BACK_J)
    layer_out[...] = (middle[...] + reduce_finish(1) + vector(7)).astype(BF16)
    gout_out[...] = collect(go_recv, take(go_full, z, br).astype(F32), br, G_O)
    loop(1, T, lambda d: arrive(vp.at[(p - d + T) % T], VEC_P, d))
    total = jnp.sum(vp[...], axis=0)
    picked = jnp.zeros((8, br), F32)
    for q in range(T):
        picked = jnp.where(p == q, total[:, q * br : (q + 1) * br], picked)
    vec_out[0:8, 0:br] = picked
    vec_out[6:7, :] = vp[p, 6:7, :hs]
    keeper = 2 * c + z // hl
    row = vp[keeper, 6:7, :]
    for i in range(2):
        at = hs + i * hl * br
        vec_out[8 + i : 9 + i, 0:br] = jnp.where(k == 0, row[:, at : at + br], row[:, at + br : at + 2 * br])
    loop(1, T, lambda d: arrive(cut(gj_back, (p - d + T) % T, br), BACK_J, d))
    for w in range(3):
        for j in range(hl):
            at = slice((w * hl + j) * hd, (w * hl + j + 1) * hd)
            for k2 in range(2):
                for half in range(2):
                    q0, q1 = 4 * half + k2, 4 * half + 2 + k2
                    head = 2 * half + 4 * (hl * k2 + j)
                    gjoint_out[:, w * width + head * hd : w * width + (head + 2) * hd] = (
                        jnp.concatenate(
                            [gj_back[q0 * br : (q0 + 1) * br, at], gj_back[q1 * br : (q1 + 1) * br, at]],
                            axis=1,
                        ).astype(F32)
                    )

    sent(small.at[p, z], SMALL_Z, 1, b)
    sent(small.at[p], SMALL_P, 1, T)
    sent(cut(jstage, 0, br), A2A_J, 1, T)
    sent(cut(estage, 0, br), A2A_E, 1, T)
    sent(cut(joint_w, 0, kb), Z_J, 1, b)
    spread_sent(exp_w, kb, Z_E, RELAY_E)
    sent(reduce_in, Z_R, 1, b)
    sent(out_in, Z_O, 1, b)
    sent(wo_sib, SIB_O, 0, 1)
    for base in (AG_N1, AG_GF, AG_N2, AG_GM):
        sent(cut(n1, 0, rows), base, 1, 8)
    for r in range(4):
        sent(cut(csend.at[0], 0, rows), RS_0 + 8 * r, 0, 4)
        sent(cut(csend.at[0], 0, rows), RS_0 + 8 * r, 5, 8)
    sent(cut(ge_send, 0, kb), G_E, 1, b)
    sent(cut(gr_send, 0, hs), G_R, 1, b)
    sent(cut(gj_send, 0, kb), G_J, 1, b)
    sent(go_sib, G_SIB, 0, 1)
    sent(cut(go_recv, 0, br), G_O, 1, b)
    sent(cut(ge_low, 0, br), BACK_E, 1, T)
    sent(cut(gj_low, 0, br), BACK_J, 1, T)
    sent(vs.at[0], VEC_Z, 1, b)
    sent(vp_own, VEC_P, 1, T)


def finish(count, vec, *refs):
    large_in, large_out, small_out = refs[:count], refs[count : 2 * count], refs[2 * count : -count - 2]
    held, sem_in, sem_out = refs[-count - 2 : -2], refs[-2], refs[-1]
    inward = [pltpu.make_async_copy(x, h, sem_in.at[i]) for i, (x, h) in enumerate(zip(large_in, held))]
    outward = [pltpu.make_async_copy(h, x, sem_out.at[i]) for i, (h, x) in enumerate(zip(held, large_out))]
    for copy in inward:
        copy.start()
    for r, out in zip((0, 1, 8, 9, 2, 3, 4, 5, 6), small_out):
        size = out.shape[0]
        out[...] = vec[r : r + 1, :size].reshape(size)
    for first, second in zip(inward, outward):
        first.wait()
        second.start()
    for copy in outward:
        copy.wait()


def fused(
    tokens, lengths, cotangent, norm1_gain, norm1_shift, joint_weight, query_bias, value_bias,
    output_weight, output_bias, norm2_gain, norm2_shift, expand_weight, expand_bias,
    reduce_weight, reduce_bias,
):
    n = lax.axis_size("dp")
    T = TENSOR
    b = n // T
    rows, width = tokens.shape
    br = joint_weight.shape[0]
    hs = reduce_weight.shape[0]
    fl = width // T
    hl = HEADS // T
    seqs = lengths.shape[1]
    kb, f, fj, tt = br * T, b * hs, 3 * fl, T * rows
    vm = pltpu.VMEM
    scratch = [
        vm((16, 128), F32), vm((T, b, 16, 128), BF16), vm((T, b, 16, 128), F32), vm((kb, fj), BF16), vm((kb, f), BF16), vm((width, fj), BF16),
        vm((width, f), BF16), vm((f, width), BF16), vm((b * br, width), BF16),
        vm((hl * br, width), BF16), vm((fl, width), BF16),
        vm((tt, width), BF16), vm((tt, width), BF16), vm((tt, width), BF16), vm((tt, width), BF16),
        vm((tt, fj), BF16), vm((tt * hl, rows), F32), vm((tt, fl), BF16),
        vm((tt, f), BF16), vm((tt, f), BF16), vm((tt, fj), BF16), vm((tt, f), F32),
        vm((4, 4 * rows, width), BF16), vm((4, 4 * rows, width), BF16),
        vm((4, 4 * rows, width), BF16), vm((4, 4 * rows, width), BF16),
        vm((4, 4 * rows, width), F32), vm((rows, width), F32), vm((rows, width), F32),
        vm((b * kb, f), BF16), vm((b * kb, f), BF16), vm((kb, f), F32),
        vm((b * hs, width), BF16), vm((b * hs, width), BF16), vm((hs, width), F32),
        vm((b * kb, fj), BF16), vm((b * kb, fj), BF16), vm((kb, fj), F32),
        vm((b * br, width), BF16), vm((hl * br, width), BF16), vm((hl * br, width), BF16), vm((b * br, width), BF16),
        vm((kb, f), BF16), vm((kb, fj), BF16), vm((kb, f), BF16), vm((kb, fj), BF16),
        vm((b, 8, width // b), F32), vm((b, 8, width // b), F32), vm((8, width // b), F32), vm((T, 8, width // b), F32),
        vm((1, fj), F32), vm((1, f), F32),
        pltpu.SemaphoreType.DMA((SEMS,)), pltpu.SemaphoreType.DMA((SEMS,)),
    ]
    sds = jax.ShapeDtypeStruct
    *large, vec = pl.pallas_call(
        functools.partial(kernel, seqs),
        out_shape=(
            sds((rows, width), BF16), sds((rows, width), F32), sds((br, 3 * width), F32),
            sds((br, width), F32), sds((br, expand_weight.shape[1]), F32), sds((hs, width), F32),
            sds((16, hs), F32),
        ),
        in_specs=[pl.BlockSpec(memory_space=pltpu.VMEM)] * 16,
        out_specs=tuple([pl.BlockSpec(memory_space=pltpu.VMEM)] * 7),
        scratch_shapes=scratch,
        compiler_params=pltpu.CompilerParams(
            collective_id=0, has_side_effects=True, vmem_limit_bytes=62 * 1024 * 1024
        ),
        name="layer",
    )(
        tokens, cotangent, joint_weight, output_weight, expand_weight, reduce_weight, lengths,
        norm1_gain, norm1_shift, query_bias, value_bias, output_bias, norm2_gain, norm2_shift,
        reduce_bias, expand_bias,
    )

    anywhere, inside = pl.BlockSpec(memory_space=pl.ANY), pl.BlockSpec(memory_space=pltpu.VMEM)
    done = pl.pallas_call(
        functools.partial(finish, len(large)),
        out_shape=tuple(sds(x.shape, x.dtype) for x in large)
        + tuple(sds((br,), F32) for _ in range(8)) + (sds((hs,), F32),),
        in_specs=[inside] + [anywhere] * len(large),
        out_specs=tuple([anywhere] * len(large) + [inside] * 9),
        scratch_shapes=[pltpu.VMEM(x.shape, x.dtype) for x in large]
        + [pltpu.SemaphoreType.DMA((len(large),))] * 2,
        name="finish",
    )(vec, *large)
    layer_output, grad_tokens, g_joint, g_out, g_exp, g_red = done[:6]
    g_g1, g_s1, g_qb, g_vb, g_ob, g_g2, g_s2, g_rb, g_eb = done[6:]
    return (
        layer_output, grad_tokens, g_g1, g_s1, g_joint, g_qb, g_vb, g_out,
        g_ob, g_g2, g_s2, g_exp, g_eb, g_red, g_rb,
    )


def fits(n, width):
    br = width // n
    return n % TENSOR == 0 and br % 16 == 0 and 2 * br * HEADS == width and n // TENSOR == 2 * (HEADS // TENSOR)


def whole(*args):
    n = lax.axis_size("dp")
    return fused(*args) if fits(n, args[0].shape[1]) else on_device(*args)


def solution(mesh):
    m, v = P("dp", None), P("dp")
    in_specs = (m, m, m, v, v, m, v, v, m, v, v, v, m, v, m, v)
    out_specs = (m, m, v, v, m, v, v, m, v, v, v, m, v, m, v)
    return jax.shard_map(
        whole, mesh=mesh, in_specs=in_specs, out_specs=out_specs, check_vma=False
    )
```
